32 devices in a mesh: dp: 4 (over y, core), mp: 8 (over z, x).
Axes of the slice: x: 2, y: 2, z: 4, core: 2. Of those that a mesh axis runs over, the one named last changes fastest.
Arguments:
- char_ids: int32 [8960, 50], P(('dp', 'mp')), may hold values from 0 to 261
- doc_lengths: int32 [40], replicated, may hold values from 1040 to 1620, as said below
- window_doc: int32 [448], P('dp'), may hold values from 0 to 39, as said below
- window_offset: int32 [448], P('dp'), may hold values from 1000 to 1619, as said below
- char_table: float32 [262, 16], replicated, may hold values from -6 to 6
- conv_weight: float32 [7, 16, 2048], P(None, None, 'dp'), may hold values from -0.5 to 0.5
- conv_bias: float32 [2048], replicated, may hold values from -3 to 3
- highway_weight: float32 [2, 2048, 4096], P(None, 'dp'), may hold values from -0.125 to 0.125
- highway_bias: float32 [2, 4096], replicated, may hold values from -3 to 3
- proj_weight: float32 [2048, 512], P('dp'), may hold values from -0.125 to 0.125
- proj_bias: float32 [512], replicated, may hold values from -3 to 3
- lstm_input_weight: float32 [2, 512, 16384], P(None, 'dp', 'mp'), may hold values from -0.25 to 0.25
- lstm_state_weight: float32 [2, 512, 16384], P(None, 'dp', 'mp'), may hold values from -0.25 to 0.25
- lstm_bias: float32 [2, 16384], P(None, 'mp'), may hold values from -3 to 3
- lstm_proj: float32 [2, 4096, 512], P(None, 'mp', 'dp'), may hold values from -0.25 to 0.25
- init_cell: float32 [2, 448, 4096], P(None, 'dp', 'mp'), may hold values from -6 to 6
- init_hidden: bfloat16 [2, 448, 512], P(None, 'dp'), may hold values from -3 to 3
- cotangent: bfloat16 [448, 20, 1024], P('dp'), may hold values from -6 to 6
Outputs:
- hidden: bfloat16 [448, 20, 1024], P('dp')
- grad_char_table: float32 [262, 16], replicated
- grad_conv_weight: float32 [7, 16, 2048], P(None, None, 'dp')
- grad_conv_bias: float32 [2048], replicated
- grad_highway_weight: float32 [2, 2048, 4096], P(None, 'dp')
- grad_highway_bias: float32 [2, 4096], replicated
- grad_proj_weight: float32 [2048, 512], P('dp')
- grad_proj_bias: float32 [512], replicated
- grad_lstm_input: float32 [2, 512, 16384], P(None, 'dp', 'mp')
- grad_lstm_state: float32 [2, 512, 16384], P(None, 'dp', 'mp')
- grad_lstm_bias: float32 [2, 16384], P(None, 'mp')
- grad_lstm_proj: float32 [2, 4096, 512], P(None, 'mp', 'dp')
The draws below stay inside these ranges and needn't reach their ends.
Inputs may be any that keep to these rules, and one draw needn't show every extreme that they name: `doc_lengths`: one document of each draw has length 1040 and one has length 1620. `window_doc`: a document number below 40. doc_lengths[window_doc] - window_offset lies between 1 and 40, and both ends occur in every draw.
All inputs are finite; a program needn't handle non-finite values.
Results may differ from the reference program's by a relative error of at most 0.025.
Values may be sent and summed in bfloat16 or wider, within the bound.
A program may use at most 448 MiB of HBM per device.

```python
import math
import jax
import jax.numpy as jnp
from jax import lax

VOCAB = 262
CHARS = 50
CDIM = 16
TAPS = 7
FILTERS = 2048
PROJ = 512
CELL = 4096
UNIT_BLOCK = 128
WIN = 20
DOCS = 40
LEN_LO = 1040
LEN_HI = 1620
GATES = 16384
ROWS = 448
TOKENS = 8960


def document_plan(key):
    length_key = jax.random.fold_in(key, 11)
    doc_key = jax.random.fold_in(key, 12)
    gap_key = jax.random.fold_in(key, 13)
    spot_key = jax.random.fold_in(key, 14)
    lengths = jax.random.randint(length_key, (DOCS,), LEN_LO, LEN_HI + 1)
    spot_draws = jax.random.randint(spot_key, (2,), 0, 1000000)
    long_spot = spot_draws[0] % DOCS
    short_spot = (long_spot + 1) % DOCS
    lengths = lengths.at[long_spot].set(LEN_HI)
    lengths = lengths.at[short_spot].set(LEN_LO)
    window_docs = jax.random.randint(doc_key, (ROWS,), 0, DOCS)
    gap_sizes = jax.random.randint(gap_key, (ROWS,), 1, 2 * WIN + 1)
    row_spot = spot_draws[1] % ROWS
    next_spot = (row_spot + 1) % ROWS
    gap_sizes = gap_sizes.at[row_spot].set(1)
    gap_sizes = gap_sizes.at[next_spot].set(2 * WIN)
    window_docs = window_docs.at[row_spot].set(long_spot)
    window_docs = window_docs.at[next_spot].set(short_spot)
    offsets = jnp.take(lengths, window_docs) - gap_sizes
    return (lengths.astype(jnp.int32), window_docs.astype(jnp.int32), offsets.astype(jnp.int32))


def draw_doc_lengths(key, part):
    return document_plan(key)[0]


def draw_window_doc(key, part):
    return document_plan(key)[1]


def draw_window_offset(key, part):
    return document_plan(key)[2]


def touch_ends(drawn, rng, smallest, high):
    spot = [jax.random.randint(jax.random.fold_in(rng, axis), (), 0, length) for axis, length in enumerate(drawn.shape)]
    main_axis = drawn.shape.index(max(drawn.shape))
    beside = spot[:main_axis] + [(spot[main_axis] + 1) % drawn.shape[main_axis]] + spot[main_axis + 1:]
    return drawn.at[tuple(spot)].set(smallest).at[tuple(beside)].set(high)


def block_levels(key, extent, split, smallest, top_value):
    loudness = 1.0
    for position, parts in split:
        draws = jax.random.uniform(jax.random.fold_in(jax.random.fold_in(key, 6), position), (parts,), jnp.float32, smallest / len(split), top_value / len(split))
        loudness = loudness * jnp.repeat(jnp.exp(draws), extent[position] // parts).reshape((-1,) + (1,) * (len(extent) - 1 - position))
    return loudness


def normal_values(own_key, shape, spread, most, cuts=(), kind=jnp.bfloat16):
    loudness = block_levels(own_key, shape, cuts, -0.22, 0.18) if cuts else 1.0
    values = jax.random.normal(own_key, shape, jnp.float32) * spread * loudness
    return jnp.minimum(jnp.maximum(values, -most), most).astype(kind)


def setup_inputs(seed: int = 0) -> dict:
    key_list = jax.random.split(jax.random.key(seed), 19)
    char_ids = touch_ends(jax.random.randint(key_list[0], (TOKENS, CHARS), 0, VOCAB), jax.random.fold_in(key_list[0], 1), 0, VOCAB - 1).astype(jnp.int32)
    doc_lengths = draw_doc_lengths(jax.random.fold_in(key_list[18], 71), 0)
    window_doc = draw_window_doc(jax.random.fold_in(key_list[18], 71), 0)
    window_offset = draw_window_offset(jax.random.fold_in(key_list[18], 71), 0)
    char_table = normal_values(key_list[4], (VOCAB, CDIM), 1.0, 6.0, (), jnp.float32)
    conv_weight = normal_values(key_list[5], (TAPS, CDIM, FILTERS), (TAPS * CDIM) ** -0.5, 0.5, ((2, 4),), jnp.float32)
    conv_bias = normal_values(key_list[6], (FILTERS,), 0.5, 3.0, (), jnp.float32)
    highway_weight = normal_values(key_list[7], (2, FILTERS, 2 * FILTERS), FILTERS ** -0.5, 0.125, ((1, 4),), jnp.float32)
    highway_bias = normal_values(key_list[8], (2, 2 * FILTERS), 0.5, 3.0, (), jnp.float32)
    proj_weight = normal_values(key_list[9], (FILTERS, PROJ), FILTERS ** -0.5, 0.125, ((0, 4),), jnp.float32)
    proj_bias = normal_values(key_list[10], (PROJ,), 0.5, 3.0, (), jnp.float32)
    lstm_input_weight = normal_values(key_list[11], (2, PROJ, GATES), PROJ ** -0.5, 0.25, ((1, 4), (2, 8)), jnp.float32)
    lstm_state_weight = normal_values(key_list[12], (2, PROJ, GATES), PROJ ** -0.5, 0.25, ((1, 4), (2, 8)), jnp.float32)
    lstm_bias = normal_values(key_list[13], (2, GATES), 0.5, 3.0, ((1, 8),), jnp.float32)
    lstm_proj = normal_values(key_list[14], (2, CELL, PROJ), (CELL // 8) ** -0.5, 0.25, ((1, 8), (2, 4)), jnp.float32)
    init_cell = normal_values(key_list[15], (2, ROWS, CELL), 1.0, 6.0, ((1, 4), (2, 8)), jnp.float32)
    init_hidden = normal_values(key_list[16], (2, ROWS, PROJ), 0.5, 3.0, ((1, 4),))
    cotangent = normal_values(key_list[17], (ROWS, WIN, 2 * PROJ), 1.0, 6.0, ((0, 4),))
    return {"char_ids": char_ids, "doc_lengths": doc_lengths, "window_doc": window_doc, "window_offset": window_offset, "char_table": char_table, "conv_weight": conv_weight, "conv_bias": conv_bias, "highway_weight": highway_weight, "highway_bias": highway_bias, "proj_weight": proj_weight, "proj_bias": proj_bias, "lstm_input_weight": lstm_input_weight, "lstm_state_weight": lstm_state_weight, "lstm_bias": lstm_bias, "lstm_proj": lstm_proj, "init_cell": init_cell, "init_hidden": init_hidden, "cotangent": cotangent}


CLIP = 3.0

@jax.custom_vjp
def low(v):
    return lax.optimization_barrier(v.astype(jnp.bfloat16)).astype(jnp.float32)

@jax.custom_vjp
def low_back(v):
    return v

def low_keep(v):
    return (low(v), None)

def low_pass(kept, grad):
    return (grad,)

def back_keep(v):
    return (v, None)

def back_low(kept, grad):
    return (low(grad),)
low.defvjp(low_keep, low_pass)
low_back.defvjp(back_keep, back_low)

def filter_widths(count):
    unit_size = count // 64
    index_row = jnp.arange(count).astype(jnp.int32)
    widths = jnp.ones((count,), jnp.int32)
    for exponent in range(6):
        widths = widths + (index_row >= unit_size * (1 << exponent)).astype(jnp.int32)
    return widths

def split_gates(pre_act, unit_count):
    leading = pre_act.shape[:-1]
    shaped = pre_act.reshape(leading + (unit_count // UNIT_BLOCK, 4, UNIT_BLOCK))
    return [shaped[..., gate_index, :].reshape(leading + (unit_count,)) for gate_index in range(4)]

def reference(char_ids, doc_lengths, window_doc, window_offset, char_table, conv_weight, conv_bias, highway_weight, highway_bias, proj_weight, proj_bias, lstm_input_weight, lstm_state_weight, lstm_bias, lstm_proj, init_cell, init_hidden, cotangent):
    highest = lax.Precision.HIGHEST
    widths = filter_widths(FILTERS)
    tap_mask = (jnp.arange(TAPS)[:, None] < widths[None, :]).astype(jnp.float32)
    valid_mask = (jnp.arange(CHARS)[:, None] <= CHARS - widths[None, :]).astype(jnp.float32)
    counts = (CHARS + 1 - widths).astype(jnp.float32)
    reset_at = jnp.take(doc_lengths, window_doc) - window_offset
    step_ids = jnp.arange(WIN).astype(jnp.int32)
    keep_fwd = (step_ids[None, :] != reset_at[:, None]).astype(jnp.float32)
    keep_bwd = (step_ids[None, :] != reset_at[:, None] - 1).astype(jnp.float32)[:, ::-1]
    keep_masks = jnp.transpose(jnp.stack([keep_fwd, keep_bwd]), (2, 0, 1))
    block_tokens = math.gcd(ROWS, 8) * WIN
    id_blocks = char_ids.reshape(TOKENS // block_tokens, block_tokens, CHARS)
    first_cell = init_cell.astype(jnp.float32)
    first_hidden = init_hidden.astype(jnp.float32)

    def forward(table_value, conv_value, conv_shift, high_value, high_shift, proj_value, proj_shift, input_value, state_value, gate_shift, cell_value):
        table_low = low(table_value)
        conv_matrix = (low(conv_value) * tap_mask[:, None, :]).reshape(TAPS * CDIM, FILTERS)

        def conv_pool(id_block):
            char_vecs = table_low[id_block]
            padded = jnp.pad(char_vecs, ((0, 0), (0, TAPS - 1), (0, 0)))
            columns = jnp.concatenate([padded[:, tap_index:tap_index + CHARS, :] for tap_index in range(TAPS)], axis=2)
            conv_out = jnp.dot(columns.reshape(-1, TAPS * CDIM), conv_matrix, precision=highest)
            conv_out = low_back(conv_out).reshape(block_tokens, CHARS, FILTERS)
            exp_total = lax.optimization_barrier(jnp.sum(jnp.exp(conv_out) * valid_mask, axis=1))
            return jnp.log(exp_total / counts)
        pooled = lax.map(jax.checkpoint(conv_pool), id_blocks).reshape(TOKENS, FILTERS)
        layer_value = jax.nn.silu(pooled + conv_shift)
        for layer_index in range(2):
            mixed = low_back(jnp.dot(low(layer_value), low(high_value[layer_index]), precision=highest) + high_shift[layer_index])
            gate_value = jax.nn.sigmoid(mixed[:, FILTERS:])
            layer_value = gate_value * layer_value + (1.0 - gate_value) * jax.nn.silu(mixed[:, :FILTERS])
        embed = low(low_back(jnp.dot(low(layer_value), low(proj_value), precision=highest) + proj_shift))
        input_pre = jnp.einsum('np,dpg->dng', embed, low(input_value), precision=highest) + gate_shift[:, None, :]
        input_pre = input_pre.reshape(2, ROWS, WIN, GATES)
        scan_input = jnp.transpose(jnp.stack([input_pre[0], input_pre[1][:, ::-1]]), (2, 0, 1, 3))
        state_low = low(state_value)
        cell_low = low(cell_value)

        def lstm_step(carry, inputs):
            cell_state, hidden_state = carry
            step_pre, keep_now = inputs
            keep_cols = keep_now[:, :, None]
            cell_prev = cell_state * keep_cols
            hidden_prev = hidden_state * keep_cols
            pre_act = low_back(step_pre + jnp.einsum('drp,dpg->drg', hidden_prev, state_low, precision=highest))
            gate_in, gate_forget, gate_cand, gate_out = split_gates(pre_act, CELL)
            cell_new = CLIP * jnp.tanh((jax.nn.sigmoid(gate_forget) * cell_prev + jax.nn.sigmoid(gate_in) * jnp.tanh(gate_cand)) / CLIP)
            cell_out = jax.nn.sigmoid(gate_out) * jnp.tanh(cell_new)
            summed = low_back(jnp.einsum('drc,dcp->drp', low(cell_out), cell_low, precision=highest))
            hidden_new = low(CLIP * jnp.tanh(summed / CLIP))
            return ((cell_new, hidden_new), hidden_new)
        carry_end, states = lax.scan(jax.checkpoint(lstm_step), (first_cell, first_hidden), (scan_input, keep_masks))
        forward_part = jnp.transpose(states[:, 0], (1, 0, 2))
        backward_part = jnp.transpose(states[::-1, 1], (1, 0, 2))
        return jnp.concatenate([forward_part, backward_part], axis=-1)
    masters = (char_table, conv_weight, conv_bias, highway_weight, highway_bias, proj_weight, proj_bias, lstm_input_weight, lstm_state_weight, lstm_bias, lstm_proj)
    masters = tuple((value.astype(jnp.float32) for value in masters))
    hidden, pullback = jax.vjp(forward, *masters)
    grads = pullback(cotangent.astype(jnp.float32))
    return (hidden.astype(jnp.bfloat16), grads[0], grads[1], grads[2], grads[3], grads[4], grads[5], grads[6], grads[7], grads[8], grads[9], grads[10])
```

```python
import functools
import math

import jax
import jax.numpy as jnp
from jax import lax
from jax.experimental import pallas as pl
from jax.experimental.pallas import tpu as pltpu
from jax.sharding import PartitionSpec as P

VOCAB = 262
CHARS = 50
CDIM = 16
TAPS = 7
FILTERS = 2048
PROJ = 512
UNIT_BLOCK = 128
WIN = 20
GATES = 16384


CLIP = 3.0


def filter_widths(count):
    unit_size = count // 64
    index_row = jnp.arange(count)
    widths = jnp.ones((count,), jnp.int32)
    for exponent in range(6):
        widths = widths + (index_row >= unit_size * (1 << exponent)).astype(jnp.int32)
    return widths


def split_gates(pre_act, unit_count):
    leading = pre_act.shape[:-1]
    shaped = pre_act.reshape(leading + (unit_count // UNIT_BLOCK, 4, UNIT_BLOCK))
    return [shaped[..., gate_index, :].reshape(leading + (unit_count,)) for gate_index in range(4)]


def join_gates(gate_parts, unit_count):
    leading = gate_parts[0].shape[:-1]
    stacked = jnp.stack(
        [
            part_value.reshape(leading + (unit_count // UNIT_BLOCK, UNIT_BLOCK))
            for part_value in gate_parts
        ],
        axis=-2,
    )
    return stacked.reshape(leading + (4 * unit_count,))


def silu_slope(value):
    sigma = jax.nn.sigmoid(value)
    return sigma * (1.0 + value * (1.0 - sigma))


def char_columns(id_block, table_low):
    flat_ids = id_block.reshape(-1)
    one_hot = flat_ids[:, None] == jnp.arange(VOCAB)[None, :]
    char_vecs = jnp.dot(
        one_hot.astype(jnp.bfloat16), table_low, preferred_element_type=jnp.float32
    ).astype(jnp.bfloat16)
    char_vecs = char_vecs.reshape(id_block.shape[0], CHARS, CDIM)
    padded = jnp.pad(char_vecs, ((0, 0), (0, TAPS - 1), (0, 0)))
    columns = jnp.concatenate(
        [padded[:, tap_index : tap_index + CHARS, :] for tap_index in range(TAPS)], axis=2
    )
    return (one_hot, columns.reshape(-1, TAPS * CDIM))


def sigmoid_of(value):
    return 0.5 * jnp.tanh(0.5 * value) + 0.5


def mp_barrier(size):
    me = lax.axis_index("mp")
    barrier = pltpu.get_barrier_semaphore()
    for offset in range(1, size):
        peer = lax.rem(me + offset, size)
        pl.semaphore_signal(
            barrier, inc=1, device_id={"mp": peer}, device_id_type=pl.DeviceIdType.MESH
        )
    pl.semaphore_wait(barrier, size - 1)


class Exchange:
    def __init__(self, size, part_ref, sum_ref, all_ref, sems):
        self.size = size
        self.me = lax.axis_index("mp")
        self.part_ref, self.sum_ref, self.all_ref = part_ref, sum_ref, all_ref
        self.part_send, self.part_recv, self.all_send, self.all_recv = sems

    def part_copy(self, way, offset, incoming):
        peer = lax.rem(self.me + (self.size - offset if incoming else offset), self.size)
        return pltpu.make_async_remote_copy(
            src_ref=self.part_ref.at[way, peer],
            dst_ref=self.sum_ref.at[way, peer if incoming else self.me],
            send_sem=self.part_send.at[way, offset],
            recv_sem=self.part_recv.at[way, offset],
            device_id={"mp": peer},
            device_id_type=pl.DeviceIdType.MESH,
        )

    def all_copy(self, way, offset, incoming):
        peer = lax.rem(self.me + (self.size - offset if incoming else offset), self.size)
        slot = peer if incoming else self.me
        return pltpu.make_async_remote_copy(
            src_ref=self.all_ref.at[way, slot],
            dst_ref=self.all_ref.at[way, slot],
            send_sem=self.all_send.at[way, offset],
            recv_sem=self.all_recv.at[way, offset],
            device_id={"mp": peer},
            device_id_type=pl.DeviceIdType.MESH,
        )

    def send_parts(self, way):
        for offset in range(1, self.size):
            self.part_copy(way, offset, False).start()

    def take_sum(self, way):
        total = self.part_ref[way, self.me].astype(jnp.float32)
        for offset in range(1, self.size):
            self.part_copy(way, offset, True).wait_recv()
            peer = lax.rem(self.me + self.size - offset, self.size)
            total = total + self.sum_ref[way, peer].astype(jnp.float32)
        for offset in range(1, self.size):
            self.part_copy(way, offset, False).wait_send()
        return total

    def send_all(self, way, value):
        self.all_ref[way, self.me] = value
        for offset in range(1, self.size):
            self.all_copy(way, offset, False).start()

    def wait_all(self, way):
        for offset in range(1, self.size):
            self.all_copy(way, offset, True).wait_recv()
        for offset in range(1, self.size):
            self.all_copy(way, offset, False).wait_send()


def forward_kernel(
    size,
    emb_ref,
    win_ref,
    wst_ref,
    wpr_ref,
    bias_ref,
    cell_ref,
    hid_ref,
    reset_ref,
    embt_ref,
    gate0_ref,
    gate1_ref,
    cprev0_ref,
    cprev1_ref,
    cnew0_ref,
    cnew1_ref,
    low0_ref,
    low1_ref,
    hprev0_ref,
    hprev1_ref,
    stat0_ref,
    stat1_ref,
    out0_ref,
    out1_ref,
    pre_ref,
    state_ref,
    part_ref,
    sum_ref,
    all_ref,
    part_send,
    part_recv,
    all_send,
    all_recv,
):
    step = pl.program_id(0)
    rows = reset_ref.shape[0]
    units = cell_ref.shape[2]
    blocks = units // UNIT_BLOCK
    wide = 4 * UNIT_BLOCK
    comm = Exchange(size, part_ref, sum_ref, all_ref, (part_send, part_recv, all_send, all_recv))
    gate_refs = (gate0_ref, gate1_ref)
    cprev_refs = (cprev0_ref, cprev1_ref)
    cnew_refs = (cnew0_ref, cnew1_ref)
    low_refs = (low0_ref, low1_ref)
    hprev_refs = (hprev0_ref, hprev1_ref)
    stat_refs = (stat0_ref, stat1_ref)
    out_refs = (out0_ref, out1_ref)

    def time_of(way, at):
        return at if way == 0 else WIN - 1 - at

    def input_part(way, at):
        emb = emb_ref[:, time_of(way, at)].reshape(rows, PROJ)
        for block in range(blocks):
            cols = slice(block * wide, (block + 1) * wide)
            pre_ref[way, :, cols] = (
                jnp.dot(emb, win_ref[way, :, cols], preferred_element_type=jnp.float32)
                + bias_ref[way, :, cols]
            )

    def emit_hidden(way):
        out_refs[way][0] = all_ref[way].reshape(rows, PROJ)

    def cell_step(way):
        now = time_of(way, step)
        keep = jnp.where(reset_ref[...] - way == now, 0.0, 1.0)
        keep_low = jnp.concatenate([keep.astype(jnp.bfloat16)] * (PROJ // UNIT_BLOCK), axis=1)
        hidden_prev = all_ref[way].reshape(rows, PROJ) * keep_low
        hprev_refs[way][0] = hidden_prev
        if way == 0:
            embt_ref[0] = emb_ref[:, step].reshape(rows, PROJ)
        for block in range(blocks):
            cols = slice(block * wide, (block + 1) * wide)
            unit = slice(block * UNIT_BLOCK, (block + 1) * UNIT_BLOCK)
            pre = pre_ref[way, :, cols] + jnp.dot(
                hidden_prev, wst_ref[way, :, cols], preferred_element_type=jnp.float32
            )
            gate_in = sigmoid_of(pre[:, :UNIT_BLOCK])
            gate_forget = sigmoid_of(pre[:, UNIT_BLOCK : 2 * UNIT_BLOCK])
            gate_cand = jnp.tanh(pre[:, 2 * UNIT_BLOCK : 3 * UNIT_BLOCK])
            gate_out = sigmoid_of(pre[:, 3 * UNIT_BLOCK :])
            cell_prev = state_ref[way, :, unit] * keep
            cell_new = CLIP * jnp.tanh(
                (gate_forget * cell_prev + gate_in * gate_cand) * (1.0 / CLIP)
            )
            gate_refs[way][0, :, cols] = jnp.concatenate(
                [gate_in, gate_forget, gate_cand, gate_out], axis=1
            )
            cprev_refs[way][0, :, unit] = cell_prev
            cnew_refs[way][0, :, unit] = cell_new
            state_ref[way, :, unit] = cell_new
            low_refs[way][0, :, unit] = (gate_out * jnp.tanh(cell_new)).astype(jnp.bfloat16)
        partial = jnp.dot(low_refs[way][0], wpr_ref[way], preferred_element_type=jnp.float32)
        part_ref[way] = partial.astype(jnp.bfloat16).reshape(size, rows // size, PROJ)
        comm.send_parts(way)

    def close_step(way):
        total = comm.take_sum(way)
        stat_refs[way][0] = total
        comm.send_all(way, (CLIP * jnp.tanh(total * (1.0 / CLIP))).astype(jnp.bfloat16))

    @pl.when(step == 0)
    def _():
        for way in range(2):
            all_ref[way] = hid_ref[way]
            state_ref[way] = cell_ref[way]
            input_part(way, 0)
        mp_barrier(size)

    @pl.when(step > 0)
    def _():
        comm.wait_all(0)
        emit_hidden(0)

    @pl.when(step < WIN)
    def _():
        cell_step(0)

    @pl.when(step > 0)
    def _():
        close_step(1)

    @pl.when(step < WIN)
    def _():
        @pl.when(step < WIN - 1)
        def _():
            input_part(0, step + 1)

        close_step(0)

    @pl.when(step > 0)
    def _():
        comm.wait_all(1)
        emit_hidden(1)

    @pl.when(step < WIN)
    def _():
        cell_step(1)

        @pl.when(step < WIN - 1)
        def _():
            input_part(1, step + 1)


def lstm_forward(size, emb, win, wst, wpr, bias, cell, hid, reset):
    rows = reset.shape[0]
    part = rows // size
    gates = win.shape[2]
    units = cell.shape[2]
    last = WIN - 1
    vmem = pl.BlockSpec(memory_space=pltpu.VMEM)

    def block(shape, index):
        return pl.BlockSpec((1,) + shape, lambda w: (index(w), 0, 0))

    now0 = lambda w: jnp.minimum(w, last)
    now1 = lambda w: last - jnp.minimum(w, last)
    past0 = lambda w: jnp.maximum(w - 1, 0)
    past1 = lambda w: last - jnp.maximum(w - 1, 0)
    outs = [((rows, PROJ), jnp.bfloat16, now0)]
    for width, kind in ((gates, jnp.float32), (units, jnp.float32), (units, jnp.float32), (units, jnp.bfloat16), (PROJ, jnp.bfloat16)):
        outs += [((rows, width), kind, now0), ((rows, width), kind, now1)]
    outs += [((part, PROJ), jnp.float32, now0), ((part, PROJ), jnp.float32, past1)]
    outs += [((rows, PROJ), jnp.bfloat16, past0), ((rows, PROJ), jnp.bfloat16, past1)]
    return pl.pallas_call(
        functools.partial(forward_kernel, size),
        grid=(WIN + 1,),
        in_specs=[vmem] * 8,
        out_specs=[block(shape, index) for shape, kind, index in outs],
        out_shape=[jax.ShapeDtypeStruct((WIN,) + shape, kind) for shape, kind, index in outs],
        scratch_shapes=[
            pltpu.VMEM((2, rows, gates), jnp.float32),
            pltpu.VMEM((2, rows, units), jnp.float32),
            pltpu.VMEM((2, size, part, PROJ), jnp.bfloat16),
            pltpu.VMEM((2, size, part, PROJ), jnp.bfloat16),
            pltpu.VMEM((2, size, part, PROJ), jnp.bfloat16),
        ]
        + [pltpu.SemaphoreType.DMA((2, size))] * 4,
        compiler_params=pltpu.CompilerParams(
            collective_id=1, has_side_effects=True, vmem_limit_bytes=56 * 2**20
        ),
    )(emb, win, wst, wpr, bias, cell, hid, reset)


def backward_kernel(
    size,
    gate0_ref,
    gate1_ref,
    cprev0_ref,
    cprev1_ref,
    cnew0_ref,
    cnew1_ref,
    cot0_ref,
    cot1_ref,
    stat0_ref,
    stat1_ref,
    win_ref,
    wst_ref,
    wpr_ref,
    reset_ref,
    first_cot_ref,
    first_stat_ref,
    da0_ref,
    da1_ref,
    ds0_ref,
    ds1_ref,
    de0_ref,
    de1_ref,
    bias_ref,
    cell_ref,
    part_ref,
    sum_ref,
    all_ref,
    part_send,
    part_recv,
    all_send,
    all_recv,
):
    step = pl.program_id(0)
    rows = reset_ref.shape[0]
    part = rows // size
    units = cell_ref.shape[2]
    blocks = units // UNIT_BLOCK
    wide = 4 * UNIT_BLOCK
    comm = Exchange(size, part_ref, sum_ref, all_ref, (part_send, part_recv, all_send, all_recv))
    gate_refs = (gate0_ref, gate1_ref)
    cprev_refs = (cprev0_ref, cprev1_ref)
    cnew_refs = (cnew0_ref, cnew1_ref)
    da_refs = (da0_ref, da1_ref)
    ds_refs = (ds0_ref, ds1_ref)
    de_refs = (de0_ref, de1_ref)

    def time_of(way, at):
        return WIN - 1 - at if way == 0 else at

    def stat_step(way, at, cot, stat, total):
        grad = cot.astype(jnp.float32)
        if total is not None:
            own = reset_ref[pl.ds(comm.me * part, part), :] - way
            keep = jnp.where(own == time_of(way, at - 1), 0.0, 1.0)
            grad = grad + total * jnp.concatenate([keep] * (PROJ // UNIT_BLOCK), axis=1)
        slope = jnp.tanh(stat * (1.0 / CLIP))
        comm.send_all(way, (grad * (1.0 - slope * slope)).astype(jnp.bfloat16))

    def cell_step(way):
        comm.wait_all(way)
        now = time_of(way, step)
        keep = jnp.where(reset_ref[...] - way == now, 0.0, 1.0)
        grad_stat = all_ref[way].reshape(rows, PROJ)
        ds_refs[way][0] = grad_stat
        for block in range(blocks):
            cols = slice(block * wide, (block + 1) * wide)
            unit = slice(block * UNIT_BLOCK, (block + 1) * UNIT_BLOCK)
            grad_out = lax.dot_general(
                grad_stat,
                wpr_ref[way, unit, :],
                (((1,), (1,)), ((), ())),
                preferred_element_type=jnp.float32,
            )
            gates = gate_refs[way][0, :, cols]
            gate_in = gates[:, :UNIT_BLOCK]
            gate_forget = gates[:, UNIT_BLOCK : 2 * UNIT_BLOCK]
            gate_cand = gates[:, 2 * UNIT_BLOCK : 3 * UNIT_BLOCK]
            gate_out = gates[:, 3 * UNIT_BLOCK :]
            cell_prev = cprev_refs[way][0, :, unit]
            cell_new = cnew_refs[way][0, :, unit]
            tanh_cell = jnp.tanh(cell_new)
            grad_total = (
                grad_out * gate_out * (1.0 - tanh_cell * tanh_cell) + cell_ref[way, :, unit]
            )
            scaled = cell_new * (1.0 / CLIP)
            grad_inner = grad_total * (1.0 - scaled * scaled)
            cell_ref[way, :, unit] = grad_inner * gate_forget * keep
            grad_pre = jnp.concatenate(
                [
                    grad_inner * gate_cand * gate_in * (1.0 - gate_in),
                    grad_inner * cell_prev * gate_forget * (1.0 - gate_forget),
                    grad_inner * gate_in * (1.0 - gate_cand * gate_cand),
                    grad_out * tanh_cell * gate_out * (1.0 - gate_out),
                ],
                axis=1,
            ).astype(jnp.bfloat16)
            da_refs[way][0, :, cols] = grad_pre
            bias_ref[way, :, cols] += jnp.sum(
                grad_pre.astype(jnp.float32).reshape(rows // 8, 8, wide), axis=0
            )

        @pl.when(step < WIN - 1)
        def _():
            partial = lax.dot_general(
                da_refs[way][0],
                wst_ref[way],
                (((1,), (1,)), ((), ())),
                preferred_element_type=jnp.float32,
            )
            part_ref[way] = partial.astype(jnp.bfloat16).reshape(size, part, PROJ)
            comm.send_parts(way)

    def embed_step(way):
        de_refs[way][0] = lax.dot_general(
            da_refs[way][0],
            win_ref[way],
            (((1,), (1,)), ((), ())),
            preferred_element_type=jnp.float32,
        )

    @pl.when(step == 0)
    def _():
        cell_ref[...] = jnp.zeros(cell_ref.shape, jnp.float32)
        bias_ref[...] = jnp.zeros(bias_ref.shape, jnp.float32)
        mp_barrier(size)
        for way in range(2):
            stat_step(way, 0, first_cot_ref[way], first_stat_ref[way], None)

    cell_step(0)

    @pl.when(step > 0)
    def _():
        stat_step(1, step, cot1_ref[0], stat1_ref[0], comm.take_sum(1))

    embed_step(0)

    @pl.when(step < WIN - 1)
    def _():
        stat_step(0, step + 1, cot0_ref[0], stat0_ref[0], comm.take_sum(0))

    cell_step(1)
    embed_step(1)


def lstm_backward(size, gates, cprevs, cnews, cots, stats, win, wst, wpr, reset):
    rows = reset.shape[0]
    part = rows // size
    width = win.shape[2]
    units = cprevs[0].shape[2]
    last = WIN - 1
    vmem = pl.BlockSpec(memory_space=pltpu.VMEM)

    def block(shape, index):
        return pl.BlockSpec((1,) + shape, lambda w: (index(w), 0, 0))

    now0 = lambda w: last - w
    now1 = lambda w: w
    next0 = lambda w: jnp.maximum(last - 1 - w, 0)
    ins = []
    for size_of in (width, units, units):
        ins += [block((rows, size_of), now0), block((rows, size_of), now1)]
    ins += [block((part, PROJ), next0), block((part, PROJ), now1)] * 2
    ins += [vmem] * 6
    outs = []
    for size_of, kind in ((width, jnp.bfloat16), (PROJ, jnp.bfloat16), (PROJ, jnp.float32)):
        outs += [((rows, size_of), kind, now0), ((rows, size_of), kind, now1)]
    first_cot = jnp.stack([cots[0][last], cots[1][0]])
    first_stat = jnp.stack([stats[0][last], stats[1][0]])
    return pl.pallas_call(
        functools.partial(backward_kernel, size),
        grid=(WIN,),
        in_specs=ins,
        out_specs=[block(shape, index) for shape, kind, index in outs]
        + [pl.BlockSpec((2, 8, width), lambda w: (0, 0, 0))],
        out_shape=[jax.ShapeDtypeStruct((WIN,) + shape, kind) for shape, kind, index in outs]
        + [jax.ShapeDtypeStruct((2, 8, width), jnp.float32)],
        scratch_shapes=[
            pltpu.VMEM((2, rows, units), jnp.float32),
            pltpu.VMEM((2, size, part, PROJ), jnp.bfloat16),
            pltpu.VMEM((2, size, part, PROJ), jnp.bfloat16),
            pltpu.VMEM((2, size, part, PROJ), jnp.bfloat16),
        ]
        + [pltpu.SemaphoreType.DMA((2, size))] * 4,
        compiler_params=pltpu.CompilerParams(
            collective_id=2, has_side_effects=True, vmem_limit_bytes=56 * 2**20
        ),
    )(*gates, *cprevs, *cnews, *cots, *stats, win, wst, wpr, reset, first_cot, first_stat)


def shards(
    char_ids,
    doc_lengths,
    window_doc,
    window_offset,
    char_table,
    conv_weight,
    conv_bias,
    highway_weight,
    highway_bias,
    proj_weight,
    proj_bias,
    lstm_input_weight,
    lstm_state_weight,
    lstm_bias,
    lstm_proj,
    init_cell,
    init_hidden,
    cotangent,
):
    tok_share = char_ids.shape[0]
    row_count = window_doc.shape[0]
    cell_local = init_cell.shape[2]
    gate_local = lstm_bias.shape[1]
    mp_index = lax.axis_index("mp")
    mp_size = lax.axis_size("mp")
    dp_index = lax.axis_index("dp")
    dp_width = conv_weight.shape[2]
    high_low = highway_weight.astype(jnp.bfloat16)
    conv_full, high_full, proj_full = (
        lax.all_gather(conv_weight.astype(jnp.bfloat16), "dp", axis=2, tiled=True),
        lax.all_gather(high_low, "dp", axis=1, tiled=True),
        lax.all_gather(proj_weight.astype(jnp.bfloat16), "dp", axis=0, tiled=True),
    )
    input_full, state_full, lproj_full = (
        lax.all_gather(lstm_input_weight.astype(jnp.bfloat16), "dp", axis=1, tiled=True),
        lax.all_gather(lstm_state_weight.astype(jnp.bfloat16), "dp", axis=1, tiled=True),
        lax.all_gather(lstm_proj.astype(jnp.bfloat16), "dp", axis=2, tiled=True),
    )
    widths = filter_widths(FILTERS)
    tap_mask = jnp.arange(TAPS)[:, None] < widths[None, :]
    conv_matrix = (conv_full * tap_mask[:, None, :].astype(jnp.bfloat16)).reshape(
        TAPS * CDIM, FILTERS
    )
    valid_mask = (jnp.arange(CHARS)[:, None] <= CHARS - widths[None, :]).astype(jnp.float32)
    counts = (CHARS + 1 - widths).astype(jnp.float32)
    table_low = char_table.astype(jnp.bfloat16)
    block_size = math.gcd(tok_share, WIN)
    rows_own = row_count // mp_size
    char_ids = char_ids.reshape(rows_own, WIN, CHARS).transpose(1, 0, 2).reshape(tok_share, CHARS)
    id_blocks = char_ids.reshape(tok_share // block_size, block_size, CHARS)

    def pool_block(id_block):
        one_hot, columns = char_columns(id_block, table_low)
        conv_out = jnp.dot(columns, conv_matrix, preferred_element_type=jnp.float32).reshape(
            block_size, CHARS, FILTERS
        )
        exp_total = jnp.sum(jnp.exp(conv_out) * valid_mask, axis=1)
        return jnp.log(exp_total / counts)

    pooled = lax.map(pool_block, id_blocks).reshape(tok_share, FILTERS)
    pre_pool = pooled + conv_bias
    layer_value = jax.nn.silu(pre_pool)
    kept_inputs = []
    kept_mixed = []
    for layer_index in range(2):
        mixed = (
            jnp.dot(
                layer_value.astype(jnp.bfloat16),
                high_full[layer_index],
                preferred_element_type=jnp.float32,
            )
            + highway_bias[layer_index]
        )
        kept_inputs.append(layer_value)
        kept_mixed.append(mixed)
        gate_value = jax.nn.sigmoid(mixed[:, FILTERS:])
        layer_value = gate_value * layer_value + (1.0 - gate_value) * jax.nn.silu(
            mixed[:, :FILTERS]
        )
    top_low = layer_value.astype(jnp.bfloat16)
    embed_local = jnp.dot(top_low, proj_full, preferred_element_type=jnp.float32) + proj_bias
    part_rows = -(-rows_own // 16) * 16
    rows = mp_size * part_rows

    def pad_rows(value, axis):
        shape = value.shape
        split = value.reshape(shape[:axis] + (mp_size, rows_own) + shape[axis + 1 :])
        widths = [(0, 0)] * split.ndim
        widths[axis + 1] = (0, part_rows - rows_own)
        return jnp.pad(split, widths)

    def drop_rows(value, axis):
        shape = value.shape
        split = value.reshape(shape[:axis] + (mp_size, part_rows) + shape[axis + 1 :])
        kept = lax.slice_in_dim(split, 0, rows_own, axis=axis + 1)
        return kept.reshape(shape[:axis] + (row_count,) + shape[axis + 1 :])

    embed_own = jnp.pad(
        embed_local.astype(jnp.bfloat16).reshape(WIN, rows_own, PROJ),
        ((0, 0), (0, part_rows - rows_own), (0, 0)),
    )
    embed_all = lax.all_gather(embed_own, "mp", axis=0)
    doc_index = jnp.arange(doc_lengths.shape[0])
    chosen_len = jnp.sum(
        jnp.where(window_doc[:, None] == doc_index[None, :], doc_lengths[None, :], 0), axis=1
    )
    reset_at = (chosen_len - window_offset).astype(jnp.int32)
    reset_rows = pad_rows(reset_at[:, None], 0).reshape(rows, 1)
    reset_wide = jnp.broadcast_to(reset_rows, (rows, UNIT_BLOCK))
    cell_rows = pad_rows(init_cell, 1).reshape(2, rows, cell_local)
    hidden_rows = pad_rows(init_hidden, 1)
    kept = lstm_forward(
        mp_size,
        embed_all,
        input_full,
        state_full,
        lproj_full,
        lstm_bias[:, None, :],
        cell_rows,
        hidden_rows,
        reset_wide,
    )
    embed_time = kept[0]
    gates, cprevs, cnews, lows, hprevs, stats, outs = (
        kept[1 + 2 * index : 3 + 2 * index] for index in range(7)
    )
    hidden = jnp.concatenate(
        [jnp.transpose(drop_rows(value, 1), (1, 0, 2)) for value in outs], axis=-1
    )
    own_cot = lax.dynamic_slice_in_dim(cotangent, mp_index * rows_own, rows_own, 0)
    own_cot = jnp.pad(
        jnp.transpose(own_cot, (1, 0, 2)), ((0, 0), (0, part_rows - rows_own), (0, 0))
    )
    cots = (own_cot[:, :, :PROJ], own_cot[:, :, PROJ:])
    back = lstm_backward(
        mp_size, gates, cprevs, cnews, cots, stats, input_full, state_full, lproj_full, reset_wide
    )
    das, dss, des = (back[2 * index : 2 * index + 2] for index in range(3))
    grad_bias = jnp.sum(back[6], axis=1)
    embed_parts = (des[0] + des[1]).astype(jnp.bfloat16)
    embed_parts = jnp.transpose(embed_parts.reshape(WIN, mp_size, part_rows, PROJ), (1, 0, 2, 3))
    grad_embed_local = lax.psum_scatter(embed_parts, "mp", scatter_dimension=0, tiled=True)
    grad_embed_local = grad_embed_local.reshape(WIN, part_rows, PROJ)[:, :rows_own]
    grad_embed_local = grad_embed_local.reshape(tok_share, PROJ)

    def outer(left, right):
        return jnp.dot(
            left.reshape(WIN * rows, -1).T,
            right.reshape(WIN * rows, -1),
            preferred_element_type=jnp.float32,
        ).astype(jnp.bfloat16)

    grad_input = jnp.stack([outer(embed_time, das[way]) for way in range(2)])
    grad_state = jnp.stack([outer(hprevs[way], das[way]) for way in range(2)])
    grad_lproj = jnp.stack([outer(lows[way], dss[way]) for way in range(2)])
    grad_input, grad_state, grad_lproj = (
        lax.psum_scatter(grad_input, "dp", scatter_dimension=1, tiled=True).astype(jnp.float32),
        lax.psum_scatter(grad_state, "dp", scatter_dimension=1, tiled=True).astype(jnp.float32),
        lax.psum_scatter(grad_lproj, "dp", scatter_dimension=2, tiled=True).astype(jnp.float32),
    )
    grad_pb = jnp.sum(grad_embed_local.astype(jnp.float32), axis=0)
    grad_hw = [None, None]
    grad_hb = [None, None]
    grad_pw = jnp.dot(top_low.T, grad_embed_local, preferred_element_type=jnp.float32)
    grad_layer = jnp.dot(grad_embed_local, proj_full.T, preferred_element_type=jnp.float32)
    for layer_index in (1, 0):
        layer_in = kept_inputs[layer_index]
        mixed = kept_mixed[layer_index]
        transform = mixed[:, :FILTERS]
        gate_value = jax.nn.sigmoid(mixed[:, FILTERS:])
        grad_gate = (
            grad_layer * (layer_in - jax.nn.silu(transform)) * gate_value * (1.0 - gate_value)
        )
        grad_trans = grad_layer * (1.0 - gate_value) * silu_slope(transform)
        grad_mixed = jnp.concatenate([grad_trans, grad_gate], axis=1).astype(jnp.bfloat16)
        grad_hw[layer_index] = jnp.dot(
            layer_in.astype(jnp.bfloat16).T, grad_mixed, preferred_element_type=jnp.float32
        )
        grad_hb[layer_index] = jnp.sum(grad_mixed.astype(jnp.float32), axis=0)
        grad_layer = grad_layer * gate_value + jnp.dot(
            grad_mixed, high_full[layer_index].T, preferred_element_type=jnp.float32
        )
    hw_terms = jnp.stack(grad_hw).reshape(2, FILTERS, 2, FILTERS)
    grad_pre_pool = grad_layer * silu_slope(pre_pool)
    grad_cb = jnp.sum(grad_pre_pool, axis=0)

    def conv_back(carry, inputs):
        grad_conv, grad_table = carry
        id_block, grad_block = inputs
        one_hot, columns = char_columns(id_block, table_low)
        conv_out = jnp.dot(columns, conv_matrix, preferred_element_type=jnp.float32).reshape(
            block_size, CHARS, FILTERS
        )
        exp_values = jnp.exp(conv_out) * valid_mask
        exp_total = jnp.sum(exp_values, axis=1)
        grad_conv_out = (
            (grad_block[:, None, :] * exp_values / exp_total[:, None, :])
            .astype(jnp.bfloat16)
            .reshape(block_size * CHARS, FILTERS)
        )
        grad_conv = grad_conv + jnp.dot(
            columns.T, grad_conv_out, preferred_element_type=jnp.float32
        )
        grad_columns = jnp.dot(
            grad_conv_out, conv_matrix.T, preferred_element_type=jnp.float32
        ).reshape(block_size, CHARS, TAPS, CDIM)
        grad_chars = jnp.zeros((block_size, CHARS + TAPS - 1, CDIM), jnp.float32)
        for tap_index in range(TAPS):
            grad_chars = grad_chars.at[:, tap_index : tap_index + CHARS, :].add(
                grad_columns[:, :, tap_index, :]
            )
        grad_chars = grad_chars[:, :CHARS, :].reshape(block_size * CHARS, CDIM)
        grad_table = grad_table + jnp.dot(
            one_hot.astype(jnp.float32).T, grad_chars, precision=lax.Precision.HIGHEST
        )
        return ((grad_conv, grad_table), None)

    grad_blocks = grad_pre_pool.reshape(tok_share // block_size, block_size, FILTERS)
    conv_init = (
        jnp.zeros((TAPS * CDIM, FILTERS), jnp.float32),
        jnp.zeros((VOCAB, CDIM), jnp.float32),
    )
    conv_sums, unused = lax.scan(conv_back, conv_init, (id_blocks, grad_blocks))
    grad_conv = conv_sums[0].reshape(TAPS, CDIM, FILTERS) * tap_mask[:, None, :].astype(jnp.float32)
    grad_table = conv_sums[1]
    bias_placed = lax.dynamic_update_slice_in_dim(
        jnp.zeros((2, GATES), jnp.float32), grad_bias, mp_index * gate_local, 1
    )
    grad_table, grad_conv, grad_cb, grad_hbs, grad_pb, bias_placed = lax.psum(
        (grad_table, grad_conv, grad_cb, jnp.stack(grad_hb), grad_pb, bias_placed), ("dp", "mp")
    )
    grad_lbias = lax.dynamic_slice_in_dim(bias_placed, mp_index * gate_local, gate_local, 1)
    grad_cw = lax.dynamic_slice_in_dim(grad_conv, dp_index * dp_width, dp_width, 2)
    hw_part, pw_part = (
        lax.psum_scatter(
            hw_terms.astype(jnp.bfloat16), "dp", scatter_dimension=1, tiled=True
        ).astype(jnp.float32),
        lax.psum_scatter(
            grad_pw.astype(jnp.bfloat16), "dp", scatter_dimension=0, tiled=True
        ).astype(jnp.float32),
    )
    hw_sum, grad_pws = (
        lax.psum(hw_part.astype(jnp.bfloat16), "mp").astype(jnp.float32),
        lax.psum(pw_part.astype(jnp.bfloat16), "mp").astype(jnp.float32),
    )
    grad_hws = hw_sum.reshape(2, hw_sum.shape[1], 2 * FILTERS)
    return (
        hidden,
        grad_table,
        grad_cw,
        grad_cb,
        grad_hws,
        grad_hbs,
        grad_pws,
        grad_pb,
        grad_input,
        grad_state,
        grad_lbias,
        grad_lproj,
    )


def solution(mesh):
    in_specs = (
        P(("dp", "mp"), None),
        P(),
        P("dp"),
        P("dp"),
        P(),
        P(None, None, "dp"),
        P(),
        P(None, "dp", None),
        P(),
        P("dp", None),
        P(),
        P(None, "dp", "mp"),
        P(None, "dp", "mp"),
        P(None, "mp"),
        P(None, "mp", "dp"),
        P(None, "dp", "mp"),
        P(None, "dp", None),
        P("dp", None, None),
    )
    out_specs = (
        P("dp", None, None),
        P(),
        P(None, None, "dp"),
        P(),
        P(None, "dp", None),
        P(),
        P("dp", None),
        P(),
        P(None, "dp", "mp"),
        P(None, "dp", "mp"),
        P(None, "mp"),
        P(None, "mp", "dp"),
    )
    return jax.shard_map(shards, mesh=mesh, in_specs=in_specs, out_specs=out_specs, check_vma=False)
```

```python
import functools
import math

import jax
import jax.numpy as jnp
from jax import lax
from jax.experimental import pallas as pl
from jax.experimental.pallas import tpu as pltpu
from jax.sharding import PartitionSpec as P

VOCAB = 262
CHARS = 50
CDIM = 16
TAPS = 7
FILTERS = 2048
PROJ = 512
UNIT_BLOCK = 128
WIN = 20
GATES = 16384


CLIP = 3.0


def filter_widths(count):
    unit_size = count // 64
    index_row = jnp.arange(count)
    widths = jnp.ones((count,), jnp.int32)
    for exponent in range(6):
        widths = widths + (index_row >= unit_size * (1 << exponent)).astype(jnp.int32)
    return widths


def split_gates(pre_act, unit_count):
    leading = pre_act.shape[:-1]
    shaped = pre_act.reshape(leading + (unit_count // UNIT_BLOCK, 4, UNIT_BLOCK))
    return [shaped[..., gate_index, :].reshape(leading + (unit_count,)) for gate_index in range(4)]


def join_gates(gate_parts, unit_count):
    leading = gate_parts[0].shape[:-1]
    stacked = jnp.stack(
        [
            part_value.reshape(leading + (unit_count // UNIT_BLOCK, UNIT_BLOCK))
            for part_value in gate_parts
        ],
        axis=-2,
    )
    return stacked.reshape(leading + (4 * unit_count,))


def silu_slope(value):
    sigma = jax.nn.sigmoid(value)
    return sigma * (1.0 + value * (1.0 - sigma))


def sigmoid_of(value):
    return 0.5 * jnp.tanh(0.5 * value) + 0.5


def mp_barrier(size):
    me = lax.axis_index("mp")
    barrier = pltpu.get_barrier_semaphore()
    for offset in range(1, size):
        peer = lax.rem(me + offset, size)
        pl.semaphore_signal(
            barrier, inc=1, device_id={"mp": peer}, device_id_type=pl.DeviceIdType.MESH
        )
    pl.semaphore_wait(barrier, size - 1)


class Exchange:
    def __init__(self, size, part_ref, sum_ref, all_ref, sems):
        self.size = size
        self.me = lax.axis_index("mp")
        self.part_ref, self.sum_ref, self.all_ref = part_ref, sum_ref, all_ref
        self.part_send, self.part_recv, self.all_send, self.all_recv = sems

    def part_copy(self, way, offset, incoming):
        peer = lax.rem(self.me + (self.size - offset if incoming else offset), self.size)
        return pltpu.make_async_remote_copy(
            src_ref=self.part_ref.at[way, peer],
            dst_ref=self.sum_ref.at[way, peer if incoming else self.me],
            send_sem=self.part_send.at[way, offset],
            recv_sem=self.part_recv.at[way, offset],
            device_id={"mp": peer},
            device_id_type=pl.DeviceIdType.MESH,
        )

    def all_copy(self, way, offset, incoming):
        peer = lax.rem(self.me + (self.size - offset if incoming else offset), self.size)
        slot = peer if incoming else self.me
        return pltpu.make_async_remote_copy(
            src_ref=self.all_ref.at[way, slot],
            dst_ref=self.all_ref.at[way, slot],
            send_sem=self.all_send.at[way, offset],
            recv_sem=self.all_recv.at[way, offset],
            device_id={"mp": peer},
            device_id_type=pl.DeviceIdType.MESH,
        )

    def send_parts(self, way):
        for offset in range(1, self.size):
            self.part_copy(way, offset, False).start()

    def take_sum(self, way):
        total = self.part_ref[way, self.me].astype(jnp.float32)
        for offset in range(1, self.size):
            self.part_copy(way, offset, True).wait_recv()
            peer = lax.rem(self.me + self.size - offset, self.size)
            total = total + self.sum_ref[way, peer].astype(jnp.float32)
        for offset in range(1, self.size):
            self.part_copy(way, offset, False).wait_send()
        return total

    def send_all(self, way, value):
        self.all_ref[way, self.me] = value
        for offset in range(1, self.size):
            self.all_copy(way, offset, False).start()

    def wait_all(self, way):
        for offset in range(1, self.size):
            self.all_copy(way, offset, True).wait_recv()
        for offset in range(1, self.size):
            self.all_copy(way, offset, False).wait_send()


def forward_kernel(
    size,
    emb_ref,
    win_ref,
    wst_ref,
    wpr_ref,
    bias_ref,
    cell_ref,
    hid_ref,
    reset_ref,
    embt_ref,
    gate0_ref,
    gate1_ref,
    cprev0_ref,
    cprev1_ref,
    cnew0_ref,
    cnew1_ref,
    low0_ref,
    low1_ref,
    hprev0_ref,
    hprev1_ref,
    stat0_ref,
    stat1_ref,
    out0_ref,
    out1_ref,
    pre_ref,
    state_ref,
    part_ref,
    sum_ref,
    all_ref,
    part_send,
    part_recv,
    all_send,
    all_recv,
):
    step = pl.program_id(0)
    rows = reset_ref.shape[0]
    units = cell_ref.shape[2]
    blocks = units // UNIT_BLOCK
    wide = 4 * UNIT_BLOCK
    comm = Exchange(size, part_ref, sum_ref, all_ref, (part_send, part_recv, all_send, all_recv))
    gate_refs = (gate0_ref, gate1_ref)
    cprev_refs = (cprev0_ref, cprev1_ref)
    cnew_refs = (cnew0_ref, cnew1_ref)
    low_refs = (low0_ref, low1_ref)
    hprev_refs = (hprev0_ref, hprev1_ref)
    stat_refs = (stat0_ref, stat1_ref)
    out_refs = (out0_ref, out1_ref)

    def time_of(way, at):
        return at if way == 0 else WIN - 1 - at

    def input_part(way, at):
        emb = emb_ref[:, time_of(way, at)].reshape(rows, PROJ)
        for block in range(blocks):
            cols = slice(block * wide, (block + 1) * wide)
            pre_ref[way, :, cols] = (
                jnp.dot(emb, win_ref[way, :, cols], preferred_element_type=jnp.float32)
                + bias_ref[way, :, cols]
            )

    def emit_hidden(way):
        out_refs[way][0] = all_ref[way].reshape(rows, PROJ)

    def cell_step(way):
        now = time_of(way, step)
        keep = jnp.where(reset_ref[...] - way == now, 0.0, 1.0)
        keep_low = jnp.concatenate([keep.astype(jnp.bfloat16)] * (PROJ // UNIT_BLOCK), axis=1)
        hidden_prev = all_ref[way].reshape(rows, PROJ) * keep_low
        hprev_refs[way][0] = hidden_prev
        if way == 0:
            embt_ref[0] = emb_ref[:, step].reshape(rows, PROJ)
        for block in range(blocks):
            cols = slice(block * wide, (block + 1) * wide)
            unit = slice(block * UNIT_BLOCK, (block + 1) * UNIT_BLOCK)
            pre = pre_ref[way, :, cols] + jnp.dot(
                hidden_prev, wst_ref[way, :, cols], preferred_element_type=jnp.float32
            )
            gate_in = sigmoid_of(pre[:, :UNIT_BLOCK])
            gate_forget = sigmoid_of(pre[:, UNIT_BLOCK : 2 * UNIT_BLOCK])
            gate_cand = jnp.tanh(pre[:, 2 * UNIT_BLOCK : 3 * UNIT_BLOCK])
            gate_out = sigmoid_of(pre[:, 3 * UNIT_BLOCK :])
            cell_prev = state_ref[way, :, unit] * keep
            cell_new = CLIP * jnp.tanh(
                (gate_forget * cell_prev + gate_in * gate_cand) * (1.0 / CLIP)
            )
            gate_refs[way][0, :, cols] = jnp.concatenate(
                [gate_in, gate_forget, gate_cand, gate_out], axis=1
            )
            cprev_refs[way][0, :, unit] = cell_prev
            cnew_refs[way][0, :, unit] = cell_new
            state_ref[way, :, unit] = cell_new
            low_refs[way][0, :, unit] = (gate_out * jnp.tanh(cell_new)).astype(jnp.bfloat16)
        partial = jnp.dot(low_refs[way][0], wpr_ref[way], preferred_element_type=jnp.float32)
        part_ref[way] = partial.astype(jnp.bfloat16).reshape(size, rows // size, PROJ)
        comm.send_parts(way)

    def close_step(way):
        total = comm.take_sum(way)
        stat_refs[way][0] = total
        comm.send_all(way, (CLIP * jnp.tanh(total * (1.0 / CLIP))).astype(jnp.bfloat16))

    @pl.when(step == 0)
    def _():
        for way in range(2):
            all_ref[way] = hid_ref[way]
            state_ref[way] = cell_ref[way]
            input_part(way, 0)
        mp_barrier(size)

    @pl.when(step > 0)
    def _():
        comm.wait_all(0)
        emit_hidden(0)

    @pl.when(step < WIN)
    def _():
        cell_step(0)

    @pl.when(step > 0)
    def _():
        close_step(1)

    @pl.when(step < WIN)
    def _():
        @pl.when(step < WIN - 1)
        def _():
            input_part(0, step + 1)

        close_step(0)

    @pl.when(step > 0)
    def _():
        comm.wait_all(1)
        emit_hidden(1)

    @pl.when(step < WIN)
    def _():
        cell_step(1)

        @pl.when(step < WIN - 1)
        def _():
            input_part(1, step + 1)


def lstm_forward(size, emb, win, wst, wpr, bias, cell, hid, reset):
    rows = reset.shape[0]
    part = rows // size
    gates = win.shape[2]
    units = cell.shape[2]
    last = WIN - 1
    vmem = pl.BlockSpec(memory_space=pltpu.VMEM)

    def block(shape, index):
        return pl.BlockSpec((1,) + shape, lambda w: (index(w), 0, 0))

    now0 = lambda w: jnp.minimum(w, last)
    now1 = lambda w: last - jnp.minimum(w, last)
    past0 = lambda w: jnp.maximum(w - 1, 0)
    past1 = lambda w: last - jnp.maximum(w - 1, 0)
    outs = [((rows, PROJ), jnp.bfloat16, now0)]
    for width, kind in ((gates, jnp.float32), (units, jnp.float32), (units, jnp.float32), (units, jnp.bfloat16), (PROJ, jnp.bfloat16)):
        outs += [((rows, width), kind, now0), ((rows, width), kind, now1)]
    outs += [((part, PROJ), jnp.float32, now0), ((part, PROJ), jnp.float32, past1)]
    outs += [((rows, PROJ), jnp.bfloat16, past0), ((rows, PROJ), jnp.bfloat16, past1)]
    return pl.pallas_call(
        functools.partial(forward_kernel, size),
        grid=(WIN + 1,),
        in_specs=[vmem] * 8,
        out_specs=[block(shape, index) for shape, kind, index in outs],
        out_shape=[jax.ShapeDtypeStruct((WIN,) + shape, kind) for shape, kind, index in outs],
        scratch_shapes=[
            pltpu.VMEM((2, rows, gates), jnp.float32),
            pltpu.VMEM((2, rows, units), jnp.float32),
            pltpu.VMEM((2, size, part, PROJ), jnp.bfloat16),
            pltpu.VMEM((2, size, part, PROJ), jnp.bfloat16),
            pltpu.VMEM((2, size, part, PROJ), jnp.bfloat16),
        ]
        + [pltpu.SemaphoreType.DMA((2, size))] * 4,
        compiler_params=pltpu.CompilerParams(
            collective_id=1, has_side_effects=True, vmem_limit_bytes=56 * 2**20
        ),
    )(emb, win, wst, wpr, bias, cell, hid, reset)


def backward_kernel(
    size,
    gate0_ref,
    gate1_ref,
    cprev0_ref,
    cprev1_ref,
    cnew0_ref,
    cnew1_ref,
    cot0_ref,
    cot1_ref,
    stat0_ref,
    stat1_ref,
    win_ref,
    wst_ref,
    wpr_ref,
    reset_ref,
    first_cot_ref,
    first_stat_ref,
    da0_ref,
    da1_ref,
    ds0_ref,
    ds1_ref,
    bias_ref,
    de_ref,
    cell_ref,
    part_ref,
    sum_ref,
    all_ref,
    part_send,
    part_recv,
    all_send,
    all_recv,
    held_ref,
    embed_part_ref,
    embed_got_ref,
    embed_send,
    embed_recv,
):
    step = pl.program_id(0)
    rows = reset_ref.shape[0]
    part = rows // size
    units = cell_ref.shape[2]
    blocks = units // UNIT_BLOCK
    wide = 4 * UNIT_BLOCK
    comm = Exchange(size, part_ref, sum_ref, all_ref, (part_send, part_recv, all_send, all_recv))
    gate_refs = (gate0_ref, gate1_ref)
    cprev_refs = (cprev0_ref, cprev1_ref)
    cnew_refs = (cnew0_ref, cnew1_ref)
    da_refs = (da0_ref, da1_ref)
    ds_refs = (ds0_ref, ds1_ref)

    def time_of(way, at):
        return WIN - 1 - at if way == 0 else at

    def stat_step(way, at, cot, stat, total):
        grad = cot.astype(jnp.float32)
        if total is not None:
            own = reset_ref[pl.ds(comm.me * part, part), :] - way
            keep = jnp.where(own == time_of(way, at - 1), 0.0, 1.0)
            grad = grad + total * jnp.concatenate([keep] * (PROJ // UNIT_BLOCK), axis=1)
        slope = jnp.tanh(stat * (1.0 / CLIP))
        comm.send_all(way, (grad * (1.0 - slope * slope)).astype(jnp.bfloat16))

    def cell_step(way):
        comm.wait_all(way)
        now = time_of(way, step)
        keep = jnp.where(reset_ref[...] - way == now, 0.0, 1.0)
        grad_stat = all_ref[way].reshape(rows, PROJ)
        ds_refs[way][0] = grad_stat
        for block in range(blocks):
            cols = slice(block * wide, (block + 1) * wide)
            unit = slice(block * UNIT_BLOCK, (block + 1) * UNIT_BLOCK)
            grad_out = lax.dot_general(
                grad_stat,
                wpr_ref[way, unit, :],
                (((1,), (1,)), ((), ())),
                preferred_element_type=jnp.float32,
            )
            gates = gate_refs[way][0, :, cols]
            gate_in = gates[:, :UNIT_BLOCK]
            gate_forget = gates[:, UNIT_BLOCK : 2 * UNIT_BLOCK]
            gate_cand = gates[:, 2 * UNIT_BLOCK : 3 * UNIT_BLOCK]
            gate_out = gates[:, 3 * UNIT_BLOCK :]
            cell_prev = cprev_refs[way][0, :, unit]
            cell_new = cnew_refs[way][0, :, unit]
            tanh_cell = jnp.tanh(cell_new)
            grad_total = (
                grad_out * gate_out * (1.0 - tanh_cell * tanh_cell) + cell_ref[way, :, unit]
            )
            scaled = cell_new * (1.0 / CLIP)
            grad_inner = grad_total * (1.0 - scaled * scaled)
            cell_ref[way, :, unit] = grad_inner * gate_forget * keep
            grad_pre = jnp.concatenate(
                [
                    grad_inner * gate_cand * gate_in * (1.0 - gate_in),
                    grad_inner * cell_prev * gate_forget * (1.0 - gate_forget),
                    grad_inner * gate_in * (1.0 - gate_cand * gate_cand),
                    grad_out * tanh_cell * gate_out * (1.0 - gate_out),
                ],
                axis=1,
            ).astype(jnp.bfloat16)
            da_refs[way][0, :, cols] = grad_pre
            bias_ref[way, :, cols] += jnp.sum(
                grad_pre.astype(jnp.float32).reshape(rows // 8, 8, wide), axis=0
            )

        @pl.when(step < WIN - 1)
        def _():
            partial = lax.dot_general(
                da_refs[way][0],
                wst_ref[way],
                (((1,), (1,)), ((), ())),
                preferred_element_type=jnp.float32,
            )
            part_ref[way] = partial.astype(jnp.bfloat16).reshape(size, part, PROJ)
            comm.send_parts(way)

    def embed_copy(src, dst, offset):
        return pltpu.make_async_remote_copy(
            src_ref=src,
            dst_ref=dst,
            send_sem=embed_send.at[offset],
            recv_sem=embed_recv.at[offset],
            device_id={"mp": lax.rem(comm.me + offset, size)},
            device_id_type=pl.DeviceIdType.MESH,
        )

    def embed_step(way):
        now = time_of(way, step)
        value = lax.dot_general(
            da_refs[way][0],
            win_ref[way],
            (((1,), (1,)), ((), ())),
            preferred_element_type=jnp.float32,
        )

        @pl.when(step < WIN // 2)
        def _():
            held_ref[now] = value

        @pl.when(step >= WIN // 2)
        def _():
            both = (value + held_ref[now]).astype(jnp.bfloat16)
            embed_part_ref[now] = both.reshape(size, part, PROJ)
            for offset in range(1, size):
                peer = lax.rem(comm.me + offset, size)
                embed_copy(
                    embed_part_ref.at[now, peer], embed_got_ref.at[comm.me, now], offset
                ).start()

    def embed_finish():
        total = embed_part_ref[:, comm.me].astype(jnp.float32)
        for offset in range(1, size):
            peer = lax.rem(comm.me + size - offset, size)
            embed_copy(embed_got_ref.at[peer], embed_got_ref.at[peer], offset).wait_recv()
            total = total + embed_got_ref[peer].astype(jnp.float32)
        de_ref[...] = total.astype(jnp.bfloat16)
        for offset in range(1, size):
            embed_copy(embed_got_ref.at[comm.me], embed_got_ref.at[comm.me], offset).wait_send()

    @pl.when(step == 0)
    def _():
        cell_ref[...] = jnp.zeros(cell_ref.shape, jnp.float32)
        bias_ref[...] = jnp.zeros(bias_ref.shape, jnp.float32)
        mp_barrier(size)
        for way in range(2):
            stat_step(way, 0, first_cot_ref[way], first_stat_ref[way], None)

    cell_step(0)

    @pl.when(step > 0)
    def _():
        stat_step(1, step, cot1_ref[0], stat1_ref[0], comm.take_sum(1))

    embed_step(0)

    @pl.when(step < WIN - 1)
    def _():
        stat_step(0, step + 1, cot0_ref[0], stat0_ref[0], comm.take_sum(0))

    cell_step(1)
    embed_step(1)

    @pl.when(step == WIN - 1)
    def _():
        embed_finish()


def lstm_backward(size, gates, cprevs, cnews, cots, stats, win, wst, wpr, reset):
    rows = reset.shape[0]
    part = rows // size
    width = win.shape[2]
    units = cprevs[0].shape[2]
    last = WIN - 1
    vmem = pl.BlockSpec(memory_space=pltpu.VMEM)

    def block(shape, index):
        return pl.BlockSpec((1,) + shape, lambda w: (index(w), 0, 0))

    now0 = lambda w: last - w
    now1 = lambda w: w
    next0 = lambda w: jnp.maximum(last - 1 - w, 0)
    ins = []
    for size_of in (width, units, units):
        ins += [block((rows, size_of), now0), block((rows, size_of), now1)]
    ins += [block((part, PROJ), next0), block((part, PROJ), now1)] * 2
    ins += [vmem] * 6
    outs = []
    for size_of, kind in ((width, jnp.bfloat16), (PROJ, jnp.bfloat16)):
        outs += [((rows, size_of), kind, now0), ((rows, size_of), kind, now1)]
    first_cot = jnp.stack([cots[0][last], cots[1][0]])
    first_stat = jnp.stack([stats[0][last], stats[1][0]])
    return pl.pallas_call(
        functools.partial(backward_kernel, size),
        grid=(WIN,),
        in_specs=ins,
        out_specs=[block(shape, index) for shape, kind, index in outs]
        + [pl.BlockSpec((2, 8, width), lambda w: (0, 0, 0)), vmem],
        out_shape=[jax.ShapeDtypeStruct((WIN,) + shape, kind) for shape, kind, index in outs]
        + [
            jax.ShapeDtypeStruct((2, 8, width), jnp.float32),
            jax.ShapeDtypeStruct((WIN, part, PROJ), jnp.bfloat16),
        ],
        scratch_shapes=[
            pltpu.VMEM((2, rows, units), jnp.float32),
            pltpu.VMEM((2, size, part, PROJ), jnp.bfloat16),
            pltpu.VMEM((2, size, part, PROJ), jnp.bfloat16),
            pltpu.VMEM((2, size, part, PROJ), jnp.bfloat16),
        ]
        + [pltpu.SemaphoreType.DMA((2, size))] * 4
        + [
            pltpu.VMEM((WIN, rows, PROJ), jnp.float32),
            pltpu.VMEM((WIN, size, part, PROJ), jnp.bfloat16),
            pltpu.VMEM((size, WIN, part, PROJ), jnp.bfloat16),
        ]
        + [pltpu.SemaphoreType.DMA((size,))] * 2,
        compiler_params=pltpu.CompilerParams(
            collective_id=2, has_side_effects=True, vmem_limit_bytes=56 * 2**20
        ),
    )(*gates, *cprevs, *cnews, *cots, *stats, win, wst, wpr, reset, first_cot, first_stat)


SHIFTS = 8
GROUP = SHIFTS * CDIM
FBLOCK = 256


def position_bound(first, width, taps):
    index = first + lax.broadcasted_iota(jnp.int32, (1, width), 1)
    bound = jnp.full((1, width), CHARS - 1, jnp.int32)
    for exponent in range(taps - 1):
        bound = bound - (index >= (FILTERS // 64) * (1 << exponent)).astype(jnp.int32)
    return bound


def group_counts():
    full = (CHARS - SHIFTS) // SHIFTS + 1
    return full, CHARS - full * SHIFTS


def windows(vec_ref, count):
    tokens = vec_ref.shape[1]
    low = vec_ref[0:count].reshape(count * tokens, GROUP)
    high = vec_ref[1 : count + 1].reshape(count * tokens, GROUP)
    return jnp.concatenate([low, high], axis=1)


def conv_forward_kernel(ids_ref, table_ref, weight_ref, total_ref, vec_ref):
    block = pl.program_id(0)
    groups, tokens, _ = vec_ref.shape
    full, extra = group_counts()

    @pl.when(block == 0)
    def _():
        vocab = table_ref.shape[1]
        for group in range(groups):
            acc = jnp.zeros((tokens, GROUP), jnp.float32)
            for shift in range(SHIFTS):
                place = group * SHIFTS + shift
                if place < CHARS:
                    column = ids_ref[:, place : place + 1]
                    hot = column == lax.broadcasted_iota(jnp.int32, (tokens, vocab), 1)
                    acc = acc + jnp.dot(
                        jnp.where(hot, 1.0, 0.0).astype(jnp.bfloat16),
                        table_ref[shift],
                        preferred_element_type=jnp.float32,
                    )
            vec_ref[group] = acc.astype(jnp.bfloat16)

    bound = position_bound(block * FBLOCK, FBLOCK, TAPS)
    left = windows(vec_ref, full)
    total = jnp.zeros((tokens, FBLOCK), jnp.float32)
    for shift in range(SHIFTS):
        out = jnp.dot(left, weight_ref[shift], preferred_element_type=jnp.float32)
        values = jnp.exp(out).reshape(full, tokens, FBLOCK)
        for group in range(full):
            place = group * SHIFTS + shift
            term = values[group]
            if place > CHARS - TAPS:
                term = jnp.where(bound >= place, term, 0.0)
            total = total + term
    total_ref[...] = total

    @pl.when(block == 0)
    def _():
        for shift in range(extra):
            out = jnp.dot(
                vec_ref[full], weight_ref[shift, :GROUP], preferred_element_type=jnp.float32
            )
            total_ref[...] += jnp.where(bound >= full * SHIFTS + shift, jnp.exp(out), 0.0)


def conv_forward(ids, table_shift, weights):
    tokens = ids.shape[0]
    groups = -(-CHARS // SHIFTS)
    vocab = table_shift.shape[1]
    return pl.pallas_call(
        conv_forward_kernel,
        grid=(FILTERS // FBLOCK,),
        in_specs=[
            pl.BlockSpec((tokens, CHARS), lambda f: (0, 0)),
            pl.BlockSpec((SHIFTS, vocab, GROUP), lambda f: (0, 0, 0)),
            pl.BlockSpec((SHIFTS, 2 * GROUP, FBLOCK), lambda f: (0, 0, f)),
        ],
        out_specs=[
            pl.BlockSpec((tokens, FBLOCK), lambda f: (0, f)),
            pl.BlockSpec((groups, tokens, GROUP), lambda f: (0, 0, 0)),
        ],
        out_shape=[
            jax.ShapeDtypeStruct((tokens, FILTERS), jnp.float32),
            jax.ShapeDtypeStruct((groups, tokens, GROUP), jnp.bfloat16),
        ],
        compiler_params=pltpu.CompilerParams(vmem_limit_bytes=56 * 2**20),
        cost_estimate=pl.CostEstimate(
            flops=2 * tokens * CHARS * 256 * FILTERS,
            bytes_accessed=12 * 2**20,
            transcendentals=tokens * CHARS * FILTERS,
        ),
    )(ids, table_shift, weights)


def conv_shift_step(
    shift, vec_ref, turned_ref, turned_extra_ref, ratio_ref, weight_ref, grad_ref, low_ref, char_ref, held_ref
):
    groups, tokens, _ = vec_ref.shape
    full, extra = group_counts()
    left = windows(vec_ref, full)
    own_rows = pl.ds(pl.multiple_of(shift * CDIM, CDIM), TAPS * CDIM)

    @pl.when(shift == 0)
    def _():
        grad_ref[...] = jnp.zeros(grad_ref.shape, jnp.float32)
        char_ref[...] = jnp.zeros(char_ref.shape, jnp.float32)

    @pl.loop(0, FILTERS // FBLOCK)
    def _(block):
        cols = pl.ds(pl.multiple_of(block * FBLOCK, FBLOCK), FBLOCK)
        bound = position_bound(block * FBLOCK, FBLOCK, TAPS)
        ratio = ratio_ref[:, cols]
        out = jnp.dot(left, weight_ref[0, :, cols], preferred_element_type=jnp.float32)
        values = jnp.exp(out).reshape(full, tokens, FBLOCK)
        for group in range(full):
            term = values[group] * ratio
            if (group + 1) * SHIFTS - 1 > CHARS - TAPS:
                term = jnp.where(bound >= group * SHIFTS + shift, term, 0.0)
            low_ref[pl.ds(group * tokens, tokens), cols] = term.astype(jnp.bfloat16)
        held_ref[...] = jnp.dot(
            turned_ref[...], low_ref[:, cols], preferred_element_type=jnp.float32
        )
        grad_ref[:, cols] += held_ref[own_rows, :]

    back = lax.dot_general(
        low_ref[...],
        weight_ref[0],
        (((1,), (1,)), ((), ())),
        preferred_element_type=jnp.float32,
    ).reshape(full, tokens, 2 * GROUP)
    for group in range(full):
        char_ref[group] += back[group, :, :GROUP]
        char_ref[group + 1] += back[group, :, GROUP:]

    @pl.when(shift < extra)
    def _():
        cols = slice(0, FBLOCK)
        bound = position_bound(0, FBLOCK, TAPS)
        out = jnp.dot(
            vec_ref[full], weight_ref[0, :GROUP, cols], preferred_element_type=jnp.float32
        )
        term = jnp.exp(out) * ratio_ref[:, cols]
        term = jnp.where(bound >= full * SHIFTS + shift, term, 0.0).astype(jnp.bfloat16)
        held_ref[...] = jnp.concatenate(
            [
                jnp.dot(turned_extra_ref[...], term, preferred_element_type=jnp.float32),
                jnp.zeros((GROUP, FBLOCK), jnp.float32),
            ],
            axis=0,
        )
        grad_ref[:, cols] += held_ref[own_rows, :]
        char_ref[full] += lax.dot_general(
            term,
            weight_ref[0, :GROUP, cols],
            (((1,), (1,)), ((), ())),
            preferred_element_type=jnp.float32,
        )


def table_gradient(hot_ref, hot_extra_ref, char_ref, vocab):
    tokens = char_ref.shape[1]
    full, extra = group_counts()
    lane = lax.broadcasted_iota(jnp.int32, (vocab, GROUP), 1) // CDIM

    def split(value):
        high = value.astype(jnp.bfloat16)
        rest = (value - high.astype(jnp.float32)).astype(jnp.bfloat16)
        return jnp.concatenate([high, rest], axis=1)

    main = split(char_ref[0:full].reshape(full * tokens, GROUP))
    last = split(char_ref[full])
    acc = jnp.zeros((vocab, GROUP), jnp.float32)
    for at in range(SHIFTS):
        row = hot_ref[at : at + 1, :]
        hot = row == lax.broadcasted_iota(jnp.int32, (vocab, full * tokens), 0)
        out = jnp.dot(
            jnp.where(hot, 1.0, 0.0).astype(jnp.bfloat16),
            main,
            preferred_element_type=jnp.float32,
        )
        if at < extra:
            row = hot_extra_ref[at : at + 1, :]
            hot = row == lax.broadcasted_iota(jnp.int32, (vocab, tokens), 0)
            out = out + jnp.dot(
                jnp.where(hot, 1.0, 0.0).astype(jnp.bfloat16),
                last,
                preferred_element_type=jnp.float32,
            )
        acc = jnp.where(lane == at, out[:, :GROUP] + out[:, GROUP:], acc)
    return acc


def conv_backward_kernel(
    hot_ref,
    hot_extra_ref,
    vec_ref,
    turned_ref,
    turned_extra_ref,
    ratio_ref,
    weight_ref,
    grad_ref,
    table_ref,
    low_ref,
    char_ref,
    held_ref,
):
    shift = pl.program_id(0)
    conv_shift_step(
        shift, vec_ref, turned_ref, turned_extra_ref, ratio_ref, weight_ref, grad_ref, low_ref, char_ref, held_ref
    )

    @pl.when(shift == SHIFTS - 1)
    def _():
        table_ref[...] = table_gradient(hot_ref, hot_extra_ref, char_ref, table_ref.shape[0])


def conv_operands(ids, vectors):
    groups, tokens, _ = vectors.shape
    full, extra = group_counts()
    turned = jnp.transpose(vectors, (0, 2, 1))
    pieces = [
        jnp.transpose(turned[half : half + full], (1, 0, 2)).reshape(GROUP, full * tokens)
        for half in range(2)
    ]
    ids_turned = ids.T
    hot_main = jnp.transpose(ids_turned[: full * SHIFTS].reshape(full, SHIFTS, tokens), (1, 0, 2))
    hot_main = hot_main.reshape(SHIFTS, full * tokens)
    hot_extra = ids_turned[full * SHIFTS :]
    return hot_main, hot_extra, vectors, jnp.concatenate(pieces, axis=0), turned[full]


def conv_backward(ids, vectors, ratio, weights):
    groups, tokens, _ = vectors.shape
    full, _ = group_counts()
    vocab = -(-VOCAB // 8) * 8
    grad, table = pl.pallas_call(
        conv_backward_kernel,
        grid=(SHIFTS,),
        in_specs=[pl.BlockSpec(memory_space=pltpu.VMEM)] * 6
        + [pl.BlockSpec((1, 2 * GROUP, FILTERS), lambda s: (s, 0, 0))],
        out_specs=[
            pl.BlockSpec((TAPS * CDIM, FILTERS), lambda s: (0, 0)),
            pl.BlockSpec((vocab, GROUP), lambda s: (0, 0)),
        ],
        out_shape=[
            jax.ShapeDtypeStruct((TAPS * CDIM, FILTERS), jnp.float32),
            jax.ShapeDtypeStruct((vocab, GROUP), jnp.float32),
        ],
        scratch_shapes=[
            pltpu.VMEM((full * tokens, FILTERS), jnp.bfloat16),
            pltpu.VMEM((groups, tokens, GROUP), jnp.float32),
            pltpu.VMEM((2 * GROUP, FBLOCK), jnp.float32),
        ],
        compiler_params=pltpu.CompilerParams(vmem_limit_bytes=58 * 2**20),
        cost_estimate=pl.CostEstimate(
            flops=6 * tokens * CHARS * 256 * FILTERS,
            bytes_accessed=16 * 2**20,
            transcendentals=tokens * CHARS * FILTERS,
        ),
    )(*conv_operands(ids, vectors), ratio, weights)
    table = table.reshape(vocab, SHIFTS, CDIM).sum(axis=1)[:VOCAB]
    return grad, table


MESH = pl.DeviceIdType.MESH
CHUNK_ROWS = 16


def tail_kernel(
    chunks,
    hot_ref,
    hot_extra_ref,
    vec_ref,
    turned_ref,
    turned_extra_ref,
    ratio_ref,
    weight_ref,
    part1_ref,
    part0_ref,
    sum_ref,
    conv_ref,
    table_ref,
    grad_ref,
    low_ref,
    char_ref,
    held_ref,
    own_ref,
    got_y_ref,
    got_x_ref,
    got_z_ref,
    all_z_ref,
    all_x_ref,
    wide_ref,
    conv_acc_ref,
    conv_got_ref,
    conv_two_ref,
    conv_in_ref,
    table_acc_ref,
    table_got_ref,
    load_sem,
    store_sem,
    y_send,
    y_recv,
    x_send,
    x_recv,
    z_send,
    z_recv,
    g_send,
    g_recv,
    h_send,
    h_recv,
    small_send,
    small_recv,
):
    tick = pl.program_id(0)
    dp = lax.axis_index("dp")
    mp = lax.axis_index("mp")
    core, high = lax.rem(dp, 2), dp // 2
    near, ring = lax.rem(mp, 2), mp // 2
    per_layer = chunks // 2
    width = FILTERS * 2
    quarter = width // 4
    core_peer = {"dp": dp + 1 - 2 * core, "mp": mp}
    high_peer = {"dp": dp + 2 - 4 * high, "mp": mp}
    near_peer = {"dp": dp, "mp": mp + 1 - 2 * near}

    def ring_index(offset):
        return lax.rem(ring + offset, 4)

    def ring_peer(offset):
        return {"dp": dp, "mp": 2 * ring_index(offset) + near}

    def remote(src, dst, send, recv, peer):
        return pltpu.make_async_remote_copy(
            src_ref=src, dst_ref=dst, send_sem=send, recv_sem=recv, device_id=peer, device_id_type=MESH
        )

    def y_copy(part, chunk, row):
        return remote(
            part.at[1 - high, row], got_y_ref.at[chunk], y_send.at[chunk], y_recv.at[chunk], high_peer
        )

    def load(chunk, act):
        slot = lax.rem(chunk, 2)
        for layer, part in enumerate((part1_ref, part0_ref)):

            @pl.when(chunk // per_layer == layer)
            def _():
                copy = pltpu.make_async_copy(
                    part.at[high, chunk - layer * per_layer], own_ref.at[slot], load_sem.at[slot]
                )
                getattr(copy, act)()

    def x_copy(chunk):
        return remote(
            got_y_ref.at[chunk, 1 - near],
            got_x_ref.at[chunk],
            x_send.at[chunk],
            x_recv.at[chunk],
            near_peer,
        )

    def columns(index):
        return pl.ds(pl.multiple_of(index * quarter, quarter), quarter)

    def z_copy(chunk, offset):
        return remote(
            got_x_ref.at[chunk, :, columns(ring_index(offset))],
            got_z_ref.at[chunk, offset - 1],
            z_send.at[chunk, offset - 1],
            z_recv.at[chunk, offset - 1],
            ring_peer(offset),
        )

    def g_copy(chunk, offset, incoming):
        cols = columns(ring_index(4 - offset) if incoming else ring)
        return remote(
            all_z_ref.at[chunk, :, cols],
            all_z_ref.at[chunk, :, cols],
            g_send.at[chunk, offset - 1],
            g_recv.at[chunk, offset - 1],
            ring_peer(offset),
        )

    def h_copy(chunk):
        return remote(
            all_z_ref.at[chunk], all_x_ref.at[chunk], h_send.at[chunk], h_recv.at[chunk], near_peer
        )

    def store(chunk):
        slot = lax.rem(chunk, 2)
        layer = 1 - chunk // per_layer
        return pltpu.make_async_copy(
            wide_ref.at[slot],
            sum_ref.at[layer, lax.rem(chunk, per_layer)],
            store_sem.at[slot],
        )

    def when_chunk(chunk, body):
        @pl.when(jnp.logical_and(chunk >= 0, chunk < chunks))
        def _():
            body(chunk)

    def do_y(chunk):
        y_copy(part1_ref, chunk, 0).wait_recv()
        load(chunk, "wait")
        slot = lax.rem(chunk, 2)
        for half in range(2):
            got_y_ref[chunk, half] = (
                got_y_ref[chunk, half].astype(jnp.float32) + own_ref[slot, half].astype(jnp.float32)
            ).astype(jnp.bfloat16)
        x_copy(chunk).start()

        @pl.when(chunk + 2 < chunks)
        def _():
            load(chunk + 2, "start")

    def do_x(chunk):
        x_copy(chunk).wait_recv()
        got_x_ref[chunk] = (
            got_x_ref[chunk].astype(jnp.float32) + got_y_ref[chunk, near].astype(jnp.float32)
        ).astype(jnp.bfloat16)
        for offset in range(1, 4):
            z_copy(chunk, offset).start()

    def do_z(chunk):
        cols = columns(ring)
        total = got_x_ref[chunk, :, cols].astype(jnp.float32)
        for offset in range(1, 4):
            z_copy(chunk, offset).wait_recv()
            total = total + got_z_ref[chunk, offset - 1].astype(jnp.float32)
        all_z_ref[chunk, :, cols] = total.astype(jnp.bfloat16)
        for offset in range(1, 4):
            g_copy(chunk, offset, False).start()

    def do_g(chunk):
        for offset in range(1, 4):
            g_copy(chunk, offset, True).wait_recv()
        h_copy(chunk).start()

    def do_h(chunk):
        h_copy(chunk).wait_recv()

        @pl.when(chunk >= 2)
        def _():
            store(chunk - 2).wait()

        slot = lax.rem(chunk, 2)
        wide_ref[slot, near] = all_z_ref[chunk].astype(jnp.float32)
        wide_ref[slot, 1 - near] = all_x_ref[chunk].astype(jnp.float32)
        store(chunk).start()

    def small_copies(stage):
        if stage == 0:
            copies = [
                remote(
                    conv_two_ref.at[1, y],
                    conv_in_ref.at[y],
                    small_send.at[0, y],
                    small_recv.at[0, y],
                    core_peer,
                )
                for y in range(2)
            ]
            peer = core_peer
        else:
            if stage == 1:
                src = conv_two_ref.at[0, 1 - high]
                peer = high_peer
            else:
                src = conv_acc_ref.at[stage - 2]
                bit = 1 << (stage - 2)
                flip = lax.rem(mp // bit, 2)
                peer = {"dp": dp, "mp": mp + bit - 2 * bit * flip}
            copies = [
                remote(
                    src,
                    conv_got_ref.at[stage - 1],
                    small_send.at[stage, 0],
                    small_recv.at[stage, 0],
                    peer,
                )
            ]
        copies.append(
            remote(
                table_acc_ref.at[stage],
                table_got_ref.at[stage],
                small_send.at[stage, 2],
                small_recv.at[stage, 2],
                peer,
            )
        )
        return copies

    def small_start(stage):
        for copy in small_copies(stage):
            copy.start()

    def small_finish(stage):
        for copy in small_copies(stage):
            copy.wait()
        total = table_acc_ref[stage] + table_got_ref[stage]
        if stage < 4:
            table_acc_ref[stage + 1] = total
        else:
            table_ref[...] = total
        if stage == 0:
            for y in range(2):
                conv_two_ref[0, y] = conv_two_ref[0, y] + conv_in_ref[y]
        elif stage == 1:
            conv_acc_ref[0] = conv_two_ref[0, high] + conv_got_ref[0]
        else:
            value = conv_acc_ref[stage - 2] + conv_got_ref[stage - 1]
            if stage < 4:
                conv_acc_ref[stage - 1] = value
            else:
                conv_ref[...] = value

    @pl.when(tick == 0)
    def _():
        barrier = pltpu.get_barrier_semaphore()
        for peer in [core_peer, high_peer, near_peer] + [ring_peer(offset) for offset in (1, 2, 3)]:
            pl.semaphore_signal(barrier, inc=1, device_id=peer, device_id_type=MESH)
        pl.semaphore_wait(barrier, 6)

        @pl.loop(0, per_layer)
        def _(row):
            y_copy(part1_ref, row, row).start()

        @pl.loop(0, per_layer)
        def _(row):
            y_copy(part0_ref, per_layer + row, row).start()

        load(jnp.int32(0), "start")
        load(jnp.int32(1), "start")

    @pl.when(tick < SHIFTS)
    def _():
        conv_shift_step(
            tick,
            vec_ref,
            turned_ref,
            turned_extra_ref,
            ratio_ref,
            weight_ref,
            grad_ref,
            low_ref,
            char_ref,
            held_ref,
        )

    @pl.when(tick == SHIFTS - 1)
    def _():
        table_acc_ref[0] = table_gradient(hot_ref, hot_extra_ref, char_ref, table_ref.shape[0])
        span = FILTERS // 4
        for y in range(2):
            mine = pl.ds(pl.multiple_of((2 * y + core) * span, span), span)
            theirs = pl.ds(pl.multiple_of((2 * y + 1 - core) * span, span), span)
            conv_two_ref[0, y] = grad_ref[:, mine]
            conv_two_ref[1, y] = grad_ref[:, theirs]
        small_start(0)

    for stage in range(5):

        @pl.when(tick == SHIFTS + stage)
        def _():
            small_finish(stage)
            if stage < 4:
                small_start(stage + 1)

    for beat in range(2):
        at = tick * 2 + beat
        when_chunk(at, do_y)
        when_chunk(at - 1, do_x)
        when_chunk(at - 2, do_z)
        when_chunk(at - 3, do_g)
        when_chunk(at - 4, do_h)

    @pl.when(tick == chunks // 2 + 1)
    def _():
        for chunk in (chunks - 2, chunks - 1):
            store(jnp.int32(chunk)).wait()

        @pl.loop(0, chunks)
        def _(chunk):
            y_copy(part1_ref, chunk, 0).wait_send()
            x_copy(chunk).wait_send()
            for offset in range(1, 4):
                z_copy(chunk, offset).wait_send()
                g_copy(chunk, offset, False).wait_send()
            h_copy(chunk).wait_send()


def conv_backward_and_sum(ids, vectors, ratio, weights, parts):
    groups, tokens, _ = vectors.shape
    full, _ = group_counts()
    vocab = -(-VOCAB // 8) * 8
    width = parts[0].shape[1]
    rows = parts[0].shape[0] // 2
    per_layer = rows // (2 * CHUNK_ROWS)
    chunks = 2 * per_layer
    parts = [part.reshape(2, per_layer, 2, CHUNK_ROWS, width) for part in parts]
    conv_rows = TAPS * CDIM
    span = FILTERS // 4
    bf16, f32 = jnp.bfloat16, jnp.float32
    dma = pltpu.SemaphoreType.DMA
    last = SHIFTS - 1
    sums, grad, table = pl.pallas_call(
        functools.partial(tail_kernel, chunks),
        grid=(chunks // 2 + 2,),
        in_specs=[pl.BlockSpec(memory_space=pltpu.VMEM)] * 6
        + [pl.BlockSpec((1, 2 * GROUP, FILTERS), lambda t: (jnp.minimum(t, last), 0, 0))]
        + [pl.BlockSpec(memory_space=pl.ANY)] * 2,
        out_specs=[
            pl.BlockSpec(memory_space=pl.ANY),
            pl.BlockSpec(memory_space=pltpu.VMEM),
            pl.BlockSpec(memory_space=pltpu.VMEM),
        ],
        out_shape=[
            jax.ShapeDtypeStruct((2, per_layer, 2, CHUNK_ROWS, width), f32),
            jax.ShapeDtypeStruct((conv_rows, span), f32),
            jax.ShapeDtypeStruct((vocab, GROUP), f32),
        ],
        scratch_shapes=[
            pltpu.VMEM((conv_rows, FILTERS), f32),
            pltpu.VMEM((full * tokens, FILTERS), bf16),
            pltpu.VMEM((groups, tokens, GROUP), f32),
            pltpu.VMEM((2 * GROUP, FBLOCK), f32),
            pltpu.VMEM((2, 2, CHUNK_ROWS, width), bf16),
            pltpu.VMEM((chunks, 2, CHUNK_ROWS, width), bf16),
            pltpu.VMEM((chunks, CHUNK_ROWS, width), bf16),
            pltpu.VMEM((chunks, 3, CHUNK_ROWS, width // 4), bf16),
            pltpu.VMEM((chunks, CHUNK_ROWS, width), bf16),
            pltpu.VMEM((chunks, CHUNK_ROWS, width), bf16),
            pltpu.VMEM((2, 2, CHUNK_ROWS, width), f32),
            pltpu.VMEM((3, conv_rows, span), f32),
            pltpu.VMEM((4, conv_rows, span), f32),
            pltpu.VMEM((2, 2, conv_rows, span), f32),
            pltpu.VMEM((2, conv_rows, span), f32),
            pltpu.VMEM((5, vocab, GROUP), f32),
            pltpu.VMEM((5, vocab, GROUP), f32),
            dma((2,)),
            dma((2,)),
            dma((chunks,)),
            dma((chunks,)),
            dma((chunks,)),
            dma((chunks,)),
            dma((chunks, 3)),
            dma((chunks, 3)),
            dma((chunks, 3)),
            dma((chunks, 3)),
            dma((chunks,)),
            dma((chunks,)),
            dma((5, 3)),
            dma((5, 3)),
        ],
        compiler_params=pltpu.CompilerParams(
            collective_id=3, has_side_effects=True, vmem_limit_bytes=62 * 2**20
        ),
    )(*conv_operands(ids, vectors), ratio, weights, *parts)
    table = table.reshape(vocab, SHIFTS, CDIM).sum(axis=1)[:VOCAB]
    return sums.reshape(2, rows, width), grad, table


def swap(value, axis, bit):
    size = lax.axis_size(axis)
    return lax.ppermute(value, axis, [(index, index ^ bit) for index in range(size)])


def halves(value, index, dim):
    half = value.shape[dim] // 2
    own = lax.dynamic_slice_in_dim(value, index * half, half, dim)
    other = lax.dynamic_slice_in_dim(value, (1 - index) * half, half, dim)
    return own, other


def scatter_sum(value, axis, dim, paired):
    if not paired:
        return lax.psum_scatter(value, axis, scatter_dimension=dim, tiled=True)
    index = lax.axis_index(axis)
    shape = value.shape
    quarter = shape[dim] // 4
    parts = value.reshape(shape[:dim] + (2, 2, quarter) + shape[dim + 1 :])
    low, high = index % 2, index // 2
    own = lax.dynamic_index_in_dim(parts, low, dim + 1, False)
    other = lax.dynamic_index_in_dim(parts, 1 - low, dim + 1, False)
    got = swap(other, axis, 1)
    both = (own.astype(jnp.float32) + got.astype(jnp.float32)).astype(value.dtype)
    own = lax.dynamic_index_in_dim(both, high, dim, False)
    other = lax.dynamic_index_in_dim(both, 1 - high, dim, False)
    got = swap(other, axis, 2)
    return (own.astype(jnp.float32) + got.astype(jnp.float32)).astype(value.dtype)


def weight_part(left, right):
    tokens, depth = left.shape
    core = lax.axis_index("dp") % 2
    parts = left.reshape(tokens, 2, 2, depth // 4)
    own = lax.dynamic_index_in_dim(parts, core, 2, False).reshape(tokens, depth // 2)
    other = lax.dynamic_index_in_dim(parts, 1 - core, 2, False).reshape(tokens, depth // 2)
    left_all = jnp.concatenate([own, swap(other, "dp", 1)], axis=0)
    right_all = jnp.concatenate([right, swap(right, "dp", 1)], axis=0)
    return jnp.dot(left_all.T, right_all, preferred_element_type=jnp.float32).astype(jnp.bfloat16)


def weight_grad(left, right, paired):
    if not paired:
        part = jnp.dot(left.T, right, preferred_element_type=jnp.float32).astype(jnp.bfloat16)
        return lax.psum_scatter(part, "dp", scatter_dimension=0, tiled=True)
    own, other = halves(weight_part(left, right), lax.axis_index("dp") // 2, 0)
    return (own.astype(jnp.float32) + swap(other, "dp", 2).astype(jnp.float32)).astype(jnp.bfloat16)


def shards(
    char_ids,
    doc_lengths,
    window_doc,
    window_offset,
    char_table,
    conv_weight,
    conv_bias,
    highway_weight,
    highway_bias,
    proj_weight,
    proj_bias,
    lstm_input_weight,
    lstm_state_weight,
    lstm_bias,
    lstm_proj,
    init_cell,
    init_hidden,
    cotangent,
):
    tok_share = char_ids.shape[0]
    row_count = window_doc.shape[0]
    cell_local = init_cell.shape[2]
    gate_local = lstm_bias.shape[1]
    mp_index = lax.axis_index("mp")
    mp_size = lax.axis_size("mp")
    paired = lax.axis_size("dp") == 4 and mp_size == 8
    dp_index = lax.axis_index("dp")
    dp_width = conv_weight.shape[2]
    high_low = highway_weight.astype(jnp.bfloat16)
    conv_full, high_full, proj_full = (
        lax.all_gather(conv_weight.astype(jnp.bfloat16), "dp", axis=2, tiled=True),
        lax.all_gather(high_low, "dp", axis=1, tiled=True),
        lax.all_gather(proj_weight.astype(jnp.bfloat16), "dp", axis=0, tiled=True),
    )
    input_full, state_full, lproj_full = (
        lax.all_gather(lstm_input_weight.astype(jnp.bfloat16), "dp", axis=1, tiled=True),
        lax.all_gather(lstm_state_weight.astype(jnp.bfloat16), "dp", axis=1, tiled=True),
        lax.all_gather(lstm_proj.astype(jnp.bfloat16), "dp", axis=2, tiled=True),
    )
    widths = filter_widths(FILTERS)
    tap_mask = jnp.arange(TAPS)[:, None] < widths[None, :]
    conv_matrix = (conv_full * tap_mask[:, None, :].astype(jnp.bfloat16)).reshape(
        TAPS * CDIM, FILTERS
    )
    conv_shifted = jnp.stack(
        [
            jnp.pad(conv_matrix, ((CDIM * shift, 2 * GROUP - CDIM * (shift + TAPS)), (0, 0)))
            for shift in range(SHIFTS)
        ]
    )
    counts = (CHARS + 1 - widths).astype(jnp.float32)
    table_low = char_table.astype(jnp.bfloat16)
    table_shifted = jnp.stack(
        [
            jnp.pad(
                table_low,
                ((0, -VOCAB % UNIT_BLOCK), (CDIM * shift, GROUP - CDIM * (shift + 1))),
            )
            for shift in range(SHIFTS)
        ]
    )
    rows_own = row_count // mp_size
    ids_time = char_ids.reshape(rows_own, WIN, CHARS).transpose(1, 0, 2).reshape(tok_share, CHARS)
    tok_pad = -tok_share % 16
    ids_time = jnp.pad(ids_time, ((0, tok_pad), (0, 0)))
    exp_total, char_vecs = conv_forward(ids_time, table_shifted, conv_shifted)
    pooled = jnp.log(exp_total[:tok_share] / counts)
    pre_pool = pooled + conv_bias
    layer_value = jax.nn.silu(pre_pool)
    kept_inputs = []
    kept_mixed = []
    for layer_index in range(2):
        mixed = (
            jnp.dot(
                layer_value.astype(jnp.bfloat16),
                high_full[layer_index],
                preferred_element_type=jnp.float32,
            )
            + highway_bias[layer_index]
        )
        kept_inputs.append(layer_value)
        kept_mixed.append(mixed)
        gate_value = jax.nn.sigmoid(mixed[:, FILTERS:])
        layer_value = gate_value * layer_value + (1.0 - gate_value) * jax.nn.silu(
            mixed[:, :FILTERS]
        )
    top_low = layer_value.astype(jnp.bfloat16)
    embed_local = jnp.dot(top_low, proj_full, preferred_element_type=jnp.float32) + proj_bias
    part_rows = -(-rows_own // 16) * 16
    rows = mp_size * part_rows

    def pad_rows(value, axis):
        shape = value.shape
        split = value.reshape(shape[:axis] + (mp_size, rows_own) + shape[axis + 1 :])
        widths = [(0, 0)] * split.ndim
        widths[axis + 1] = (0, part_rows - rows_own)
        return jnp.pad(split, widths)

    def drop_rows(value, axis):
        shape = value.shape
        split = value.reshape(shape[:axis] + (mp_size, part_rows) + shape[axis + 1 :])
        kept = lax.slice_in_dim(split, 0, rows_own, axis=axis + 1)
        return kept.reshape(shape[:axis] + (row_count,) + shape[axis + 1 :])

    embed_own = jnp.pad(
        embed_local.astype(jnp.bfloat16).reshape(WIN, rows_own, PROJ),
        ((0, 0), (0, part_rows - rows_own), (0, 0)),
    )
    embed_all = lax.all_gather(embed_own, "mp", axis=0)
    doc_index = jnp.arange(doc_lengths.shape[0])
    chosen_len = jnp.sum(
        jnp.where(window_doc[:, None] == doc_index[None, :], doc_lengths[None, :], 0), axis=1
    )
    reset_at = (chosen_len - window_offset).astype(jnp.int32)
    reset_rows = pad_rows(reset_at[:, None], 0).reshape(rows, 1)
    reset_wide = jnp.broadcast_to(reset_rows, (rows, UNIT_BLOCK))
    cell_rows = pad_rows(init_cell, 1).reshape(2, rows, cell_local)
    hidden_rows = pad_rows(init_hidden, 1)
    kept = lstm_forward(
        mp_size,
        embed_all,
        input_full,
        state_full,
        lproj_full,
        lstm_bias[:, None, :],
        cell_rows,
        hidden_rows,
        reset_wide,
    )
    embed_time = kept[0]
    gates, cprevs, cnews, lows, hprevs, stats, outs = (
        kept[1 + 2 * index : 3 + 2 * index] for index in range(7)
    )
    hidden = jnp.concatenate(
        [jnp.transpose(drop_rows(value, 1), (1, 0, 2)) for value in outs], axis=-1
    )
    own_cot = lax.dynamic_slice_in_dim(cotangent, mp_index * rows_own, rows_own, 0)
    own_cot = jnp.pad(
        jnp.transpose(own_cot, (1, 0, 2)), ((0, 0), (0, part_rows - rows_own), (0, 0))
    )
    cots = (own_cot[:, :, :PROJ], own_cot[:, :, PROJ:])
    back = lstm_backward(
        mp_size, gates, cprevs, cnews, cots, stats, input_full, state_full, lproj_full, reset_wide
    )
    das, dss = back[0:2], back[2:4]
    grad_bias = jnp.sum(back[4], axis=1)
    grad_embed_local = back[5][:, :rows_own].reshape(tok_share, PROJ)

    def outer(left, right):
        return jnp.dot(
            left.reshape(WIN * rows, -1).T,
            right.reshape(WIN * rows, -1),
            preferred_element_type=jnp.float32,
        ).astype(jnp.bfloat16)

    grad_input, grad_state, grad_lproj = (
        jnp.stack(
            [
                scatter_sum(outer(left[way], right[way]), "dp", dim, paired).astype(jnp.float32)
                for way in range(2)
            ]
        )
        for left, right, dim in (((embed_time,) * 2, das, 0), (hprevs, das, 0), (lows, dss, 1))
    )
    grad_pb = jnp.sum(grad_embed_local.astype(jnp.float32), axis=0)
    summed = []
    grad_hb = [None, None]
    pw_part = weight_grad(top_low, grad_embed_local, paired)
    pw_sum = lax.psum(pw_part, "mp")
    grad_layer = jnp.dot(grad_embed_local, proj_full.T, preferred_element_type=jnp.float32)
    for layer_index in (1, 0):
        layer_in = kept_inputs[layer_index]
        mixed = kept_mixed[layer_index]
        transform = mixed[:, :FILTERS]
        gate_value = jax.nn.sigmoid(mixed[:, FILTERS:])
        grad_gate = (
            grad_layer * (layer_in - jax.nn.silu(transform)) * gate_value * (1.0 - gate_value)
        )
        grad_trans = grad_layer * (1.0 - gate_value) * silu_slope(transform)
        grad_mixed = jnp.concatenate([grad_trans, grad_gate], axis=1).astype(jnp.bfloat16)
        layer_low = layer_in.astype(jnp.bfloat16)
        if paired:
            summed.append(weight_part(layer_low, grad_mixed))
        else:
            summed.append(lax.psum(weight_grad(layer_low, grad_mixed, paired), "mp"))
        grad_hb[layer_index] = jnp.sum(grad_mixed.astype(jnp.float32), axis=0)
        grad_layer = grad_layer * gate_value + jnp.dot(
            grad_mixed, high_full[layer_index].T, preferred_element_type=jnp.float32
        )
    grad_pre_pool = grad_layer * silu_slope(pre_pool)
    grad_cb = jnp.sum(grad_pre_pool, axis=0)

    ratio = jnp.pad(grad_pre_pool / exp_total[:tok_share], ((0, tok_pad), (0, 0)))
    low_mask = tap_mask[:, None, :].astype(jnp.float32)
    if paired:
        grad_hws, grad_conv, grad_table = conv_backward_and_sum(
            ids_time, char_vecs, ratio, conv_shifted, summed
        )
        own_mask = lax.dynamic_slice_in_dim(low_mask, dp_index * dp_width, dp_width, 2)
        grad_cw = grad_conv.reshape(TAPS, CDIM, dp_width) * own_mask
        small = []
    else:
        grad_conv, grad_table = conv_backward(ids_time, char_vecs, ratio, conv_shifted)
        grad_conv = grad_conv.reshape(TAPS, CDIM, FILTERS) * low_mask
        small = [grad_table, grad_conv]
        grad_hws = jnp.stack([summed[1].astype(jnp.float32), summed[0].astype(jnp.float32)])
    small += [grad_cb, jnp.stack(grad_hb), grad_pb]
    flat = jnp.concatenate([value.reshape(-1) for value in small])
    flat = jnp.pad(flat, (0, -flat.size % 1024)).reshape(-1, UNIT_BLOCK)
    flat = lax.psum(flat, ("dp", "mp")).reshape(-1)
    pieces = []
    start = 0
    for value in small:
        pieces.append(flat[start : start + value.size].reshape(value.shape))
        start += value.size
    grad_cb, grad_hbs, grad_pb = pieces[-3:]
    if not paired:
        grad_table = pieces[0]
        grad_cw = lax.dynamic_slice_in_dim(pieces[1], dp_index * dp_width, dp_width, 2)
    grad_lbias = lax.psum(grad_bias, "dp")
    grad_pws = pw_sum.astype(jnp.float32)
    return (
        hidden,
        grad_table,
        grad_cw,
        grad_cb,
        grad_hws,
        grad_hbs,
        grad_pws,
        grad_pb,
        grad_input,
        grad_state,
        grad_lbias,
        grad_lproj,
    )


def solution(mesh):
    in_specs = (
        P(("dp", "mp"), None),
        P(),
        P("dp"),
        P("dp"),
        P(),
        P(None, None, "dp"),
        P(),
        P(None, "dp", None),
        P(),
        P("dp", None),
        P(),
        P(None, "dp", "mp"),
        P(None, "dp", "mp"),
        P(None, "mp"),
        P(None, "mp", "dp"),
        P(None, "dp", "mp"),
        P(None, "dp", None),
        P("dp", None, None),
    )
    out_specs = (
        P("dp", None, None),
        P(),
        P(None, None, "dp"),
        P(),
        P(None, "dp", None),
        P(),
        P("dp", None),
        P(),
        P(None, "dp", "mp"),
        P(None, "dp", "mp"),
        P(None, "mp"),
        P(None, "mp", "dp"),
    )
    return jax.shard_map(shards, mesh=mesh, in_specs=in_specs, out_specs=out_specs, check_vma=False)
```

```python
import functools
import math

import jax
import jax.numpy as jnp
from jax import lax
from jax.experimental import pallas as pl
from jax.experimental.pallas import tpu as pltpu
from jax.sharding import PartitionSpec as P

VOCAB = 262
CHARS = 50
CDIM = 16
TAPS = 7
FILTERS = 2048
PROJ = 512
UNIT_BLOCK = 128
WIN = 20
GATES = 16384


CLIP = 3.0


def filter_widths(count):
    unit_size = count // 64
    index_row = jnp.arange(count)
    widths = jnp.ones((count,), jnp.int32)
    for exponent in range(6):
        widths = widths + (index_row >= unit_size * (1 << exponent)).astype(jnp.int32)
    return widths


def silu_slope(value):
    sigma = jax.nn.sigmoid(value)
    return sigma * (1.0 + value * (1.0 - sigma))


def sigmoid_of(value):
    return 0.5 * jnp.tanh(0.5 * value) + 0.5


def mp_barrier(size):
    me = lax.axis_index("mp")
    barrier = pltpu.get_barrier_semaphore()
    for offset in range(1, size):
        peer = lax.rem(me + offset, size)
        pl.semaphore_signal(
            barrier, inc=1, device_id={"mp": peer}, device_id_type=pl.DeviceIdType.MESH
        )
    pl.semaphore_wait(barrier, size - 1)


class Exchange:
    def __init__(self, size, part_ref, sum_ref, all_ref, sems):
        self.size = size
        self.me = lax.axis_index("mp")
        self.part_ref, self.sum_ref, self.all_ref = part_ref, sum_ref, all_ref
        self.part_send, self.part_recv, self.all_send, self.all_recv = sems

    def part_copy(self, way, offset, incoming):
        peer = lax.rem(self.me + (self.size - offset if incoming else offset), self.size)
        return pltpu.make_async_remote_copy(
            src_ref=self.part_ref.at[way, peer],
            dst_ref=self.sum_ref.at[way, peer if incoming else self.me],
            send_sem=self.part_send.at[way, offset],
            recv_sem=self.part_recv.at[way, offset],
            device_id={"mp": peer},
            device_id_type=pl.DeviceIdType.MESH,
        )

    def all_copy(self, way, offset, incoming):
        peer = lax.rem(self.me + (self.size - offset if incoming else offset), self.size)
        slot = peer if incoming else self.me
        return pltpu.make_async_remote_copy(
            src_ref=self.all_ref.at[way, slot],
            dst_ref=self.all_ref.at[way, slot],
            send_sem=self.all_send.at[way, offset],
            recv_sem=self.all_recv.at[way, offset],
            device_id={"mp": peer},
            device_id_type=pl.DeviceIdType.MESH,
        )

    def send_parts(self, way):
        for offset in range(1, self.size):
            self.part_copy(way, offset, False).start()

    def take_sum(self, way):
        total = self.part_ref[way, self.me].astype(jnp.float32)
        for offset in range(1, self.size):
            self.part_copy(way, offset, True).wait_recv()
            peer = lax.rem(self.me + self.size - offset, self.size)
            total = total + self.sum_ref[way, peer].astype(jnp.float32)
        for offset in range(1, self.size):
            self.part_copy(way, offset, False).wait_send()
        return total

    def send_all(self, way, value):
        self.all_ref[way, self.me] = value
        for offset in range(1, self.size):
            self.all_copy(way, offset, False).start()

    def wait_all(self, way):
        for offset in range(1, self.size):
            self.all_copy(way, offset, True).wait_recv()
        for offset in range(1, self.size):
            self.all_copy(way, offset, False).wait_send()


def forward_kernel(
    size,
    emb_ref,
    win_ref,
    wst_ref,
    wpr_ref,
    bias_ref,
    cell_ref,
    hid_ref,
    reset_ref,
    embt_ref,
    gate0_ref,
    gate1_ref,
    cprev0_ref,
    cprev1_ref,
    cnew0_ref,
    cnew1_ref,
    low0_ref,
    low1_ref,
    hprev0_ref,
    hprev1_ref,
    stat0_ref,
    stat1_ref,
    out0_ref,
    out1_ref,
    pre_ref,
    state_ref,
    part_ref,
    sum_ref,
    all_ref,
    part_send,
    part_recv,
    all_send,
    all_recv,
):
    step = pl.program_id(0)
    rows = reset_ref.shape[0]
    units = cell_ref.shape[2]
    blocks = units // UNIT_BLOCK
    wide = 4 * UNIT_BLOCK
    comm = Exchange(size, part_ref, sum_ref, all_ref, (part_send, part_recv, all_send, all_recv))
    gate_refs = (gate0_ref, gate1_ref)
    cprev_refs = (cprev0_ref, cprev1_ref)
    cnew_refs = (cnew0_ref, cnew1_ref)
    low_refs = (low0_ref, low1_ref)
    hprev_refs = (hprev0_ref, hprev1_ref)
    stat_refs = (stat0_ref, stat1_ref)
    out_refs = (out0_ref, out1_ref)

    def time_of(way, at):
        return at if way == 0 else WIN - 1 - at

    def input_part(way, at):
        emb = emb_ref[:, time_of(way, at)].reshape(rows, PROJ)
        for block in range(blocks):
            cols = slice(block * wide, (block + 1) * wide)
            pre_ref[way, :, cols] = (
                jnp.dot(emb, win_ref[way, :, cols], preferred_element_type=jnp.float32)
                + bias_ref[way, :, cols]
            )

    def emit_hidden(way):
        out_refs[way][0] = all_ref[way].reshape(rows, PROJ)

    def cell_step(way):
        now = time_of(way, step)
        keep = jnp.where(reset_ref[...] - way == now, 0.0, 1.0)
        keep_low = jnp.concatenate([keep.astype(jnp.bfloat16)] * (PROJ // UNIT_BLOCK), axis=1)
        hidden_prev = all_ref[way].reshape(rows, PROJ) * keep_low
        hprev_refs[way][0] = hidden_prev
        if way == 0:
            embt_ref[0] = emb_ref[:, step].reshape(rows, PROJ)
        for block in range(blocks):
            cols = slice(block * wide, (block + 1) * wide)
            unit = slice(block * UNIT_BLOCK, (block + 1) * UNIT_BLOCK)
            pre = pre_ref[way, :, cols] + jnp.dot(
                hidden_prev, wst_ref[way, :, cols], preferred_element_type=jnp.float32
            )
            gate_in = sigmoid_of(pre[:, :UNIT_BLOCK])
            gate_forget = sigmoid_of(pre[:, UNIT_BLOCK : 2 * UNIT_BLOCK])
            gate_cand = jnp.tanh(pre[:, 2 * UNIT_BLOCK : 3 * UNIT_BLOCK])
            gate_out = sigmoid_of(pre[:, 3 * UNIT_BLOCK :])
            cell_prev = state_ref[way, :, unit] * keep
            cell_new = CLIP * jnp.tanh(
                (gate_forget * cell_prev + gate_in * gate_cand) * (1.0 / CLIP)
            )
            gate_refs[way][0, :, cols] = jnp.concatenate(
                [gate_in, gate_forget, gate_cand, gate_out], axis=1
            )
            cprev_refs[way][0, :, unit] = cell_prev
            cnew_refs[way][0, :, unit] = cell_new
            state_ref[way, :, unit] = cell_new
            low_refs[way][0, :, unit] = (gate_out * jnp.tanh(cell_new)).astype(jnp.bfloat16)
        partial = jnp.dot(low_refs[way][0], wpr_ref[way], preferred_element_type=jnp.float32)
        part_ref[way] = partial.astype(jnp.bfloat16).reshape(size, rows // size, PROJ)
        comm.send_parts(way)

    def close_step(way):
        total = comm.take_sum(way)
        stat_refs[way][0] = total
        comm.send_all(way, (CLIP * jnp.tanh(total * (1.0 / CLIP))).astype(jnp.bfloat16))

    @pl.when(step == 0)
    def _():
        for way in range(2):
            all_ref[way] = hid_ref[way]
            state_ref[way] = cell_ref[way]
            input_part(way, 0)
        mp_barrier(size)

    @pl.when(step > 0)
    def _():
        comm.wait_all(0)
        emit_hidden(0)

    @pl.when(step < WIN)
    def _():
        cell_step(0)

    @pl.when(step > 0)
    def _():
        close_step(1)

    @pl.when(step < WIN)
    def _():
        @pl.when(step < WIN - 1)
        def _():
            input_part(0, step + 1)

        close_step(0)

    @pl.when(step > 0)
    def _():
        comm.wait_all(1)
        emit_hidden(1)

    @pl.when(step < WIN)
    def _():
        cell_step(1)

        @pl.when(step < WIN - 1)
        def _():
            input_part(1, step + 1)


def lstm_forward(size, emb, win, wst, wpr, bias, cell, hid, reset):
    rows = reset.shape[0]
    part = rows // size
    gates = win.shape[2]
    units = cell.shape[2]
    last = WIN - 1
    vmem = pl.BlockSpec(memory_space=pltpu.VMEM)

    def block(shape, index):
        return pl.BlockSpec((1,) + shape, lambda w: (index(w), 0, 0))

    now0 = lambda w: jnp.minimum(w, last)
    now1 = lambda w: last - jnp.minimum(w, last)
    past0 = lambda w: jnp.maximum(w - 1, 0)
    past1 = lambda w: last - jnp.maximum(w - 1, 0)
    outs = [((rows, PROJ), jnp.bfloat16, now0)]
    for width, kind in ((gates, jnp.float32), (units, jnp.float32), (units, jnp.float32), (units, jnp.bfloat16), (PROJ, jnp.bfloat16)):
        outs += [((rows, width), kind, now0), ((rows, width), kind, now1)]
    outs += [((part, PROJ), jnp.float32, now0), ((part, PROJ), jnp.float32, past1)]
    outs += [((rows, PROJ), jnp.bfloat16, past0), ((rows, PROJ), jnp.bfloat16, past1)]
    return pl.pallas_call(
        functools.partial(forward_kernel, size),
        grid=(WIN + 1,),
        in_specs=[vmem] * 8,
        out_specs=[block(shape, index) for shape, kind, index in outs],
        out_shape=[jax.ShapeDtypeStruct((WIN,) + shape, kind) for shape, kind, index in outs],
        scratch_shapes=[
            pltpu.VMEM((2, rows, gates), jnp.float32),
            pltpu.VMEM((2, rows, units), jnp.float32),
            pltpu.VMEM((2, size, part, PROJ), jnp.bfloat16),
            pltpu.VMEM((2, size, part, PROJ), jnp.bfloat16),
            pltpu.VMEM((2, size, part, PROJ), jnp.bfloat16),
        ]
        + [pltpu.SemaphoreType.DMA((2, size))] * 4,
        compiler_params=pltpu.CompilerParams(
            collective_id=1, has_side_effects=True, vmem_limit_bytes=56 * 2**20
        ),
    )(emb, win, wst, wpr, bias, cell, hid, reset)


def backward_kernel(
    size,
    gate0_ref,
    gate1_ref,
    cprev0_ref,
    cprev1_ref,
    cnew0_ref,
    cnew1_ref,
    cot0_ref,
    cot1_ref,
    stat0_ref,
    stat1_ref,
    win_ref,
    wst_ref,
    wpr_ref,
    reset_ref,
    first_cot_ref,
    first_stat_ref,
    da0_ref,
    da1_ref,
    ds0_ref,
    ds1_ref,
    bias_ref,
    de_ref,
    cell_ref,
    part_ref,
    sum_ref,
    all_ref,
    part_send,
    part_recv,
    all_send,
    all_recv,
    held_ref,
    embed_part_ref,
    embed_got_ref,
    embed_send,
    embed_recv,
):
    step = pl.program_id(0)
    rows = reset_ref.shape[0]
    part = rows // size
    units = cell_ref.shape[2]
    blocks = units // UNIT_BLOCK
    wide = 4 * UNIT_BLOCK
    comm = Exchange(size, part_ref, sum_ref, all_ref, (part_send, part_recv, all_send, all_recv))
    gate_refs = (gate0_ref, gate1_ref)
    cprev_refs = (cprev0_ref, cprev1_ref)
    cnew_refs = (cnew0_ref, cnew1_ref)
    da_refs = (da0_ref, da1_ref)
    ds_refs = (ds0_ref, ds1_ref)

    def time_of(way, at):
        return WIN - 1 - at if way == 0 else at

    def stat_step(way, at, cot, stat, total):
        grad = cot.astype(jnp.float32)
        if total is not None:
            own = reset_ref[pl.ds(comm.me * part, part), :] - way
            keep = jnp.where(own == time_of(way, at - 1), 0.0, 1.0)
            grad = grad + total * jnp.concatenate([keep] * (PROJ // UNIT_BLOCK), axis=1)
        slope = jnp.tanh(stat * (1.0 / CLIP))
        comm.send_all(way, (grad * (1.0 - slope * slope)).astype(jnp.bfloat16))

    def cell_step(way):
        comm.wait_all(way)
        now = time_of(way, step)
        keep = jnp.where(reset_ref[...] - way == now, 0.0, 1.0)
        grad_stat = all_ref[way].reshape(rows, PROJ)
        ds_refs[way][0] = grad_stat
        for block in range(blocks):
            cols = slice(block * wide, (block + 1) * wide)
            unit = slice(block * UNIT_BLOCK, (block + 1) * UNIT_BLOCK)
            grad_out = lax.dot_general(
                grad_stat,
                wpr_ref[way, unit, :],
                (((1,), (1,)), ((), ())),
                preferred_element_type=jnp.float32,
            )
            gates = gate_refs[way][0, :, cols]
            gate_in = gates[:, :UNIT_BLOCK]
            gate_forget = gates[:, UNIT_BLOCK : 2 * UNIT_BLOCK]
            gate_cand = gates[:, 2 * UNIT_BLOCK : 3 * UNIT_BLOCK]
            gate_out = gates[:, 3 * UNIT_BLOCK :]
            cell_prev = cprev_refs[way][0, :, unit]
            cell_new = cnew_refs[way][0, :, unit]
            tanh_cell = jnp.tanh(cell_new)
            grad_total = (
                grad_out * gate_out * (1.0 - tanh_cell * tanh_cell) + cell_ref[way, :, unit]
            )
            scaled = cell_new * (1.0 / CLIP)
            grad_inner = grad_total * (1.0 - scaled * scaled)
            cell_ref[way, :, unit] = grad_inner * gate_forget * keep
            grad_pre = jnp.concatenate(
                [
                    grad_inner * gate_cand * gate_in * (1.0 - gate_in),
                    grad_inner * cell_prev * gate_forget * (1.0 - gate_forget),
                    grad_inner * gate_in * (1.0 - gate_cand * gate_cand),
                    grad_out * tanh_cell * gate_out * (1.0 - gate_out),
                ],
                axis=1,
            ).astype(jnp.bfloat16)
            da_refs[way][0, :, cols] = grad_pre
            bias_ref[way, :, cols] += jnp.sum(
                grad_pre.astype(jnp.float32).reshape(rows // 8, 8, wide), axis=0
            )

        @pl.when(step < WIN - 1)
        def _():
            partial = lax.dot_general(
                da_refs[way][0],
                wst_ref[way],
                (((1,), (1,)), ((), ())),
                preferred_element_type=jnp.float32,
            )
            part_ref[way] = partial.astype(jnp.bfloat16).reshape(size, part, PROJ)
            comm.send_parts(way)

    def embed_copy(src, dst, offset):
        return pltpu.make_async_remote_copy(
            src_ref=src,
            dst_ref=dst,
            send_sem=embed_send.at[offset],
            recv_sem=embed_recv.at[offset],
            device_id={"mp": lax.rem(comm.me + offset, size)},
            device_id_type=pl.DeviceIdType.MESH,
        )

    def embed_step(way):
        now = time_of(way, step)
        value = lax.dot_general(
            da_refs[way][0],
            win_ref[way],
            (((1,), (1,)), ((), ())),
            preferred_element_type=jnp.float32,
        )

        @pl.when(step < WIN // 2)
        def _():
            held_ref[now] = value

        @pl.when(step >= WIN // 2)
        def _():
            both = (value + held_ref[now]).astype(jnp.bfloat16)
            embed_part_ref[now] = both.reshape(size, part, PROJ)
            for offset in range(1, size):
                peer = lax.rem(comm.me + offset, size)
                embed_copy(
                    embed_part_ref.at[now, peer], embed_got_ref.at[comm.me, now], offset
                ).start()

    def embed_finish():
        total = embed_part_ref[:, comm.me].astype(jnp.float32)
        for offset in range(1, size):
            peer = lax.rem(comm.me + size - offset, size)
            embed_copy(embed_got_ref.at[peer], embed_got_ref.at[peer], offset).wait_recv()
            total = total + embed_got_ref[peer].astype(jnp.float32)
        de_ref[...] = total.astype(jnp.bfloat16)
        for offset in range(1, size):
            embed_copy(embed_got_ref.at[comm.me], embed_got_ref.at[comm.me], offset).wait_send()

    @pl.when(step == 0)
    def _():
        cell_ref[...] = jnp.zeros(cell_ref.shape, jnp.float32)
        bias_ref[...] = jnp.zeros(bias_ref.shape, jnp.float32)
        mp_barrier(size)
        for way in range(2):
            stat_step(way, 0, first_cot_ref[way], first_stat_ref[way], None)

    cell_step(0)

    @pl.when(step > 0)
    def _():
        stat_step(1, step, cot1_ref[0], stat1_ref[0], comm.take_sum(1))

    embed_step(0)

    @pl.when(step < WIN - 1)
    def _():
        stat_step(0, step + 1, cot0_ref[0], stat0_ref[0], comm.take_sum(0))

    cell_step(1)
    embed_step(1)

    @pl.when(step == WIN - 1)
    def _():
        embed_finish()


def lstm_backward(size, gates, cprevs, cnews, cots, stats, win, wst, wpr, reset):
    rows = reset.shape[0]
    part = rows // size
    width = win.shape[2]
    units = cprevs[0].shape[2]
    last = WIN - 1
    vmem = pl.BlockSpec(memory_space=pltpu.VMEM)

    def block(shape, index):
        return pl.BlockSpec((1,) + shape, lambda w: (index(w), 0, 0))

    now0 = lambda w: last - w
    now1 = lambda w: w
    next0 = lambda w: jnp.maximum(last - 1 - w, 0)
    ins = []
    for size_of in (width, units, units):
        ins += [block((rows, size_of), now0), block((rows, size_of), now1)]
    ins += [block((part, PROJ), next0), block((part, PROJ), now1)] * 2
    ins += [vmem] * 6
    outs = []
    for size_of, kind in ((width, jnp.bfloat16), (PROJ, jnp.bfloat16)):
        outs += [((rows, size_of), kind, now0), ((rows, size_of), kind, now1)]
    first_cot = jnp.stack([cots[0][last], cots[1][0]])
    first_stat = jnp.stack([stats[0][last], stats[1][0]])
    return pl.pallas_call(
        functools.partial(backward_kernel, size),
        grid=(WIN,),
        in_specs=ins,
        out_specs=[block(shape, index) for shape, kind, index in outs]
        + [pl.BlockSpec((2, 8, width), lambda w: (0, 0, 0)), vmem],
        out_shape=[jax.ShapeDtypeStruct((WIN,) + shape, kind) for shape, kind, index in outs]
        + [
            jax.ShapeDtypeStruct((2, 8, width), jnp.float32),
            jax.ShapeDtypeStruct((WIN, part, PROJ), jnp.bfloat16),
        ],
        scratch_shapes=[
            pltpu.VMEM((2, rows, units), jnp.float32),
            pltpu.VMEM((2, size, part, PROJ), jnp.bfloat16),
            pltpu.VMEM((2, size, part, PROJ), jnp.bfloat16),
            pltpu.VMEM((2, size, part, PROJ), jnp.bfloat16),
        ]
        + [pltpu.SemaphoreType.DMA((2, size))] * 4
        + [
            pltpu.VMEM((WIN, rows, PROJ), jnp.float32),
            pltpu.VMEM((WIN, size, part, PROJ), jnp.bfloat16),
            pltpu.VMEM((size, WIN, part, PROJ), jnp.bfloat16),
        ]
        + [pltpu.SemaphoreType.DMA((size,))] * 2,
        compiler_params=pltpu.CompilerParams(
            collective_id=2, has_side_effects=True, vmem_limit_bytes=56 * 2**20
        ),
    )(*gates, *cprevs, *cnews, *cots, *stats, win, wst, wpr, reset, first_cot, first_stat)


SHIFTS = 8
GROUP = SHIFTS * CDIM
FBLOCK = 256


def position_bound(first, width, taps):
    index = first + lax.broadcasted_iota(jnp.int32, (1, width), 1)
    bound = jnp.full((1, width), CHARS - 1, jnp.int32)
    for exponent in range(taps - 1):
        bound = bound - (index >= (FILTERS // 64) * (1 << exponent)).astype(jnp.int32)
    return bound


def group_counts():
    full = (CHARS - SHIFTS) // SHIFTS + 1
    return full, CHARS - full * SHIFTS


def windows(vec_ref, count):
    tokens = vec_ref.shape[1]
    low = vec_ref[0:count].reshape(count * tokens, GROUP)
    high = vec_ref[1 : count + 1].reshape(count * tokens, GROUP)
    return jnp.concatenate([low, high], axis=1)


def char_vectors(ids_ref, table_ref, vec_ref):
    groups, tokens, _ = vec_ref.shape
    vocab = table_ref.shape[1]
    for group in range(groups):
        acc = jnp.zeros((tokens, GROUP), jnp.float32)
        for shift in range(SHIFTS):
            place = group * SHIFTS + shift
            if place < CHARS:
                column = ids_ref[:, place : place + 1]
                hot = column == lax.broadcasted_iota(jnp.int32, (tokens, vocab), 1)
                acc = acc + jnp.dot(
                    jnp.where(hot, 1.0, 0.0).astype(jnp.bfloat16),
                    table_ref[shift],
                    preferred_element_type=jnp.float32,
                )
        vec_ref[group] = acc.astype(jnp.bfloat16)


def conv_block(block, cols, vec_ref, weight_ref, total_ref):
    _, tokens, _ = vec_ref.shape
    full, extra = group_counts()
    bound = position_bound(block * FBLOCK, FBLOCK, TAPS)
    left = windows(vec_ref, full)
    total = jnp.zeros((tokens, FBLOCK), jnp.float32)
    for shift in range(SHIFTS):
        out = jnp.dot(left, weight_ref[shift, :, cols], preferred_element_type=jnp.float32)
        values = jnp.exp(out).reshape(full, tokens, FBLOCK)
        for group in range(full):
            place = group * SHIFTS + shift
            term = values[group]
            if place > CHARS - TAPS:
                term = jnp.where(bound >= place, term, 0.0)
            total = total + term
    total_ref[:, cols] = total

    @pl.when(block == 0)
    def _():
        for shift in range(extra):
            out = jnp.dot(
                vec_ref[full], weight_ref[shift, :GROUP, cols], preferred_element_type=jnp.float32
            )
            total_ref[:, cols] += jnp.where(
                bound >= full * SHIFTS + shift, jnp.exp(out), 0.0
            )


def conv_forward_kernel(ids_ref, table_ref, weight_ref, total_ref, vec_ref):
    block = pl.program_id(0)

    @pl.when(block == 0)
    def _():
        char_vectors(ids_ref, table_ref, vec_ref)

    conv_block(block, slice(None), vec_ref, weight_ref, total_ref)


def conv_forward(ids, table_shift, weights):
    tokens = ids.shape[0]
    groups = -(-CHARS // SHIFTS)
    vocab = table_shift.shape[1]
    return pl.pallas_call(
        conv_forward_kernel,
        grid=(FILTERS // FBLOCK,),
        in_specs=[
            pl.BlockSpec((tokens, CHARS), lambda f: (0, 0)),
            pl.BlockSpec((SHIFTS, vocab, GROUP), lambda f: (0, 0, 0)),
            pl.BlockSpec((SHIFTS, 2 * GROUP, FBLOCK), lambda f: (0, 0, f)),
        ],
        out_specs=[
            pl.BlockSpec((tokens, FBLOCK), lambda f: (0, f)),
            pl.BlockSpec((groups, tokens, GROUP), lambda f: (0, 0, 0)),
        ],
        out_shape=[
            jax.ShapeDtypeStruct((tokens, FILTERS), jnp.float32),
            jax.ShapeDtypeStruct((groups, tokens, GROUP), jnp.bfloat16),
        ],
        compiler_params=pltpu.CompilerParams(vmem_limit_bytes=56 * 2**20),
        cost_estimate=pl.CostEstimate(
            flops=2 * tokens * CHARS * 256 * FILTERS,
            bytes_accessed=12 * 2**20,
            transcendentals=tokens * CHARS * FILTERS,
        ),
    )(ids, table_shift, weights)


def conv_shift_step(
    shift, vec_ref, turned_ref, turned_extra_ref, ratio_ref, weight_ref, grad_ref, low_ref, char_ref, held_ref
):
    groups, tokens, _ = vec_ref.shape
    full, extra = group_counts()
    left = windows(vec_ref, full)
    own_rows = pl.ds(pl.multiple_of(shift * CDIM, CDIM), TAPS * CDIM)

    @pl.when(shift == 0)
    def _():
        grad_ref[...] = jnp.zeros(grad_ref.shape, jnp.float32)
        char_ref[...] = jnp.zeros(char_ref.shape, jnp.float32)

    @pl.loop(0, FILTERS // FBLOCK)
    def _(block):
        cols = pl.ds(pl.multiple_of(block * FBLOCK, FBLOCK), FBLOCK)
        bound = position_bound(block * FBLOCK, FBLOCK, TAPS)
        ratio = ratio_ref[:, cols]
        out = jnp.dot(left, weight_ref[0, :, cols], preferred_element_type=jnp.float32)
        values = jnp.exp(out).reshape(full, tokens, FBLOCK)
        for group in range(full):
            term = values[group] * ratio
            if (group + 1) * SHIFTS - 1 > CHARS - TAPS:
                term = jnp.where(bound >= group * SHIFTS + shift, term, 0.0)
            low_ref[pl.ds(group * tokens, tokens), cols] = term.astype(jnp.bfloat16)
        held_ref[...] = jnp.dot(
            turned_ref[...], low_ref[:, cols], preferred_element_type=jnp.float32
        )
        grad_ref[:, cols] += held_ref[own_rows, :]

    back = lax.dot_general(
        low_ref[...],
        weight_ref[0],
        (((1,), (1,)), ((), ())),
        preferred_element_type=jnp.float32,
    ).reshape(full, tokens, 2 * GROUP)
    for group in range(full):
        char_ref[group] += back[group, :, :GROUP]
        char_ref[group + 1] += back[group, :, GROUP:]

    @pl.when(shift < extra)
    def _():
        cols = slice(0, FBLOCK)
        bound = position_bound(0, FBLOCK, TAPS)
        out = jnp.dot(
            vec_ref[full], weight_ref[0, :GROUP, cols], preferred_element_type=jnp.float32
        )
        term = jnp.exp(out) * ratio_ref[:, cols]
        term = jnp.where(bound >= full * SHIFTS + shift, term, 0.0).astype(jnp.bfloat16)
        held_ref[...] = jnp.concatenate(
            [
                jnp.dot(turned_extra_ref[...], term, preferred_element_type=jnp.float32),
                jnp.zeros((GROUP, FBLOCK), jnp.float32),
            ],
            axis=0,
        )
        grad_ref[:, cols] += held_ref[own_rows, :]
        char_ref[full] += lax.dot_general(
            term,
            weight_ref[0, :GROUP, cols],
            (((1,), (1,)), ((), ())),
            preferred_element_type=jnp.float32,
        )


def table_gradient(hot_ref, hot_extra_ref, char_ref, vocab):
    tokens = char_ref.shape[1]
    full, extra = group_counts()
    lane = lax.broadcasted_iota(jnp.int32, (vocab, GROUP), 1) // CDIM

    def split(value):
        high = value.astype(jnp.bfloat16)
        rest = (value - high.astype(jnp.float32)).astype(jnp.bfloat16)
        return jnp.concatenate([high, rest], axis=1)

    main = split(char_ref[0:full].reshape(full * tokens, GROUP))
    last = split(char_ref[full])
    acc = jnp.zeros((vocab, GROUP), jnp.float32)
    for at in range(SHIFTS):
        row = hot_ref[at : at + 1, :]
        hot = row == lax.broadcasted_iota(jnp.int32, (vocab, full * tokens), 0)
        out = jnp.dot(
            jnp.where(hot, 1.0, 0.0).astype(jnp.bfloat16),
            main,
            preferred_element_type=jnp.float32,
        )
        if at < extra:
            row = hot_extra_ref[at : at + 1, :]
            hot = row == lax.broadcasted_iota(jnp.int32, (vocab, tokens), 0)
            out = out + jnp.dot(
                jnp.where(hot, 1.0, 0.0).astype(jnp.bfloat16),
                last,
                preferred_element_type=jnp.float32,
            )
        acc = jnp.where(lane == at, out[:, :GROUP] + out[:, GROUP:], acc)
    return acc


def conv_backward_kernel(
    hot_ref,
    hot_extra_ref,
    vec_ref,
    turned_ref,
    turned_extra_ref,
    ratio_ref,
    weight_ref,
    grad_ref,
    table_ref,
    low_ref,
    char_ref,
    held_ref,
):
    shift = pl.program_id(0)
    conv_shift_step(
        shift, vec_ref, turned_ref, turned_extra_ref, ratio_ref, weight_ref, grad_ref, low_ref, char_ref, held_ref
    )

    @pl.when(shift == SHIFTS - 1)
    def _():
        table_ref[...] = table_gradient(hot_ref, hot_extra_ref, char_ref, table_ref.shape[0])


def conv_operands(ids, vectors):
    groups, tokens, _ = vectors.shape
    full, extra = group_counts()
    turned = jnp.transpose(vectors, (0, 2, 1))
    pieces = [
        jnp.transpose(turned[half : half + full], (1, 0, 2)).reshape(GROUP, full * tokens)
        for half in range(2)
    ]
    ids_turned = ids.T
    hot_main = jnp.transpose(ids_turned[: full * SHIFTS].reshape(full, SHIFTS, tokens), (1, 0, 2))
    hot_main = hot_main.reshape(SHIFTS, full * tokens)
    hot_extra = ids_turned[full * SHIFTS :]
    return hot_main, hot_extra, vectors, jnp.concatenate(pieces, axis=0), turned[full]


def conv_backward(ids, vectors, ratio, weights):
    groups, tokens, _ = vectors.shape
    full, _ = group_counts()
    vocab = -(-VOCAB // 8) * 8
    grad, table = pl.pallas_call(
        conv_backward_kernel,
        grid=(SHIFTS,),
        in_specs=[pl.BlockSpec(memory_space=pltpu.VMEM)] * 6
        + [pl.BlockSpec((1, 2 * GROUP, FILTERS), lambda s: (s, 0, 0))],
        out_specs=[
            pl.BlockSpec((TAPS * CDIM, FILTERS), lambda s: (0, 0)),
            pl.BlockSpec((vocab, GROUP), lambda s: (0, 0)),
        ],
        out_shape=[
            jax.ShapeDtypeStruct((TAPS * CDIM, FILTERS), jnp.float32),
            jax.ShapeDtypeStruct((vocab, GROUP), jnp.float32),
        ],
        scratch_shapes=[
            pltpu.VMEM((full * tokens, FILTERS), jnp.bfloat16),
            pltpu.VMEM((groups, tokens, GROUP), jnp.float32),
            pltpu.VMEM((2 * GROUP, FBLOCK), jnp.float32),
        ],
        compiler_params=pltpu.CompilerParams(vmem_limit_bytes=58 * 2**20),
        cost_estimate=pl.CostEstimate(
            flops=6 * tokens * CHARS * 256 * FILTERS,
            bytes_accessed=16 * 2**20,
            transcendentals=tokens * CHARS * FILTERS,
        ),
    )(*conv_operands(ids, vectors), ratio, weights)
    table = table.reshape(vocab, SHIFTS, CDIM).sum(axis=1)[:VOCAB]
    return grad, table


MESH = pl.DeviceIdType.MESH
CHUNK_ROWS = 16
SLACK = 2
BEATS = 2
AHEAD = 2
BIAS_ROWS = 32


def tail_kernel(
    chunks,
    hot_ref,
    hot_extra_ref,
    vec_ref,
    turned_ref,
    turned_extra_ref,
    ratio_ref,
    weight_ref,
    part1_ref,
    part0_ref,
    part2_ref,
    small_ref,
    sum_ref,
    conv_ref,
    table_ref,
    grad_ref,
    low_ref,
    char_ref,
    held_ref,
    own_ref,
    got_y_ref,
    got_x_ref,
    got_z_ref,
    all_z_ref,
    all_x_ref,
    wide_ref,
    conv_acc_ref,
    conv_got_ref,
    conv_two_ref,
    conv_in_ref,
    table_acc_ref,
    table_got_ref,
    load_sem,
    store_sem,
    y_send,
    y_recv,
    x_send,
    x_recv,
    z_send,
    z_recv,
    g_send,
    g_recv,
    h_send,
    h_recv,
    small_send,
    small_recv,
):
    tick = pl.program_id(0)
    dp = lax.axis_index("dp")
    mp = lax.axis_index("mp")
    core, high = lax.rem(dp, 2), dp // 2
    near, ring = lax.rem(mp, 2), mp // 2
    per_layer = part1_ref.shape[1]
    width = FILTERS * 2
    quarter = width // 4
    parts = (part1_ref, part0_ref, part2_ref)
    vocab = table_ref.shape[0] - small_ref.shape[0]
    core_peer = {"dp": dp + 1 - 2 * core, "mp": mp}
    high_peer = {"dp": dp + 2 - 4 * high, "mp": mp}
    near_peer = {"dp": dp, "mp": mp + 1 - 2 * near}

    def ring_index(offset):
        return lax.rem(ring + offset, 4)

    def ring_peer(offset):
        return {"dp": dp, "mp": 2 * ring_index(offset) + near}

    def remote(src, dst, send, recv, peer):
        return pltpu.make_async_remote_copy(
            src_ref=src, dst_ref=dst, send_sem=send, recv_sem=recv, device_id=peer, device_id_type=MESH
        )

    def y_copy(part, chunk, row):
        return remote(
            part.at[1 - high, row], got_y_ref.at[chunk], y_send.at[chunk], y_recv.at[chunk], high_peer
        )

    def y_start(chunk):
        for layer, part in enumerate(parts):

            @pl.when(chunk // per_layer == layer)
            def _():
                y_copy(part, chunk, chunk - layer * per_layer).start()

    def load(chunk, act):
        slot = lax.rem(chunk, 2)
        for layer, part in enumerate(parts):

            @pl.when(chunk // per_layer == layer)
            def _():
                copy = pltpu.make_async_copy(
                    part.at[high, chunk - layer * per_layer], own_ref.at[slot], load_sem.at[slot]
                )
                getattr(copy, act)()

    def x_copy(chunk):
        return remote(
            got_y_ref.at[chunk, 1 - near],
            got_x_ref.at[chunk],
            x_send.at[chunk],
            x_recv.at[chunk],
            near_peer,
        )

    def columns(index):
        return pl.ds(pl.multiple_of(index * quarter, quarter), quarter)

    def z_copy(chunk, offset):
        return remote(
            got_x_ref.at[chunk, :, columns(ring_index(offset))],
            got_z_ref.at[chunk, offset - 1],
            z_send.at[chunk, offset - 1],
            z_recv.at[chunk, offset - 1],
            ring_peer(offset),
        )

    def g_copy(chunk, offset, incoming):
        cols = columns(ring_index(4 - offset) if incoming else ring)
        return remote(
            all_z_ref.at[chunk, :, cols],
            all_z_ref.at[chunk, :, cols],
            g_send.at[chunk, offset - 1],
            g_recv.at[chunk, offset - 1],
            ring_peer(offset),
        )

    def h_copy(chunk):
        return remote(
            all_z_ref.at[chunk], all_x_ref.at[chunk], h_send.at[chunk], h_recv.at[chunk], near_peer
        )

    def store(chunk):
        slot = lax.rem(chunk, 2)
        return pltpu.make_async_copy(wide_ref.at[slot], sum_ref.at[chunk], store_sem.at[slot])

    def when_chunk(chunk, body):
        @pl.when(jnp.logical_and(chunk >= 0, chunk < chunks))
        def _():
            body(chunk)

    def do_y(chunk):
        y_copy(part1_ref, chunk, 0).wait_recv()
        load(chunk, "wait")
        slot = lax.rem(chunk, 2)
        for half in range(2):
            got_y_ref[chunk, half] = (
                got_y_ref[chunk, half].astype(jnp.float32) + own_ref[slot, half].astype(jnp.float32)
            ).astype(jnp.bfloat16)
        x_copy(chunk).start()

        @pl.when(chunk + AHEAD < chunks)
        def _():
            y_start(chunk + AHEAD)

        @pl.when(chunk + 2 < chunks)
        def _():
            load(chunk + 2, "start")

    def do_x(chunk):
        x_copy(chunk).wait_recv()
        got_x_ref[chunk] = (
            got_x_ref[chunk].astype(jnp.float32) + got_y_ref[chunk, near].astype(jnp.float32)
        ).astype(jnp.bfloat16)
        for offset in range(1, 4):
            z_copy(chunk, offset).start()

    def do_z(chunk):
        cols = columns(ring)
        total = got_x_ref[chunk, :, cols].astype(jnp.float32)
        for offset in range(1, 4):
            z_copy(chunk, offset).wait_recv()
            total = total + got_z_ref[chunk, offset - 1].astype(jnp.float32)
        all_z_ref[chunk, :, cols] = total.astype(jnp.bfloat16)
        for offset in range(1, 4):
            g_copy(chunk, offset, False).start()

    def do_g(chunk):
        for offset in range(1, 4):
            g_copy(chunk, offset, True).wait_recv()
        h_copy(chunk).start()

    def do_h(chunk):
        h_copy(chunk).wait_recv()

        @pl.when(chunk >= 2)
        def _():
            store(chunk - 2).wait()

        slot = lax.rem(chunk, 2)
        wide_ref[slot, near] = all_z_ref[chunk]
        wide_ref[slot, 1 - near] = all_x_ref[chunk]
        store(chunk).start()

    def small_copies(stage):
        if stage == 0:
            copies = [
                remote(
                    conv_two_ref.at[1, y],
                    conv_in_ref.at[y],
                    small_send.at[0, y],
                    small_recv.at[0, y],
                    core_peer,
                )
                for y in range(2)
            ]
            peer = core_peer
        else:
            if stage == 1:
                src = conv_two_ref.at[0, 1 - high]
                peer = high_peer
            else:
                src = conv_acc_ref.at[stage - 2]
                bit = 1 << (stage - 2)
                flip = lax.rem(mp // bit, 2)
                peer = {"dp": dp, "mp": mp + bit - 2 * bit * flip}
            copies = [
                remote(
                    src,
                    conv_got_ref.at[stage - 1],
                    small_send.at[stage, 0],
                    small_recv.at[stage, 0],
                    peer,
                )
            ]
        count = table_ref.shape[0] - (BIAS_ROWS if stage > 1 else 0)
        copies.append(
            remote(
                table_acc_ref.at[stage, pl.ds(0, count)],
                table_got_ref.at[stage, pl.ds(0, count)],
                small_send.at[stage, 2],
                small_recv.at[stage, 2],
                peer,
            )
        )
        return copies

    def small_start(stage):
        for copy in small_copies(stage):
            copy.start()

    def small_finish(stage):
        for copy in small_copies(stage):
            copy.wait()
        count = table_ref.shape[0] - (BIAS_ROWS if stage > 1 else 0)
        total = table_acc_ref[stage, :count] + table_got_ref[stage, :count]
        if stage == 1:
            table_ref[count - BIAS_ROWS :] = total[count - BIAS_ROWS :]
        if stage < 4:
            table_acc_ref[stage + 1, :count] = total
        else:
            table_ref[:count] = total
        if stage == 0:
            for y in range(2):
                conv_two_ref[0, y] = conv_two_ref[0, y] + conv_in_ref[y]
        elif stage == 1:
            conv_acc_ref[0] = conv_two_ref[0, high] + conv_got_ref[0]
        else:
            value = conv_acc_ref[stage - 2] + conv_got_ref[stage - 1]
            if stage < 4:
                conv_acc_ref[stage - 1] = value
            else:
                conv_ref[...] = value

    @pl.when(tick == 0)
    def _():
        barrier = pltpu.get_barrier_semaphore()
        for peer in [core_peer, high_peer, near_peer] + [ring_peer(offset) for offset in (1, 2, 3)]:
            pl.semaphore_signal(barrier, inc=1, device_id=peer, device_id_type=MESH)
        pl.semaphore_wait(barrier, 6)

        for chunk in range(AHEAD):
            y_start(jnp.int32(chunk))

        load(jnp.int32(0), "start")
        load(jnp.int32(1), "start")

    @pl.when(tick < SHIFTS)
    def _():
        conv_shift_step(
            tick,
            vec_ref,
            turned_ref,
            turned_extra_ref,
            ratio_ref,
            weight_ref,
            grad_ref,
            low_ref,
            char_ref,
            held_ref,
        )

    @pl.when(tick == SHIFTS - 1)
    def _():
        table_acc_ref[0, :vocab] = table_gradient(hot_ref, hot_extra_ref, char_ref, vocab)
        table_acc_ref[0, vocab:] = small_ref[...]
        span = FILTERS // 4
        for y in range(2):
            mine = pl.ds(pl.multiple_of((2 * y + core) * span, span), span)
            theirs = pl.ds(pl.multiple_of((2 * y + 1 - core) * span, span), span)
            conv_two_ref[0, y] = grad_ref[:, mine]
            conv_two_ref[1, y] = grad_ref[:, theirs]
        small_start(0)

    for stage in range(5):

        @pl.when(tick == SHIFTS + stage)
        def _():
            small_finish(stage)
            if stage < 4:
                small_start(stage + 1)

    for beat in range(BEATS):
        at = tick * BEATS + beat
        when_chunk(at, do_y)
        when_chunk(at - SLACK, do_x)
        when_chunk(at - 2 * SLACK, do_z)
        when_chunk(at - 3 * SLACK, do_g)
        when_chunk(at - 4 * SLACK, do_h)

    @pl.when(tick == pl.num_programs(0) - 1)
    def _():
        for chunk in (chunks - 2, chunks - 1):
            store(jnp.int32(chunk)).wait()

        @pl.loop(0, chunks)
        def _(chunk):
            y_copy(part1_ref, chunk, 0).wait_send()
            x_copy(chunk).wait_send()
            for offset in range(1, 4):
                z_copy(chunk, offset).wait_send()
                g_copy(chunk, offset, False).wait_send()
            h_copy(chunk).wait_send()


def conv_backward_and_sum(ids, vectors, ratio, weights, parts, small):
    groups, tokens, _ = vectors.shape
    full, _ = group_counts()
    vocab = -(-VOCAB // 8) * 8
    width = parts[0].shape[1]
    parts = [part.reshape(2, -1, 2, CHUNK_ROWS, width) for part in parts]
    chunks = sum(part.shape[1] for part in parts)
    table_rows = vocab + small.shape[0]
    conv_rows = TAPS * CDIM
    span = FILTERS // 4
    bf16, f32 = jnp.bfloat16, jnp.float32
    dma = pltpu.SemaphoreType.DMA
    last = SHIFTS - 1
    sums, grad, table = pl.pallas_call(
        functools.partial(tail_kernel, chunks),
        grid=(-(-(chunks + 4 * SLACK) // BEATS),),
        in_specs=[pl.BlockSpec(memory_space=pltpu.VMEM)] * 6
        + [pl.BlockSpec((1, 2 * GROUP, FILTERS), lambda t: (jnp.minimum(t, last), 0, 0))]
        + [pl.BlockSpec(memory_space=pl.ANY)] * 3
        + [pl.BlockSpec(memory_space=pltpu.VMEM)],
        out_specs=[
            pl.BlockSpec(memory_space=pl.ANY),
            pl.BlockSpec(memory_space=pltpu.VMEM),
            pl.BlockSpec(memory_space=pltpu.VMEM),
        ],
        out_shape=[
            jax.ShapeDtypeStruct((chunks, 2, CHUNK_ROWS, width), bf16),
            jax.ShapeDtypeStruct((conv_rows, span), f32),
            jax.ShapeDtypeStruct((table_rows, GROUP), f32),
        ],
        scratch_shapes=[
            pltpu.VMEM((conv_rows, FILTERS), f32),
            pltpu.VMEM((full * tokens, FILTERS), bf16),
            pltpu.VMEM((groups, tokens, GROUP), f32),
            pltpu.VMEM((2 * GROUP, FBLOCK), f32),
            pltpu.VMEM((2, 2, CHUNK_ROWS, width), bf16),
            pltpu.VMEM((chunks, 2, CHUNK_ROWS, width), bf16),
            pltpu.VMEM((chunks, CHUNK_ROWS, width), bf16),
            pltpu.VMEM((chunks, 3, CHUNK_ROWS, width // 4), bf16),
            pltpu.VMEM((chunks, CHUNK_ROWS, width), bf16),
            pltpu.VMEM((chunks, CHUNK_ROWS, width), bf16),
            pltpu.VMEM((2, 2, CHUNK_ROWS, width), bf16),
            pltpu.VMEM((3, conv_rows, span), f32),
            pltpu.VMEM((4, conv_rows, span), f32),
            pltpu.VMEM((2, 2, conv_rows, span), f32),
            pltpu.VMEM((2, conv_rows, span), f32),
            pltpu.VMEM((5, table_rows, GROUP), f32),
            pltpu.VMEM((5, table_rows, GROUP), f32),
            dma((2,)),
            dma((2,)),
            dma((chunks,)),
            dma((chunks,)),
            dma((chunks,)),
            dma((chunks,)),
            dma((chunks, 3)),
            dma((chunks, 3)),
            dma((chunks, 3)),
            dma((chunks, 3)),
            dma((chunks,)),
            dma((chunks,)),
            dma((5, 3)),
            dma((5, 3)),
        ],
        compiler_params=pltpu.CompilerParams(
            collective_id=3, has_side_effects=True, vmem_limit_bytes=62 * 2**20
        ),
    )(*conv_operands(ids, vectors), ratio, weights, *parts, small)
    rest = table[vocab:]
    table = table[:vocab].reshape(vocab, SHIFTS, CDIM).sum(axis=1)[:VOCAB]
    found = []
    start = 0
    for part in parts:
        found.append(sums[start : start + part.shape[1]].reshape(-1, width))
        start += part.shape[1]
    return found, grad, table, rest


GROUPS = tuple(("high", layer, part) for layer in range(2) for part in range(2)) + (("proj", 0, 0),)
LOCAL = tuple((item, side) for item in range(3) for side in range(2))
START_STEPS = len(LOCAL) + 4


def start_kernel(
    ids_ref,
    table_ref,
    conv_ref,
    high_ref,
    proj_ref,
    win_ref,
    wst_ref,
    wpr_ref,
    total_ref,
    vec_ref,
    weight_ref,
    high_all,
    proj_all,
    win_all,
    wst_all,
    wpr_all,
    conv_got,
    conv_send,
    conv_recv,
    own_sem,
    core_send,
    core_recv,
    y_send,
    y_recv,
    x_send,
    x_recv,
    z_send,
    z_recv,
    c_send,
    c_recv,
    ly_send,
    ly_recv,
    lc_send,
    lc_recv,
):
    step = pl.program_id(0)
    dp = lax.axis_index("dp")
    mp = lax.axis_index("mp")
    core, high = lax.rem(dp, 2), dp // 2
    near, ring = lax.rem(mp, 2), lax.rem(mp // 2, 2)
    across = dp + 2 - 4 * high
    core_peer = {"dp": dp + 1 - 2 * core, "mp": mp}
    high_peer = {"dp": across, "mp": mp}
    both_peer = {"dp": across + 1 - 2 * core, "mp": mp}
    near_peer = {"dp": dp, "mp": mp + 1 - 2 * near}
    ring_peer = {"dp": dp, "mp": mp + 2 - 4 * ring}
    lanes = wpr_ref.shape[2]
    mine = 2 * ring + near
    beside = 2 * ring + 1 - near
    beyond = 2 * (1 - ring)

    def from_shard(index, place):
        kind, layer, part = GROUPS[index]
        if kind == "high":
            return high_ref.at[layer, 4 * part + place]
        return proj_ref.at[place]

    def in_full(index, place, quarter):
        kind, layer, part = GROUPS[index]
        if kind == "high":
            return high_all.at[layer, quarter, 4 * part + place]
        return proj_all.at[quarter, place]

    def local_full(item, side, quarter):
        if item == 2:
            cols = pl.ds(pl.multiple_of(quarter * lanes, lanes), lanes)
            return wpr_all.at[side, :, cols]
        return (win_all, wst_all)[item].at[side, quarter]

    def own_pair(index):
        if index < 2:
            return high_ref.at[index], high_all.at[index, dp]
        if index == 2:
            return proj_ref, proj_all.at[dp]
        item, side = LOCAL[index - 3]
        return (win_ref, wst_ref, wpr_ref)[item].at[side], local_full(item, side, dp)

    owned = 3 + len(LOCAL)

    def remote(src, dst, send, recv, peer):
        return pltpu.make_async_remote_copy(
            src_ref=src, dst_ref=dst, send_sem=send, recv_sem=recv, device_id=peer, device_id_type=MESH
        )

    def own_copy(index):
        src, dst = own_pair(index)
        return pltpu.make_async_copy(src, dst, own_sem.at[index])

    def core_copy(index):
        src, dst = own_pair(index)
        return remote(src, dst, core_send.at[index], core_recv.at[index], core_peer)

    def y_copy(index):
        return remote(
            from_shard(index, mine),
            in_full(index, mine, dp),
            y_send.at[index],
            y_recv.at[index],
            high_peer,
        )

    def x_copy(index):
        place = in_full(index, mine, across)
        return remote(place, place, x_send.at[index], x_recv.at[index], near_peer)

    def z_copy(index, which):
        place = in_full(index, 2 * ring + which, across)
        return remote(
            place, place, z_send.at[index, which], z_recv.at[index, which], ring_peer
        )

    def c_copy(index, place):
        ref = in_full(index, place, across)
        return remote(ref, ref, c_send.at[index, place], c_recv.at[index, place], core_peer)

    def ly_copy(index):
        item, side = LOCAL[index]
        return remote(
            (win_ref, wst_ref, wpr_ref)[item].at[side],
            local_full(item, side, dp),
            ly_send.at[index],
            ly_recv.at[index],
            high_peer,
        )

    def lc_copy(index):
        item, side = LOCAL[index]
        ref = local_full(item, side, across)
        return remote(ref, ref, lc_send.at[index], lc_recv.at[index], core_peer)

    conv_peers = (core_peer, high_peer, both_peer)

    def conv_copy(index):
        return remote(
            conv_ref, conv_got.at[dp], conv_send.at[index], conv_recv.at[index], conv_peers[index]
        )

    @pl.when(step == 0)
    def _():
        barrier = pltpu.get_barrier_semaphore()
        for peer in (core_peer, high_peer, both_peer, near_peer, ring_peer):
            pl.semaphore_signal(barrier, inc=1, device_id=peer, device_id_type=MESH)
        pl.semaphore_wait(barrier, 5)
        for index in range(3):
            conv_copy(index).start()
        y_copy(0).start()
        y_copy(1).start()
        ly_copy(0).start()
        for index in range(2):
            core_copy(index).start()
            own_copy(index).start()
        char_vectors(ids_ref, table_ref, vec_ref)
        weight_ref[...] = jnp.zeros(weight_ref.shape, jnp.bfloat16)
        conv_got[dp] = conv_ref[...]
        for index in range(3):
            conv_copy(index).wait()
        span = conv_ref.shape[1]
        tap = lax.broadcasted_iota(jnp.int32, (TAPS * CDIM, span), 0) // CDIM
        for quarter in range(4):
            bound = position_bound(quarter * span, span, TAPS)
            part = conv_got[quarter]
            part = part * jnp.where(tap < CHARS - bound, 1.0, 0.0).astype(jnp.bfloat16)
            for shift in range(SHIFTS):
                weight_ref[
                    shift,
                    CDIM * shift : CDIM * (shift + TAPS),
                    quarter * span : (quarter + 1) * span,
                ] = part

    for index in range(len(GROUPS)):

        @pl.when(step == index + 1)
        def _():
            y_copy(index).wait_recv()
            if index + 2 < len(GROUPS):
                y_copy(index + 2).start()
            x_copy(index).start()
            z_copy(index, near).start()
            c_copy(index, mine).start()

        @pl.when(step == index + 2)
        def _():
            x_copy(index).wait_recv()
            z_copy(index, 1 - near).start()
            c_copy(index, beside).start()

        @pl.when(step == index + 3)
        def _():
            for which in range(2):
                z_copy(index, which).wait_recv()
                c_copy(index, beyond + which).start()

    for index in range(len(LOCAL)):
        if index:

            @pl.when(step == index)
            def _():
                ly_copy(index).start()

        @pl.when(step == index + 1)
        def _():
            core_copy(index + 3).start()
            own_copy(index + 3).start()

        @pl.when(step == index + 3)
        def _():
            ly_copy(index).wait_recv()
            lc_copy(index).start()

    @pl.when(step == 1)
    def _():
        core_copy(2).start()
        own_copy(2).start()

    @pl.when(jnp.logical_and(step >= 1, step <= FILTERS // (2 * FBLOCK)))
    def _():
        for half in range(2):
            block = 2 * (step - 1) + half
            cols = pl.ds(pl.multiple_of(block * FBLOCK, FBLOCK), FBLOCK)
            conv_block(block, cols, vec_ref, weight_ref, total_ref)

    @pl.when(step == START_STEPS - 1)
    def _():
        for index in range(owned):
            own_copy(index).wait()
            core_copy(index).wait()
        for index in range(len(GROUPS)):
            y_copy(index).wait_send()
            x_copy(index).wait_send()
            for which in range(2):
                z_copy(index, which).wait_send()
            for place in range(4):
                c_copy(index, place).wait()
        for index in range(len(LOCAL)):
            ly_copy(index).wait_send()
            lc_copy(index).wait()


def start_gather(ids, table_shift, conv, highway, proj, win, wst, wpr):
    tokens = ids.shape[0]
    groups = -(-CHARS // SHIFTS)
    bf16 = jnp.bfloat16
    depth, wide = highway.shape[1:]
    rows = proj.shape[0]
    highway = highway.reshape(2, 8, depth // 8, wide)
    proj = proj.reshape(4, rows // 4, PROJ)
    vmem = pl.BlockSpec(memory_space=pltpu.VMEM)
    hbm = pl.BlockSpec(memory_space=pl.ANY)
    dma = pltpu.SemaphoreType.DMA
    count, local = len(GROUPS), len(LOCAL)
    total, vec, weight, high, proj, win, wst, wpr = pl.pallas_call(
        start_kernel,
        grid=(START_STEPS,),
        in_specs=[vmem] * 8,
        out_specs=[vmem] * 3 + [hbm] * 5,
        out_shape=[
            jax.ShapeDtypeStruct((tokens, FILTERS), jnp.float32),
            jax.ShapeDtypeStruct((groups, tokens, GROUP), bf16),
            jax.ShapeDtypeStruct((SHIFTS, 2 * GROUP, FILTERS), bf16),
            jax.ShapeDtypeStruct((2, 4) + highway.shape[1:], bf16),
            jax.ShapeDtypeStruct((4,) + proj.shape, bf16),
            jax.ShapeDtypeStruct((2, 4) + win.shape[1:], bf16),
            jax.ShapeDtypeStruct((2, 4) + wst.shape[1:], bf16),
            jax.ShapeDtypeStruct(wpr.shape[:2] + (4 * wpr.shape[2],), bf16),
        ],
        scratch_shapes=[pltpu.VMEM((4,) + conv.shape, bf16)]
        + [dma((3,))] * 2
        + [dma((3 + local,))] * 3
        + [dma((count,))] * 4
        + [dma((count, 2))] * 2
        + [dma((count, 4))] * 2
        + [dma((local,))] * 4,
        compiler_params=pltpu.CompilerParams(
            collective_id=4, has_side_effects=True, vmem_limit_bytes=40 * 2**20
        ),
    )(ids, table_shift, conv, highway, proj, win, wst, wpr)
    return (
        total,
        vec,
        weight,
        high.reshape(2, 4 * depth, wide),
        proj.reshape(4 * rows, PROJ),
        win.reshape(2, PROJ, -1),
        wst.reshape(2, PROJ, -1),
        wpr,
    )


def swap(value, axis, bit):
    size = lax.axis_size(axis)
    return lax.ppermute(value, axis, [(index, index ^ bit) for index in range(size)])


def scatter_start(value, axis, dim):
    index = lax.axis_index(axis)
    quarter = value.shape[dim] // 4
    low, high = index % 2, index // 2

    def pick(side, part):
        return lax.dynamic_slice_in_dim(value, (2 * side + part) * quarter, quarter, dim)

    def both(side):
        got = swap(pick(side, 1 - low), axis, 1)
        return (pick(side, low).astype(jnp.float32) + got.astype(jnp.float32)).astype(value.dtype)

    return both(high), swap(both(1 - high), axis, 2)


def weight_part(left, right):
    tokens, depth = left.shape
    core = lax.axis_index("dp") % 2
    quarter = depth // 4

    def columns(which):
        return jnp.concatenate(
            [
                lax.dynamic_slice_in_dim(left, (2 * half + which) * quarter, quarter, 1)
                for half in range(2)
            ],
            axis=1,
        )

    own, other = columns(core), columns(1 - core)
    left_all = jnp.concatenate([own, swap(other, "dp", 1)], axis=0)
    right_all = jnp.concatenate([right, swap(right, "dp", 1)], axis=0)
    return jnp.dot(left_all.T, right_all, preferred_element_type=jnp.float32).astype(jnp.bfloat16)


def weight_grad(left, right):
    part = jnp.dot(left.T, right, preferred_element_type=jnp.float32).astype(jnp.bfloat16)
    return lax.psum_scatter(part, "dp", scatter_dimension=0, tiled=True)


def shards(
    char_ids,
    doc_lengths,
    window_doc,
    window_offset,
    char_table,
    conv_weight,
    conv_bias,
    highway_weight,
    highway_bias,
    proj_weight,
    proj_bias,
    lstm_input_weight,
    lstm_state_weight,
    lstm_bias,
    lstm_proj,
    init_cell,
    init_hidden,
    cotangent,
):
    tok_share = char_ids.shape[0]
    row_count = window_doc.shape[0]
    cell_local = init_cell.shape[2]
    gate_local = lstm_bias.shape[1]
    mp_index = lax.axis_index("mp")
    mp_size = lax.axis_size("mp")
    paired = lax.axis_size("dp") == 4 and mp_size == 8
    dp_index = lax.axis_index("dp")
    dp_width = conv_weight.shape[2]
    widths = filter_widths(FILTERS)
    tap_mask = jnp.arange(TAPS)[:, None] < widths[None, :]
    lows = [
        value.astype(jnp.bfloat16)
        for value in (
            conv_weight,
            highway_weight,
            proj_weight,
            lstm_input_weight,
            lstm_state_weight,
            lstm_proj,
        )
    ]
    counts = (CHARS + 1 - widths).astype(jnp.float32)
    table_low = char_table.astype(jnp.bfloat16)
    table_shifted = jnp.stack(
        [
            jnp.pad(
                table_low,
                ((0, -VOCAB % UNIT_BLOCK), (CDIM * shift, GROUP - CDIM * (shift + 1))),
            )
            for shift in range(SHIFTS)
        ]
    )
    rows_own = row_count // mp_size
    ids_time = char_ids.reshape(rows_own, WIN, CHARS).transpose(1, 0, 2).reshape(tok_share, CHARS)
    tok_pad = -tok_share % 16
    ids_time = jnp.pad(ids_time, ((0, tok_pad), (0, 0)))
    if paired:
        lows[0] = lows[0].reshape(TAPS * CDIM, dp_width)
        (
            exp_total,
            char_vecs,
            conv_shifted,
            high_full,
            proj_full,
            input_full,
            state_full,
            lproj_full,
        ) = start_gather(ids_time, table_shifted, *lows)
    else:
        conv_full, high_full, proj_full, input_full, state_full, lproj_full = (
            lax.all_gather(value, "dp", axis=dim, tiled=True)
            for value, dim in zip(lows, (2, 1, 0, 1, 1, 2))
        )
        conv_matrix = (conv_full * tap_mask[:, None, :].astype(jnp.bfloat16)).reshape(
            TAPS * CDIM, FILTERS
        )
        conv_shifted = jnp.stack(
            [
                jnp.pad(conv_matrix, ((CDIM * shift, 2 * GROUP - CDIM * (shift + TAPS)), (0, 0)))
                for shift in range(SHIFTS)
            ]
        )
        exp_total, char_vecs = conv_forward(ids_time, table_shifted, conv_shifted)
    pooled = jnp.log(exp_total[:tok_share] / counts)
    pre_pool = pooled + conv_bias
    layer_value = jax.nn.silu(pre_pool)
    kept_inputs = []
    kept_mixed = []
    for layer_index in range(2):
        mixed = (
            jnp.dot(
                layer_value.astype(jnp.bfloat16),
                high_full[layer_index],
                preferred_element_type=jnp.float32,
            )
            + highway_bias[layer_index]
        )
        kept_inputs.append(layer_value)
        kept_mixed.append(mixed)
        gate_value = jax.nn.sigmoid(mixed[:, FILTERS:])
        layer_value = gate_value * layer_value + (1.0 - gate_value) * jax.nn.silu(
            mixed[:, :FILTERS]
        )
    top_low = layer_value.astype(jnp.bfloat16)
    embed_local = jnp.dot(top_low, proj_full, preferred_element_type=jnp.float32) + proj_bias
    part_rows = -(-rows_own // 16) * 16
    rows = mp_size * part_rows

    def pad_rows(value, axis):
        shape = value.shape
        split = value.reshape(shape[:axis] + (mp_size, rows_own) + shape[axis + 1 :])
        widths = [(0, 0)] * split.ndim
        widths[axis + 1] = (0, part_rows - rows_own)
        return jnp.pad(split, widths)

    def drop_rows(value, axis):
        shape = value.shape
        split = value.reshape(shape[:axis] + (mp_size, part_rows) + shape[axis + 1 :])
        kept = lax.slice_in_dim(split, 0, rows_own, axis=axis + 1)
        return kept.reshape(shape[:axis] + (row_count,) + shape[axis + 1 :])

    embed_own = jnp.pad(
        embed_local.astype(jnp.bfloat16).reshape(WIN, rows_own, PROJ),
        ((0, 0), (0, part_rows - rows_own), (0, 0)),
    )
    embed_all = lax.all_gather(embed_own, "mp", axis=0)
    doc_index = jnp.arange(doc_lengths.shape[0])
    chosen_len = jnp.sum(
        jnp.where(window_doc[:, None] == doc_index[None, :], doc_lengths[None, :], 0), axis=1
    )
    reset_at = (chosen_len - window_offset).astype(jnp.int32)
    reset_rows = pad_rows(reset_at[:, None], 0).reshape(rows, 1)
    reset_wide = jnp.broadcast_to(reset_rows, (rows, UNIT_BLOCK))
    cell_rows = pad_rows(init_cell, 1).reshape(2, rows, cell_local)
    hidden_rows = pad_rows(init_hidden, 1)
    kept = lstm_forward(
        mp_size,
        embed_all,
        input_full,
        state_full,
        lproj_full,
        lstm_bias[:, None, :],
        cell_rows,
        hidden_rows,
        reset_wide,
    )
    embed_time = kept[0]
    gates, cprevs, cnews, lows, hprevs, stats, outs = (
        kept[1 + 2 * index : 3 + 2 * index] for index in range(7)
    )
    hidden = jnp.concatenate(
        [jnp.transpose(drop_rows(value, 1), (1, 0, 2)) for value in outs], axis=-1
    )
    own_cot = lax.dynamic_slice_in_dim(cotangent, mp_index * rows_own, rows_own, 0)
    own_cot = jnp.pad(
        jnp.transpose(own_cot, (1, 0, 2)), ((0, 0), (0, part_rows - rows_own), (0, 0))
    )
    cots = (own_cot[:, :, :PROJ], own_cot[:, :, PROJ:])
    back = lstm_backward(
        mp_size, gates, cprevs, cnews, cots, stats, input_full, state_full, lproj_full, reset_wide
    )
    das, dss = back[0:2], back[2:4]
    grad_bias = jnp.sum(back[4], axis=1)
    grad_embed_local = back[5][:, :rows_own].reshape(tok_share, PROJ)

    def outer(left, right):
        return jnp.dot(
            left.reshape(WIN * rows, -1).T,
            right.reshape(WIN * rows, -1),
            preferred_element_type=jnp.float32,
        ).astype(jnp.bfloat16)

    grad_pb = jnp.sum(grad_embed_local.astype(jnp.float32), axis=0)
    summed = []
    grad_hb = [None, None]
    grad_layer = jnp.dot(grad_embed_local, proj_full.T, preferred_element_type=jnp.float32)
    for layer_index in (1, 0):
        layer_in = kept_inputs[layer_index]
        mixed = kept_mixed[layer_index]
        transform = mixed[:, :FILTERS]
        gate_value = jax.nn.sigmoid(mixed[:, FILTERS:])
        grad_gate = (
            grad_layer * (layer_in - jax.nn.silu(transform)) * gate_value * (1.0 - gate_value)
        )
        grad_trans = grad_layer * (1.0 - gate_value) * silu_slope(transform)
        grad_mixed = jnp.concatenate([grad_trans, grad_gate], axis=1).astype(jnp.bfloat16)
        layer_low = layer_in.astype(jnp.bfloat16)
        if paired:
            summed.append(weight_part(layer_low, grad_mixed))
        else:
            summed.append(lax.psum(weight_grad(layer_low, grad_mixed), "mp"))
        grad_hb[layer_index] = jnp.sum(grad_mixed.astype(jnp.float32), axis=0)
        grad_layer = grad_layer * gate_value + jnp.dot(
            grad_mixed, high_full[layer_index].T, preferred_element_type=jnp.float32
        )
    grad_pre_pool = grad_layer * silu_slope(pre_pool)
    grad_cb = jnp.sum(grad_pre_pool, axis=0)

    ratio = jnp.pad(grad_pre_pool / exp_total[:tok_share], ((0, tok_pad), (0, 0)))
    low_mask = tap_mask[:, None, :].astype(jnp.float32)
    das, dss, _ = lax.optimization_barrier((das, dss, ratio))
    lstm_parts = [
        (outer(left[way], right[way]), dim)
        for left, right, dim in (((embed_time,) * 2, das, 0), (hprevs, das, 0), (lows, dss, 1))
        for way in range(2)
    ]
    shared = [grad_cb, jnp.stack(grad_hb), grad_pb]

    def flatten(values, unit):
        flat = jnp.concatenate([value.reshape(-1) for value in values])
        return jnp.pad(flat, (0, -flat.size % unit)).reshape(-1, UNIT_BLOCK)

    def unflatten(flat, values):
        flat, pieces, start = flat.reshape(-1), [], 0
        for value in values:
            pieces.append(flat[start : start + value.size].reshape(value.shape))
            start += value.size
        return pieces

    if paired:
        lstm_parts = [scatter_start(part, "dp", dim) for part, dim in lstm_parts]
        pw_part = weight_part(top_low, grad_embed_local).reshape(2, -1, summed[0].shape[1])
        small = flatten(shared, 8 * UNIT_BLOCK)
        count = small.shape[0]
        small = jnp.concatenate([small, grad_bias.reshape(BIAS_ROWS, UNIT_BLOCK)])
        (high_one, high_zero, pw_sum), grad_conv, grad_table, rest = conv_backward_and_sum(
            ids_time, char_vecs, ratio, conv_shifted, summed + [pw_part], small
        )
        lstm_parts, rest = lax.optimization_barrier((lstm_parts, rest))
        lstm_parts = [
            own.astype(jnp.float32) + got.astype(jnp.float32) for own, got in lstm_parts
        ]
        own_mask = lax.dynamic_slice_in_dim(low_mask, dp_index * dp_width, dp_width, 2)
        grad_cw = grad_conv.reshape(TAPS, CDIM, dp_width) * own_mask
        grad_cb, grad_hbs, grad_pb = unflatten(rest[:count], shared)
        grad_lbias = rest[count:].reshape(grad_bias.shape)
        grad_hws = jnp.stack([high_zero.astype(jnp.float32), high_one.astype(jnp.float32)])
        grad_pws = pw_sum.reshape(-1, PROJ).astype(jnp.float32)
    else:
        lstm_parts = [
            lax.psum_scatter(part, "dp", scatter_dimension=dim, tiled=True).astype(jnp.float32)
            for part, dim in lstm_parts
        ]
        pw_part = weight_grad(top_low, grad_embed_local)
        grad_pws = lax.psum(pw_part, "mp").astype(jnp.float32)
        grad_conv, grad_table = conv_backward(ids_time, char_vecs, ratio, conv_shifted)
        grad_conv = grad_conv.reshape(TAPS, CDIM, FILTERS) * low_mask
        grad_hws = jnp.stack([summed[1].astype(jnp.float32), summed[0].astype(jnp.float32)])
        shared = [grad_table, grad_conv] + shared
        flat = lax.psum(flatten(shared, 8 * UNIT_BLOCK), ("dp", "mp"))
        grad_table, grad_conv, grad_cb, grad_hbs, grad_pb = unflatten(flat, shared)
        grad_cw = lax.dynamic_slice_in_dim(grad_conv, dp_index * dp_width, dp_width, 2)
        grad_lbias = lax.psum(grad_bias, "dp")
    grad_input, grad_state, grad_lproj = (
        jnp.stack(lstm_parts[2 * index : 2 * index + 2]) for index in range(3)
    )
    return (
        hidden,
        grad_table,
        grad_cw,
        grad_cb,
        grad_hws,
        grad_hbs,
        grad_pws,
        grad_pb,
        grad_input,
        grad_state,
        grad_lbias,
        grad_lproj,
    )


def solution(mesh):
    in_specs = (
        P(("dp", "mp"), None),
        P(),
        P("dp"),
        P("dp"),
        P(),
        P(None, None, "dp"),
        P(),
        P(None, "dp", None),
        P(),
        P("dp", None),
        P(),
        P(None, "dp", "mp"),
        P(None, "dp", "mp"),
        P(None, "mp"),
        P(None, "mp", "dp"),
        P(None, "dp", "mp"),
        P(None, "dp", None),
        P("dp", None, None),
    )
    out_specs = (
        P("dp", None, None),
        P(),
        P(None, None, "dp"),
        P(),
        P(None, "dp", None),
        P(),
        P("dp", None),
        P(),
        P(None, "dp", "mp"),
        P(None, "dp", "mp"),
        P(None, "mp"),
        P(None, "mp", "dp"),
    )
    return jax.shard_map(shards, mesh=mesh, in_specs=in_specs, out_specs=out_specs, check_vma=False)
```

```python
import functools
import math

import jax
import jax.numpy as jnp
from jax import lax
from jax.experimental import pallas as pl
from jax.experimental.pallas import tpu as pltpu
from jax.sharding import PartitionSpec as P

VOCAB = 262
CHARS = 50
CDIM = 16
TAPS = 7
FILTERS = 2048
PROJ = 512
UNIT_BLOCK = 128
WIN = 20
GATES = 16384


CLIP = 3.0


def filter_widths(count):
    unit_size = count // 64
    index_row = jnp.arange(count)
    widths = jnp.ones((count,), jnp.int32)
    for exponent in range(6):
        widths = widths + (index_row >= unit_size * (1 << exponent)).astype(jnp.int32)
    return widths


def silu_slope(value):
    sigma = jax.nn.sigmoid(value)
    return sigma * (1.0 + value * (1.0 - sigma))


def sigmoid_of(value):
    return 0.5 * jnp.tanh(0.5 * value) + 0.5


def mp_barrier(size):
    me = lax.axis_index("mp")
    barrier = pltpu.get_barrier_semaphore()
    for offset in range(1, size):
        peer = lax.rem(me + offset, size)
        pl.semaphore_signal(
            barrier, inc=1, device_id={"mp": peer}, device_id_type=pl.DeviceIdType.MESH
        )
    pl.semaphore_wait(barrier, size - 1)


class Exchange:
    def __init__(self, size, part_ref, sum_ref, all_ref, sems):
        self.size = size
        self.me = lax.axis_index("mp")
        self.part_ref, self.sum_ref, self.all_ref = part_ref, sum_ref, all_ref
        self.part_send, self.part_recv, self.all_send, self.all_recv = sems

    def part_copy(self, way, offset, incoming):
        peer = lax.rem(self.me + (self.size - offset if incoming else offset), self.size)
        return pltpu.make_async_remote_copy(
            src_ref=self.part_ref.at[way, peer],
            dst_ref=self.sum_ref.at[way, peer if incoming else self.me],
            send_sem=self.part_send.at[way, offset],
            recv_sem=self.part_recv.at[way, offset],
            device_id={"mp": peer},
            device_id_type=pl.DeviceIdType.MESH,
        )

    def all_copy(self, way, offset, incoming):
        peer = lax.rem(self.me + (self.size - offset if incoming else offset), self.size)
        slot = peer if incoming else self.me
        return pltpu.make_async_remote_copy(
            src_ref=self.all_ref.at[way, slot],
            dst_ref=self.all_ref.at[way, slot],
            send_sem=self.all_send.at[way, offset],
            recv_sem=self.all_recv.at[way, offset],
            device_id={"mp": peer},
            device_id_type=pl.DeviceIdType.MESH,
        )

    def send_parts(self, way):
        for offset in range(1, self.size):
            self.part_copy(way, offset, False).start()

    def take_sum(self, way):
        total = self.part_ref[way, self.me].astype(jnp.float32)
        for offset in range(1, self.size):
            self.part_copy(way, offset, True).wait_recv()
            peer = lax.rem(self.me + self.size - offset, self.size)
            total = total + self.sum_ref[way, peer].astype(jnp.float32)
        for offset in range(1, self.size):
            self.part_copy(way, offset, False).wait_send()
        return total

    def send_all(self, way, value):
        self.all_ref[way, self.me] = value
        for offset in range(1, self.size):
            self.all_copy(way, offset, False).start()

    def wait_all(self, way):
        for offset in range(1, self.size):
            self.all_copy(way, offset, True).wait_recv()
        for offset in range(1, self.size):
            self.all_copy(way, offset, False).wait_send()


def forward_kernel(
    size,
    emb_ref,
    win_ref,
    wst_ref,
    wpr_ref,
    bias_ref,
    cell_ref,
    hid_ref,
    reset_ref,
    embt_ref,
    gate0_ref,
    gate1_ref,
    cprev0_ref,
    cprev1_ref,
    cnew0_ref,
    cnew1_ref,
    low0_ref,
    low1_ref,
    hprev0_ref,
    hprev1_ref,
    stat0_ref,
    stat1_ref,
    out0_ref,
    out1_ref,
    pre_ref,
    state_ref,
    part_ref,
    sum_ref,
    all_ref,
    part_send,
    part_recv,
    all_send,
    all_recv,
):
    step = pl.program_id(0)
    rows = reset_ref.shape[0]
    units = cell_ref.shape[2]
    blocks = units // UNIT_BLOCK
    wide = 4 * UNIT_BLOCK
    comm = Exchange(size, part_ref, sum_ref, all_ref, (part_send, part_recv, all_send, all_recv))
    gate_refs = (gate0_ref, gate1_ref)
    cprev_refs = (cprev0_ref, cprev1_ref)
    cnew_refs = (cnew0_ref, cnew1_ref)
    low_refs = (low0_ref, low1_ref)
    hprev_refs = (hprev0_ref, hprev1_ref)
    stat_refs = (stat0_ref, stat1_ref)
    out_refs = (out0_ref, out1_ref)

    def time_of(way, at):
        return at if way == 0 else WIN - 1 - at

    def input_part(way, at):
        emb = emb_ref[:, time_of(way, at)].reshape(rows, PROJ)
        for block in range(blocks):
            cols = slice(block * wide, (block + 1) * wide)
            pre_ref[way, :, cols] = (
                jnp.dot(emb, win_ref[way, :, cols], preferred_element_type=jnp.float32)
                + bias_ref[way, :, cols]
            )

    def emit_hidden(way):
        out_refs[way][0] = all_ref[way].reshape(rows, PROJ)

    def cell_step(way):
        now = time_of(way, step)
        keep = jnp.where(reset_ref[...] - way == now, 0.0, 1.0)
        keep_low = jnp.concatenate([keep.astype(jnp.bfloat16)] * (PROJ // UNIT_BLOCK), axis=1)
        hidden_prev = all_ref[way].reshape(rows, PROJ) * keep_low
        hprev_refs[way][0] = hidden_prev
        if way == 0:
            embt_ref[0] = emb_ref[:, step].reshape(rows, PROJ)
        for block in range(blocks):
            cols = slice(block * wide, (block + 1) * wide)
            unit = slice(block * UNIT_BLOCK, (block + 1) * UNIT_BLOCK)
            pre = pre_ref[way, :, cols] + jnp.dot(
                hidden_prev, wst_ref[way, :, cols], preferred_element_type=jnp.float32
            )
            gate_in = sigmoid_of(pre[:, :UNIT_BLOCK])
            gate_forget = sigmoid_of(pre[:, UNIT_BLOCK : 2 * UNIT_BLOCK])
            gate_cand = jnp.tanh(pre[:, 2 * UNIT_BLOCK : 3 * UNIT_BLOCK])
            gate_out = sigmoid_of(pre[:, 3 * UNIT_BLOCK :])
            cell_prev = state_ref[way, :, unit] * keep
            cell_new = CLIP * jnp.tanh(
                (gate_forget * cell_prev + gate_in * gate_cand) * (1.0 / CLIP)
            )
            gate_refs[way][0, :, cols] = jnp.concatenate(
                [gate_in, gate_forget, gate_cand, gate_out], axis=1
            )
            cprev_refs[way][0, :, unit] = cell_prev
            cnew_refs[way][0, :, unit] = cell_new
            state_ref[way, :, unit] = cell_new
            low_refs[way][0, :, unit] = (gate_out * jnp.tanh(cell_new)).astype(jnp.bfloat16)
        partial = jnp.dot(low_refs[way][0], wpr_ref[way], preferred_element_type=jnp.float32)
        part_ref[way] = partial.astype(jnp.bfloat16).reshape(size, rows // size, PROJ)
        comm.send_parts(way)

    def close_step(way):
        total = comm.take_sum(way)
        stat_refs[way][0] = total
        comm.send_all(way, (CLIP * jnp.tanh(total * (1.0 / CLIP))).astype(jnp.bfloat16))

    @pl.when(step == 0)
    def _():
        for way in range(2):
            all_ref[way] = hid_ref[way]
            state_ref[way] = cell_ref[way]
            input_part(way, 0)
        mp_barrier(size)

    @pl.when(step > 0)
    def _():
        comm.wait_all(0)
        emit_hidden(0)

    @pl.when(step < WIN)
    def _():
        cell_step(0)

    @pl.when(step > 0)
    def _():
        close_step(1)

    @pl.when(step < WIN)
    def _():
        @pl.when(step < WIN - 1)
        def _():
            input_part(0, step + 1)

        close_step(0)

    @pl.when(step > 0)
    def _():
        comm.wait_all(1)
        emit_hidden(1)

    @pl.when(step < WIN)
    def _():
        cell_step(1)

        @pl.when(step < WIN - 1)
        def _():
            input_part(1, step + 1)


def lstm_forward(size, emb, win, wst, wpr, bias, cell, hid, reset):
    rows = reset.shape[0]
    part = rows // size
    gates = win.shape[2]
    units = cell.shape[2]
    last = WIN - 1
    vmem = pl.BlockSpec(memory_space=pltpu.VMEM)

    def block(shape, index):
        return pl.BlockSpec((1,) + shape, lambda w: (index(w), 0, 0))

    now0 = lambda w: jnp.minimum(w, last)
    now1 = lambda w: last - jnp.minimum(w, last)
    past0 = lambda w: jnp.maximum(w - 1, 0)
    past1 = lambda w: last - jnp.maximum(w - 1, 0)
    outs = [((rows, PROJ), jnp.bfloat16, now0)]
    for width, kind in ((gates, jnp.float32), (units, jnp.float32), (units, jnp.float32), (units, jnp.bfloat16), (PROJ, jnp.bfloat16)):
        outs += [((rows, width), kind, now0), ((rows, width), kind, now1)]
    outs += [((part, PROJ), jnp.float32, now0), ((part, PROJ), jnp.float32, past1)]
    outs += [((rows, PROJ), jnp.bfloat16, past0), ((rows, PROJ), jnp.bfloat16, past1)]
    return pl.pallas_call(
        functools.partial(forward_kernel, size),
        grid=(WIN + 1,),
        in_specs=[vmem] * 8,
        out_specs=[block(shape, index) for shape, kind, index in outs],
        out_shape=[jax.ShapeDtypeStruct((WIN,) + shape, kind) for shape, kind, index in outs],
        scratch_shapes=[
            pltpu.VMEM((2, rows, gates), jnp.float32),
            pltpu.VMEM((2, rows, units), jnp.float32),
            pltpu.VMEM((2, size, part, PROJ), jnp.bfloat16),
            pltpu.VMEM((2, size, part, PROJ), jnp.bfloat16),
            pltpu.VMEM((2, size, part, PROJ), jnp.bfloat16),
        ]
        + [pltpu.SemaphoreType.DMA((2, size))] * 4,
        compiler_params=pltpu.CompilerParams(
            collective_id=1, has_side_effects=True, vmem_limit_bytes=56 * 2**20
        ),
    )(emb, win, wst, wpr, bias, cell, hid, reset)


def backward_kernel(
    size,
    gate0_ref,
    gate1_ref,
    cprev0_ref,
    cprev1_ref,
    cnew0_ref,
    cnew1_ref,
    cot0_ref,
    cot1_ref,
    stat0_ref,
    stat1_ref,
    win_ref,
    wst_ref,
    wpr_ref,
    reset_ref,
    first_cot_ref,
    first_stat_ref,
    da0_ref,
    da1_ref,
    ds0_ref,
    ds1_ref,
    bias_ref,
    de_ref,
    cell_ref,
    part_ref,
    sum_ref,
    all_ref,
    part_send,
    part_recv,
    all_send,
    all_recv,
    held_ref,
    embed_part_ref,
    embed_got_ref,
    embed_send,
    embed_recv,
):
    step = pl.program_id(0)
    rows = reset_ref.shape[0]
    part = rows // size
    units = cell_ref.shape[2]
    blocks = units // UNIT_BLOCK
    wide = 4 * UNIT_BLOCK
    comm = Exchange(size, part_ref, sum_ref, all_ref, (part_send, part_recv, all_send, all_recv))
    gate_refs = (gate0_ref, gate1_ref)
    cprev_refs = (cprev0_ref, cprev1_ref)
    cnew_refs = (cnew0_ref, cnew1_ref)
    da_refs = (da0_ref, da1_ref)
    ds_refs = (ds0_ref, ds1_ref)

    def time_of(way, at):
        return WIN - 1 - at if way == 0 else at

    def stat_step(way, at, cot, stat, total):
        grad = cot.astype(jnp.float32)
        if total is not None:
            own = reset_ref[pl.ds(comm.me * part, part), :] - way
            keep = jnp.where(own == time_of(way, at - 1), 0.0, 1.0)
            grad = grad + total * jnp.concatenate([keep] * (PROJ // UNIT_BLOCK), axis=1)
        slope = jnp.tanh(stat * (1.0 / CLIP))
        comm.send_all(way, (grad * (1.0 - slope * slope)).astype(jnp.bfloat16))

    def cell_step(way):
        comm.wait_all(way)
        now = time_of(way, step)
        keep = jnp.where(reset_ref[...] - way == now, 0.0, 1.0)
        grad_stat = all_ref[way].reshape(rows, PROJ)
        ds_refs[way][0] = grad_stat
        for block in range(blocks):
            cols = slice(block * wide, (block + 1) * wide)
            unit = slice(block * UNIT_BLOCK, (block + 1) * UNIT_BLOCK)
            grad_out = lax.dot_general(
                grad_stat,
                wpr_ref[way, unit, :],
                (((1,), (1,)), ((), ())),
                preferred_element_type=jnp.float32,
            )
            gates = gate_refs[way][0, :, cols]
            gate_in = gates[:, :UNIT_BLOCK]
            gate_forget = gates[:, UNIT_BLOCK : 2 * UNIT_BLOCK]
            gate_cand = gates[:, 2 * UNIT_BLOCK : 3 * UNIT_BLOCK]
            gate_out = gates[:, 3 * UNIT_BLOCK :]
            cell_prev = cprev_refs[way][0, :, unit]
            cell_new = cnew_refs[way][0, :, unit]
            tanh_cell = jnp.tanh(cell_new)
            grad_total = (
                grad_out * gate_out * (1.0 - tanh_cell * tanh_cell) + cell_ref[way, :, unit]
            )
            scaled = cell_new * (1.0 / CLIP)
            grad_inner = grad_total * (1.0 - scaled * scaled)
            cell_ref[way, :, unit] = grad_inner * gate_forget * keep
            grad_pre = jnp.concatenate(
                [
                    grad_inner * gate_cand * gate_in * (1.0 - gate_in),
                    grad_inner * cell_prev * gate_forget * (1.0 - gate_forget),
                    grad_inner * gate_in * (1.0 - gate_cand * gate_cand),
                    grad_out * tanh_cell * gate_out * (1.0 - gate_out),
                ],
                axis=1,
            ).astype(jnp.bfloat16)
            da_refs[way][0, :, cols] = grad_pre
            bias_ref[way, :, cols] += jnp.sum(
                grad_pre.astype(jnp.float32).reshape(rows // 8, 8, wide), axis=0
            )

        @pl.when(step < WIN - 1)
        def _():
            partial = lax.dot_general(
                da_refs[way][0],
                wst_ref[way],
                (((1,), (1,)), ((), ())),
                preferred_element_type=jnp.float32,
            )
            part_ref[way] = partial.astype(jnp.bfloat16).reshape(size, part, PROJ)
            comm.send_parts(way)

    def embed_copy(src, dst, offset):
        return pltpu.make_async_remote_copy(
            src_ref=src,
            dst_ref=dst,
            send_sem=embed_send.at[offset],
            recv_sem=embed_recv.at[offset],
            device_id={"mp": lax.rem(comm.me + offset, size)},
            device_id_type=pl.DeviceIdType.MESH,
        )

    def embed_step(way):
        now = time_of(way, step)
        value = lax.dot_general(
            da_refs[way][0],
            win_ref[way],
            (((1,), (1,)), ((), ())),
            preferred_element_type=jnp.float32,
        )

        @pl.when(step < WIN // 2)
        def _():
            held_ref[now] = value

        @pl.when(step >= WIN // 2)
        def _():
            both = (value + held_ref[now]).astype(jnp.bfloat16)
            embed_part_ref[now] = both.reshape(size, part, PROJ)
            for offset in range(1, size):
                peer = lax.rem(comm.me + offset, size)
                embed_copy(
                    embed_part_ref.at[now, peer], embed_got_ref.at[comm.me, now], offset
                ).start()

    def embed_finish():
        total = embed_part_ref[:, comm.me].astype(jnp.float32)
        for offset in range(1, size):
            peer = lax.rem(comm.me + size - offset, size)
            embed_copy(embed_got_ref.at[peer], embed_got_ref.at[peer], offset).wait_recv()
            total = total + embed_got_ref[peer].astype(jnp.float32)
        de_ref[...] = total.astype(jnp.bfloat16)
        for offset in range(1, size):
            embed_copy(embed_got_ref.at[comm.me], embed_got_ref.at[comm.me], offset).wait_send()

    @pl.when(step == 0)
    def _():
        cell_ref[...] = jnp.zeros(cell_ref.shape, jnp.float32)
        bias_ref[...] = jnp.zeros(bias_ref.shape, jnp.float32)
        mp_barrier(size)
        for way in range(2):
            stat_step(way, 0, first_cot_ref[way], first_stat_ref[way], None)

    cell_step(0)

    @pl.when(step > 0)
    def _():
        stat_step(1, step, cot1_ref[0], stat1_ref[0], comm.take_sum(1))

    embed_step(0)

    @pl.when(step < WIN - 1)
    def _():
        stat_step(0, step + 1, cot0_ref[0], stat0_ref[0], comm.take_sum(0))

    cell_step(1)
    embed_step(1)

    @pl.when(step == WIN - 1)
    def _():
        embed_finish()


def lstm_backward(size, gates, cprevs, cnews, cots, stats, win, wst, wpr, reset):
    rows = reset.shape[0]
    part = rows // size
    width = win.shape[2]
    units = cprevs[0].shape[2]
    last = WIN - 1
    vmem = pl.BlockSpec(memory_space=pltpu.VMEM)

    def block(shape, index):
        return pl.BlockSpec((1,) + shape, lambda w: (index(w), 0, 0))

    now0 = lambda w: last - w
    now1 = lambda w: w
    next0 = lambda w: jnp.maximum(last - 1 - w, 0)
    ins = []
    for size_of in (width, units, units):
        ins += [block((rows, size_of), now0), block((rows, size_of), now1)]
    ins += [block((part, PROJ), next0), block((part, PROJ), now1)] * 2
    ins += [vmem] * 6
    outs = []
    for size_of, kind in ((width, jnp.bfloat16), (PROJ, jnp.bfloat16)):
        outs += [((rows, size_of), kind, now0), ((rows, size_of), kind, now1)]
    first_cot = jnp.stack([cots[0][last], cots[1][0]])
    first_stat = jnp.stack([stats[0][last], stats[1][0]])
    return pl.pallas_call(
        functools.partial(backward_kernel, size),
        grid=(WIN,),
        in_specs=ins,
        out_specs=[block(shape, index) for shape, kind, index in outs]
        + [pl.BlockSpec((2, 8, width), lambda w: (0, 0, 0)), vmem],
        out_shape=[jax.ShapeDtypeStruct((WIN,) + shape, kind) for shape, kind, index in outs]
        + [
            jax.ShapeDtypeStruct((2, 8, width), jnp.float32),
            jax.ShapeDtypeStruct((WIN, part, PROJ), jnp.bfloat16),
        ],
        scratch_shapes=[
            pltpu.VMEM((2, rows, units), jnp.float32),
            pltpu.VMEM((2, size, part, PROJ), jnp.bfloat16),
            pltpu.VMEM((2, size, part, PROJ), jnp.bfloat16),
            pltpu.VMEM((2, size, part, PROJ), jnp.bfloat16),
        ]
        + [pltpu.SemaphoreType.DMA((2, size))] * 4
        + [
            pltpu.VMEM((WIN, rows, PROJ), jnp.float32),
            pltpu.VMEM((WIN, size, part, PROJ), jnp.bfloat16),
            pltpu.VMEM((size, WIN, part, PROJ), jnp.bfloat16),
        ]
        + [pltpu.SemaphoreType.DMA((size,))] * 2,
        compiler_params=pltpu.CompilerParams(
            collective_id=2, has_side_effects=True, vmem_limit_bytes=56 * 2**20
        ),
    )(*gates, *cprevs, *cnews, *cots, *stats, win, wst, wpr, reset, first_cot, first_stat)


class RingExchange(Exchange):
    def __init__(self, part_ref, sum_ref, all_ref, sems):
        super().__init__(4, part_ref, sum_ref, all_ref, sems)
        self.near = lax.rem(self.me, 2)
        self.me = self.me // 2

    def part_copy(self, way, offset, incoming):
        peer = lax.rem(self.me + (4 - offset if incoming else offset), 4)
        return pltpu.make_async_remote_copy(
            src_ref=self.part_ref.at[way, peer],
            dst_ref=self.sum_ref.at[way, peer if incoming else self.me],
            send_sem=self.part_send.at[way, offset],
            recv_sem=self.part_recv.at[way, offset],
            device_id={"mp": 2 * peer + self.near},
            device_id_type=pl.DeviceIdType.MESH,
        )

    def all_copy(self, way, offset, incoming):
        peer = lax.rem(self.me + (4 - offset if incoming else offset), 4)
        slot = peer if incoming else self.me
        return pltpu.make_async_remote_copy(
            src_ref=self.all_ref.at[way, slot],
            dst_ref=self.all_ref.at[way, slot],
            send_sem=self.all_send.at[way, offset],
            recv_sem=self.all_recv.at[way, offset],
            device_id={"mp": 2 * peer + self.near},
            device_id_type=pl.DeviceIdType.MESH,
        )


def ring_forward_kernel(
    emb_ref,
    win_ref,
    wst_ref,
    wpr_ref,
    bias_ref,
    cell_ref,
    hid_ref,
    reset_ref,
    embt_ref,
    gate_ref,
    cprev_ref,
    cnew_ref,
    low_ref,
    hprev_ref,
    stat_ref,
    out_ref,
    pre_ref,
    state_ref,
    part_ref,
    sum_ref,
    all_ref,
    stage_ref,
    part_send,
    part_recv,
    all_send,
    all_recv,
    out_sem,
    out_send,
    out_recv,
):
    step = pl.program_id(0)
    half_rows = reset_ref.shape[1]
    part = half_rows // 4
    units = wpr_ref.shape[1]
    blocks = units // UNIT_BLOCK
    wide = 4 * UNIT_BLOCK
    comm = RingExchange(part_ref, sum_ref, all_ref, (part_send, part_recv, all_send, all_recv))
    near = comm.near

    def time_of(at):
        return at + near * (WIN - 1 - 2 * at)

    def input_part(at):
        emb = emb_ref[:, :, time_of(at)]
        halves = [emb[:, way].reshape(half_rows, PROJ) for way in range(2)]
        both = jnp.concatenate(halves, axis=0)
        slot = lax.rem(at, 2)
        for owner in range(2):
            for block in range(blocks):
                cols = slice(block * wide, (block + 1) * wide)
                pre_ref[slot, owner, :, cols] = (
                    jnp.dot(both, win_ref[owner, :, cols], preferred_element_type=jnp.float32)
                    + bias_ref[owner, :, cols]
                )

    def out_copies(way, at, incoming):
        slot = lax.rem(at, 2)
        now = time_of(at)
        src = stage_ref.at[way, slot]
        other = WIN - 1 - now if incoming else now
        return (
            pltpu.make_async_copy(src, out_ref.at[near, now, :, way], out_sem.at[way, slot]),
            pltpu.make_async_remote_copy(
                src_ref=src,
                dst_ref=out_ref.at[1 - near if incoming else near, other, :, way],
                send_sem=out_send.at[way, slot],
                recv_sem=out_recv.at[way, at],
                device_id={"mp": 2 * comm.me + 1 - near},
                device_id_type=pl.DeviceIdType.MESH,
            ),
        )

    def emit_hidden(way):
        at = step - 1

        @pl.when(at >= 2)
        def _():
            local, remote = out_copies(way, at - 2, False)
            local.wait()
            remote.wait_send()

        stage_ref[way, lax.rem(at, 2)] = all_ref[way]
        for copy in out_copies(way, at, False):
            copy.start()

    def cell_step(way):
        now = time_of(step)
        keep = jnp.where(reset_ref[way] - near == now, 0.0, 1.0)
        keep_low = jnp.concatenate([keep.astype(jnp.bfloat16)] * (PROJ // UNIT_BLOCK), axis=1)
        hidden_prev = all_ref[way].reshape(half_rows, PROJ) * keep_low
        hprev_ref[0, way] = hidden_prev
        embt_ref[0, way] = emb_ref[:, way, now].reshape(half_rows, PROJ)
        slot = lax.rem(step, 2)
        rows = slice(way * half_rows, (way + 1) * half_rows)
        partial = None
        for owner in range(2):
            for block in range(blocks):
                cols = slice(block * wide, (block + 1) * wide)
                unit = slice(block * UNIT_BLOCK, (block + 1) * UNIT_BLOCK)
                spot = slice(
                    owner * units + block * UNIT_BLOCK, owner * units + (block + 1) * UNIT_BLOCK
                )
                place = slice((owner * blocks + block) * wide, (owner * blocks + block + 1) * wide)
                pre = pre_ref[slot, owner, rows, cols] + jnp.dot(
                    hidden_prev, wst_ref[owner, :, cols], preferred_element_type=jnp.float32
                )
                gate_in = sigmoid_of(pre[:, :UNIT_BLOCK])
                gate_forget = sigmoid_of(pre[:, UNIT_BLOCK : 2 * UNIT_BLOCK])
                gate_cand = jnp.tanh(pre[:, 2 * UNIT_BLOCK : 3 * UNIT_BLOCK])
                gate_out = sigmoid_of(pre[:, 3 * UNIT_BLOCK :])
                cell_prev = state_ref[way, owner, :, unit] * keep
                cell_new = CLIP * jnp.tanh(
                    (gate_forget * cell_prev + gate_in * gate_cand) * (1.0 / CLIP)
                )
                gate_ref[0, way, :, place] = jnp.concatenate(
                    [gate_in, gate_forget, gate_cand, gate_out], axis=1
                )
                cprev_ref[0, way, :, spot] = cell_prev
                cnew_ref[0, way, :, spot] = cell_new
                state_ref[way, owner, :, unit] = cell_new
                low_ref[0, way, :, spot] = (gate_out * jnp.tanh(cell_new)).astype(jnp.bfloat16)
            term = jnp.dot(
                low_ref[0, way, :, owner * units : (owner + 1) * units],
                wpr_ref[owner],
                preferred_element_type=jnp.float32,
            )
            partial = term if partial is None else partial + term
        part_ref[way] = partial.astype(jnp.bfloat16).reshape(4, part, PROJ)
        comm.send_parts(way)

    def close_step(way, at):
        total = comm.take_sum(way)
        stat_ref[way, at] = total
        comm.send_all(way, (CLIP * jnp.tanh(total * (1.0 / CLIP))).astype(jnp.bfloat16))

    @pl.when(step == 0)
    def _():
        for way in range(2):
            all_ref[way] = hid_ref[way]
            state_ref[way] = cell_ref[way]
        input_part(jnp.int32(0))
        mp_barrier(8)

    @pl.when(step > 0)
    def _():
        comm.wait_all(0)
        emit_hidden(0)

    @pl.when(step < WIN)
    def _():
        cell_step(0)

    @pl.when(step > 0)
    def _():
        close_step(1, step - 1)

    @pl.when(step < WIN)
    def _():
        @pl.when(step < WIN - 1)
        def _():
            input_part(step + 1)

        close_step(0, step)

    @pl.when(step > 0)
    def _():
        comm.wait_all(1)
        emit_hidden(1)

    @pl.when(step < WIN)
    def _():
        cell_step(1)

    @pl.when(step == WIN)
    def _():
        for way in range(2):
            for at in (WIN - 2, WIN - 1):
                local, remote = out_copies(way, jnp.int32(at), False)
                local.wait()
                remote.wait_send()

            @pl.loop(0, WIN)
            def _(at):
                out_copies(way, at, True)[1].wait_recv()


def ring_forward(emb, win, wst, wpr, bias, cell, hid, reset):
    half_rows = reset.shape[1]
    part = half_rows // 4
    gates = 2 * win.shape[2]
    units = 2 * wpr.shape[1]
    last = WIN - 1
    vmem = pl.BlockSpec(memory_space=pltpu.VMEM)
    bf16, f32 = jnp.bfloat16, jnp.float32
    dma = pltpu.SemaphoreType.DMA
    widths = (
        (PROJ, bf16),
        (gates, f32),
        (units, f32),
        (units, f32),
        (units, bf16),
        (PROJ, bf16),
    )
    return pl.pallas_call(
        ring_forward_kernel,
        grid=(WIN + 1,),
        in_specs=[vmem] * 8,
        out_specs=[
            pl.BlockSpec((1, 2, half_rows, width), lambda w: (jnp.minimum(w, last), 0, 0, 0))
            for width, kind in widths
        ]
        + [vmem, pl.BlockSpec(memory_space=pl.ANY)],
        out_shape=[
            jax.ShapeDtypeStruct((WIN, 2, half_rows, width), kind) for width, kind in widths
        ]
        + [
            jax.ShapeDtypeStruct((2, WIN, part, PROJ), f32),
            jax.ShapeDtypeStruct((2, WIN, 4, 2, part, PROJ), bf16),
        ],
        scratch_shapes=[
            pltpu.VMEM((2, 2, 2 * half_rows, gates // 2), f32),
            pltpu.VMEM((2, 2, half_rows, units // 2), f32),
            pltpu.VMEM((2, 4, part, PROJ), bf16),
            pltpu.VMEM((2, 4, part, PROJ), bf16),
            pltpu.VMEM((2, 4, part, PROJ), bf16),
            pltpu.VMEM((2, 2, 4, part, PROJ), bf16),
        ]
        + [dma((2, 4))] * 4
        + [dma((2, 2))] * 2
        + [dma((2, WIN))],
        compiler_params=pltpu.CompilerParams(
            collective_id=5, has_side_effects=True, vmem_limit_bytes=56 * 2**20
        ),
    )(emb, win, wst, wpr, bias, cell, hid, reset)


def ring_backward_kernel(
    gate_ref,
    cprev_ref,
    cnew_ref,
    cot_ref,
    stat_ref,
    win_ref,
    wst_ref,
    wpr_ref,
    reset_ref,
    da_ref,
    ds_ref,
    bias_ref,
    de_ref,
    cell_ref,
    part_ref,
    sum_ref,
    all_ref,
    part_send,
    part_recv,
    all_send,
    all_recv,
    embed_part_ref,
    embed_got_ref,
    embed_send,
    embed_recv,
):
    step = pl.program_id(0)
    half_rows = reset_ref.shape[1]
    part = half_rows // 4
    units = wpr_ref.shape[1]
    blocks = units // UNIT_BLOCK
    wide = 4 * UNIT_BLOCK
    comm = RingExchange(part_ref, sum_ref, all_ref, (part_send, part_recv, all_send, all_recv))
    near = comm.near
    device = lax.axis_index("mp")

    def scan_of(at):
        return WIN - 1 - at

    def time_of(at):
        back = scan_of(at)
        return back + near * (WIN - 1 - 2 * back)

    def stat_step(way, at, total):
        grad = cot_ref[way, time_of(at)].astype(jnp.float32)
        if total is not None:
            own = reset_ref[way, pl.ds(comm.me * part, part), :] - near
            keep = jnp.where(own == time_of(at - 1), 0.0, 1.0)
            grad = grad + total * jnp.concatenate([keep] * (PROJ // UNIT_BLOCK), axis=1)
        slope = jnp.tanh(stat_ref[way, scan_of(at)] * (1.0 / CLIP))
        comm.send_all(way, (grad * (1.0 - slope * slope)).astype(jnp.bfloat16))

    def cell_step(way):
        comm.wait_all(way)
        keep = jnp.where(reset_ref[way] - near == time_of(step), 0.0, 1.0)
        grad_stat = all_ref[way].reshape(half_rows, PROJ)
        ds_ref[0, way] = grad_stat
        for owner in range(2):
            for block in range(blocks):
                unit = slice(block * UNIT_BLOCK, (block + 1) * UNIT_BLOCK)
                spot = slice(
                    owner * units + block * UNIT_BLOCK, owner * units + (block + 1) * UNIT_BLOCK
                )
                place = slice((owner * blocks + block) * wide, (owner * blocks + block + 1) * wide)
                grad_out = lax.dot_general(
                    grad_stat,
                    wpr_ref[owner, unit, :],
                    (((1,), (1,)), ((), ())),
                    preferred_element_type=jnp.float32,
                )
                gates = gate_ref[0, way, :, place]
                gate_in = gates[:, :UNIT_BLOCK]
                gate_forget = gates[:, UNIT_BLOCK : 2 * UNIT_BLOCK]
                gate_cand = gates[:, 2 * UNIT_BLOCK : 3 * UNIT_BLOCK]
                gate_out = gates[:, 3 * UNIT_BLOCK :]
                cell_prev = cprev_ref[0, way, :, spot]
                cell_new = cnew_ref[0, way, :, spot]
                tanh_cell = jnp.tanh(cell_new)
                grad_total = (
                    grad_out * gate_out * (1.0 - tanh_cell * tanh_cell) + cell_ref[way, :, spot]
                )
                scaled = cell_new * (1.0 / CLIP)
                grad_inner = grad_total * (1.0 - scaled * scaled)
                cell_ref[way, :, spot] = grad_inner * gate_forget * keep
                grad_pre = jnp.concatenate(
                    [
                        grad_inner * gate_cand * gate_in * (1.0 - gate_in),
                        grad_inner * cell_prev * gate_forget * (1.0 - gate_forget),
                        grad_inner * gate_in * (1.0 - gate_cand * gate_cand),
                        grad_out * tanh_cell * gate_out * (1.0 - gate_out),
                    ],
                    axis=1,
                ).astype(jnp.bfloat16)
                da_ref[0, way, :, place] = grad_pre
                bias_ref[:, place] += jnp.sum(
                    grad_pre.astype(jnp.float32).reshape(half_rows // 8, 8, wide), axis=0
                )

        @pl.when(step < WIN - 1)
        def _():
            partial = None
            for owner in range(2):
                span = slice(owner * blocks * wide, (owner + 1) * blocks * wide)
                term = lax.dot_general(
                    da_ref[0, way, :, span],
                    wst_ref[owner],
                    (((1,), (1,)), ((), ())),
                    preferred_element_type=jnp.float32,
                )
                partial = term if partial is None else partial + term
            part_ref[way] = partial.astype(jnp.bfloat16).reshape(4, part, PROJ)
            comm.send_parts(way)

    def embed_copy(src, dst, offset):
        return pltpu.make_async_remote_copy(
            src_ref=src,
            dst_ref=dst,
            send_sem=embed_send.at[offset],
            recv_sem=embed_recv.at[offset],
            device_id={"mp": lax.rem(device + offset, 8)},
            device_id_type=pl.DeviceIdType.MESH,
        )

    def embed_step():
        now = time_of(step)
        total = None
        for owner in range(2):
            span = slice(owner * blocks * wide, (owner + 1) * blocks * wide)
            both = jnp.concatenate([da_ref[0, 0, :, span], da_ref[0, 1, :, span]], axis=0)
            term = lax.dot_general(
                both,
                win_ref[owner],
                (((1,), (1,)), ((), ())),
                preferred_element_type=jnp.float32,
            )
            total = term if total is None else total + term
        total = total.astype(jnp.bfloat16)
        for way in range(2):
            embed_part_ref[now, way] = total[way * half_rows : (way + 1) * half_rows].reshape(
                4, part, PROJ
            )
        for offset in range(1, 8):
            peer = lax.rem(device + offset, 8)
            embed_copy(
                embed_part_ref.at[now, lax.rem(peer, 2), peer // 2],
                embed_got_ref.at[device, now],
                offset,
            ).start()

    def embed_finish():
        total = embed_part_ref[:, near, comm.me].astype(jnp.float32)
        for offset in range(1, 8):
            peer = lax.rem(device + 8 - offset, 8)
            embed_copy(embed_got_ref.at[peer], embed_got_ref.at[peer], offset).wait_recv()
            total = total + embed_got_ref[peer].astype(jnp.float32)
        de_ref[...] = total.astype(jnp.bfloat16)
        for offset in range(1, 8):
            embed_copy(embed_got_ref.at[device], embed_got_ref.at[device], offset).wait_send()

    @pl.when(step == 0)
    def _():
        cell_ref[...] = jnp.zeros(cell_ref.shape, jnp.float32)
        bias_ref[...] = jnp.zeros(bias_ref.shape, jnp.float32)
        mp_barrier(8)
        for way in range(2):
            stat_step(way, 0, None)

    cell_step(0)

    @pl.when(step > 0)
    def _():
        stat_step(1, step, comm.take_sum(1))

    @pl.when(step < WIN - 1)
    def _():
        stat_step(0, step + 1, comm.take_sum(0))

    cell_step(1)
    embed_step()

    @pl.when(step == WIN - 1)
    def _():
        embed_finish()


def ring_backward(gates, cprevs, cnews, cots, stats, win, wst, wpr, reset):
    half_rows = reset.shape[1]
    part = half_rows // 4
    width = 2 * win.shape[2]
    units = 2 * wpr.shape[1]
    last = WIN - 1
    vmem = pl.BlockSpec(memory_space=pltpu.VMEM)
    bf16, f32 = jnp.bfloat16, jnp.float32
    dma = pltpu.SemaphoreType.DMA

    def block(size):
        return pl.BlockSpec((1, 2, half_rows, size), lambda w: (last - w, 0, 0, 0))

    return pl.pallas_call(
        ring_backward_kernel,
        grid=(WIN,),
        in_specs=[block(width), block(units), block(units)] + [vmem] * 6,
        out_specs=[block(width), block(PROJ), vmem, vmem],
        out_shape=[
            jax.ShapeDtypeStruct((WIN, 2, half_rows, width), bf16),
            jax.ShapeDtypeStruct((WIN, 2, half_rows, PROJ), bf16),
            jax.ShapeDtypeStruct((8, width), f32),
            jax.ShapeDtypeStruct((WIN, part, PROJ), bf16),
        ],
        scratch_shapes=[
            pltpu.VMEM((2, half_rows, units), f32),
            pltpu.VMEM((2, 4, part, PROJ), bf16),
            pltpu.VMEM((2, 4, part, PROJ), bf16),
            pltpu.VMEM((2, 4, part, PROJ), bf16),
        ]
        + [dma((2, 4))] * 4
        + [
            pltpu.VMEM((WIN, 2, 4, part, PROJ), bf16),
            pltpu.VMEM((8, WIN, part, PROJ), bf16),
        ]
        + [dma((8,))] * 2,
        compiler_params=pltpu.CompilerParams(
            collective_id=6, has_side_effects=True, vmem_limit_bytes=56 * 2**20
        ),
    )(gates, cprevs, cnews, cots, stats, win, wst, wpr, reset)


SHIFTS = 8
GROUP = SHIFTS * CDIM
FBLOCK = 256


def position_bound(first, width, taps):
    index = first + lax.broadcasted_iota(jnp.int32, (1, width), 1)
    bound = jnp.full((1, width), CHARS - 1, jnp.int32)
    for exponent in range(taps - 1):
        bound = bound - (index >= (FILTERS // 64) * (1 << exponent)).astype(jnp.int32)
    return bound


def group_counts():
    full = (CHARS - SHIFTS) // SHIFTS + 1
    return full, CHARS - full * SHIFTS


def windows(vec_ref, count):
    tokens = vec_ref.shape[1]
    low = vec_ref[0:count].reshape(count * tokens, GROUP)
    high = vec_ref[1 : count + 1].reshape(count * tokens, GROUP)
    return jnp.concatenate([low, high], axis=1)


def char_vectors(ids_ref, table_ref, vec_ref):
    groups, tokens, _ = vec_ref.shape
    vocab = table_ref.shape[1]
    for group in range(groups):
        acc = jnp.zeros((tokens, GROUP), jnp.float32)
        for shift in range(SHIFTS):
            place = group * SHIFTS + shift
            if place < CHARS:
                column = ids_ref[:, place : place + 1]
                hot = column == lax.broadcasted_iota(jnp.int32, (tokens, vocab), 1)
                acc = acc + jnp.dot(
                    jnp.where(hot, 1.0, 0.0).astype(jnp.bfloat16),
                    table_ref[shift],
                    preferred_element_type=jnp.float32,
                )
        vec_ref[group] = acc.astype(jnp.bfloat16)


def conv_block(block, cols, vec_ref, weight_ref, total_ref):
    _, tokens, _ = vec_ref.shape
    full, extra = group_counts()
    bound = position_bound(block * FBLOCK, FBLOCK, TAPS)
    left = windows(vec_ref, full)
    total = jnp.zeros((tokens, FBLOCK), jnp.float32)
    for shift in range(SHIFTS):
        out = jnp.dot(left, weight_ref[shift, :, cols], preferred_element_type=jnp.float32)
        values = jnp.exp(out).reshape(full, tokens, FBLOCK)
        for group in range(full):
            place = group * SHIFTS + shift
            term = values[group]
            if place > CHARS - TAPS:
                term = jnp.where(bound >= place, term, 0.0)
            total = total + term
    total_ref[:, cols] = total

    @pl.when(block == 0)
    def _():
        for shift in range(extra):
            out = jnp.dot(
                vec_ref[full], weight_ref[shift, :GROUP, cols], preferred_element_type=jnp.float32
            )
            total_ref[:, cols] += jnp.where(
                bound >= full * SHIFTS + shift, jnp.exp(out), 0.0
            )


def conv_forward_kernel(ids_ref, table_ref, weight_ref, total_ref, vec_ref):
    block = pl.program_id(0)

    @pl.when(block == 0)
    def _():
        char_vectors(ids_ref, table_ref, vec_ref)

    conv_block(block, slice(None), vec_ref, weight_ref, total_ref)


def conv_forward(ids, table_shift, weights):
    tokens = ids.shape[0]
    groups = -(-CHARS // SHIFTS)
    vocab = table_shift.shape[1]
    return pl.pallas_call(
        conv_forward_kernel,
        grid=(FILTERS // FBLOCK,),
        in_specs=[
            pl.BlockSpec((tokens, CHARS), lambda f: (0, 0)),
            pl.BlockSpec((SHIFTS, vocab, GROUP), lambda f: (0, 0, 0)),
            pl.BlockSpec((SHIFTS, 2 * GROUP, FBLOCK), lambda f: (0, 0, f)),
        ],
        out_specs=[
            pl.BlockSpec((tokens, FBLOCK), lambda f: (0, f)),
            pl.BlockSpec((groups, tokens, GROUP), lambda f: (0, 0, 0)),
        ],
        out_shape=[
            jax.ShapeDtypeStruct((tokens, FILTERS), jnp.float32),
            jax.ShapeDtypeStruct((groups, tokens, GROUP), jnp.bfloat16),
        ],
        compiler_params=pltpu.CompilerParams(vmem_limit_bytes=56 * 2**20),
        cost_estimate=pl.CostEstimate(
            flops=2 * tokens * CHARS * 256 * FILTERS,
            bytes_accessed=12 * 2**20,
            transcendentals=tokens * CHARS * FILTERS,
        ),
    )(ids, table_shift, weights)


def conv_shift_step(
    shift, vec_ref, turned_ref, turned_extra_ref, ratio_ref, weight_ref, grad_ref, low_ref, char_ref, held_ref
):
    groups, tokens, _ = vec_ref.shape
    full, extra = group_counts()
    left = windows(vec_ref, full)
    own_rows = pl.ds(pl.multiple_of(shift * CDIM, CDIM), TAPS * CDIM)

    @pl.when(shift == 0)
    def _():
        grad_ref[...] = jnp.zeros(grad_ref.shape, jnp.float32)
        char_ref[...] = jnp.zeros(char_ref.shape, jnp.float32)

    @pl.loop(0, FILTERS // FBLOCK)
    def _(block):
        cols = pl.ds(pl.multiple_of(block * FBLOCK, FBLOCK), FBLOCK)
        bound = position_bound(block * FBLOCK, FBLOCK, TAPS)
        ratio = ratio_ref[:, cols]
        out = jnp.dot(left, weight_ref[0, :, cols], preferred_element_type=jnp.float32)
        values = jnp.exp(out).reshape(full, tokens, FBLOCK)
        for group in range(full):
            term = values[group] * ratio
            if (group + 1) * SHIFTS - 1 > CHARS - TAPS:
                term = jnp.where(bound >= group * SHIFTS + shift, term, 0.0)
            low_ref[pl.ds(group * tokens, tokens), cols] = term.astype(jnp.bfloat16)
        held_ref[...] = jnp.dot(
            turned_ref[...], low_ref[:, cols], preferred_element_type=jnp.float32
        )
        grad_ref[:, cols] += held_ref[own_rows, :]

    back = lax.dot_general(
        low_ref[...],
        weight_ref[0],
        (((1,), (1,)), ((), ())),
        preferred_element_type=jnp.float32,
    ).reshape(full, tokens, 2 * GROUP)
    for group in range(full):
        char_ref[group] += back[group, :, :GROUP]
        char_ref[group + 1] += back[group, :, GROUP:]

    @pl.when(shift < extra)
    def _():
        cols = slice(0, FBLOCK)
        bound = position_bound(0, FBLOCK, TAPS)
        out = jnp.dot(
            vec_ref[full], weight_ref[0, :GROUP, cols], preferred_element_type=jnp.float32
        )
        term = jnp.exp(out) * ratio_ref[:, cols]
        term = jnp.where(bound >= full * SHIFTS + shift, term, 0.0).astype(jnp.bfloat16)
        held_ref[...] = jnp.concatenate(
            [
                jnp.dot(turned_extra_ref[...], term, preferred_element_type=jnp.float32),
                jnp.zeros((GROUP, FBLOCK), jnp.float32),
            ],
            axis=0,
        )
        grad_ref[:, cols] += held_ref[own_rows, :]
        char_ref[full] += lax.dot_general(
            term,
            weight_ref[0, :GROUP, cols],
            (((1,), (1,)), ((), ())),
            preferred_element_type=jnp.float32,
        )


def table_gradient(hot_ref, hot_extra_ref, char_ref, vocab):
    tokens = char_ref.shape[1]
    full, extra = group_counts()
    lane = lax.broadcasted_iota(jnp.int32, (vocab, GROUP), 1) // CDIM

    def split(value):
        high = value.astype(jnp.bfloat16)
        rest = (value - high.astype(jnp.float32)).astype(jnp.bfloat16)
        return jnp.concatenate([high, rest], axis=1)

    main = split(char_ref[0:full].reshape(full * tokens, GROUP))
    last = split(char_ref[full])
    acc = jnp.zeros((vocab, GROUP), jnp.float32)
    for at in range(SHIFTS):
        row = hot_ref[at : at + 1, :]
        hot = row == lax.broadcasted_iota(jnp.int32, (vocab, full * tokens), 0)
        out = jnp.dot(
            jnp.where(hot, 1.0, 0.0).astype(jnp.bfloat16),
            main,
            preferred_element_type=jnp.float32,
        )
        if at < extra:
            row = hot_extra_ref[at : at + 1, :]
            hot = row == lax.broadcasted_iota(jnp.int32, (vocab, tokens), 0)
            out = out + jnp.dot(
                jnp.where(hot, 1.0, 0.0).astype(jnp.bfloat16),
                last,
                preferred_element_type=jnp.float32,
            )
        acc = jnp.where(lane == at, out[:, :GROUP] + out[:, GROUP:], acc)
    return acc


def conv_backward_kernel(
    hot_ref,
    hot_extra_ref,
    vec_ref,
    turned_ref,
    turned_extra_ref,
    ratio_ref,
    weight_ref,
    grad_ref,
    table_ref,
    low_ref,
    char_ref,
    held_ref,
):
    shift = pl.program_id(0)
    conv_shift_step(
        shift, vec_ref, turned_ref, turned_extra_ref, ratio_ref, weight_ref, grad_ref, low_ref, char_ref, held_ref
    )

    @pl.when(shift == SHIFTS - 1)
    def _():
        table_ref[...] = table_gradient(hot_ref, hot_extra_ref, char_ref, table_ref.shape[0])


def conv_operands(ids, vectors):
    groups, tokens, _ = vectors.shape
    full, extra = group_counts()
    turned = jnp.transpose(vectors, (0, 2, 1))
    pieces = [
        jnp.transpose(turned[half : half + full], (1, 0, 2)).reshape(GROUP, full * tokens)
        for half in range(2)
    ]
    ids_turned = ids.T
    hot_main = jnp.transpose(ids_turned[: full * SHIFTS].reshape(full, SHIFTS, tokens), (1, 0, 2))
    hot_main = hot_main.reshape(SHIFTS, full * tokens)
    hot_extra = ids_turned[full * SHIFTS :]
    return hot_main, hot_extra, vectors, jnp.concatenate(pieces, axis=0), turned[full]


def conv_backward(ids, vectors, ratio, weights):
    groups, tokens, _ = vectors.shape
    full, _ = group_counts()
    vocab = -(-VOCAB // 8) * 8
    grad, table = pl.pallas_call(
        conv_backward_kernel,
        grid=(SHIFTS,),
        in_specs=[pl.BlockSpec(memory_space=pltpu.VMEM)] * 6
        + [pl.BlockSpec((1, 2 * GROUP, FILTERS), lambda s: (s, 0, 0))],
        out_specs=[
            pl.BlockSpec((TAPS * CDIM, FILTERS), lambda s: (0, 0)),
            pl.BlockSpec((vocab, GROUP), lambda s: (0, 0)),
        ],
        out_shape=[
            jax.ShapeDtypeStruct((TAPS * CDIM, FILTERS), jnp.float32),
            jax.ShapeDtypeStruct((vocab, GROUP), jnp.float32),
        ],
        scratch_shapes=[
            pltpu.VMEM((full * tokens, FILTERS), jnp.bfloat16),
            pltpu.VMEM((groups, tokens, GROUP), jnp.float32),
            pltpu.VMEM((2 * GROUP, FBLOCK), jnp.float32),
        ],
        compiler_params=pltpu.CompilerParams(vmem_limit_bytes=58 * 2**20),
        cost_estimate=pl.CostEstimate(
            flops=6 * tokens * CHARS * 256 * FILTERS,
            bytes_accessed=16 * 2**20,
            transcendentals=tokens * CHARS * FILTERS,
        ),
    )(*conv_operands(ids, vectors), ratio, weights)
    table = table.reshape(vocab, SHIFTS, CDIM).sum(axis=1)[:VOCAB]
    return grad, table


MESH = pl.DeviceIdType.MESH
CHUNK_ROWS = 16
SLACK = 2
BEATS = 2
AHEAD = 2
BIAS_ROWS = 32


def tail_kernel(
    chunks,
    hot_ref,
    hot_extra_ref,
    vec_ref,
    turned_ref,
    turned_extra_ref,
    ratio_ref,
    weight_ref,
    part1_ref,
    part0_ref,
    part2_ref,
    small_ref,
    high_sum_ref,
    proj_sum_ref,
    conv_ref,
    table_ref,
    grad_ref,
    low_ref,
    char_ref,
    held_ref,
    own_ref,
    got_y_ref,
    got_x_ref,
    got_z_ref,
    all_z_ref,
    all_x_ref,
    wide_ref,
    conv_acc_ref,
    conv_got_ref,
    conv_two_ref,
    conv_in_ref,
    table_acc_ref,
    table_got_ref,
    load_sem,
    store_sem,
    y_send,
    y_recv,
    x_send,
    x_recv,
    z_send,
    z_recv,
    g_send,
    g_recv,
    h_send,
    h_recv,
    small_send,
    small_recv,
):
    tick = pl.program_id(0)
    dp = lax.axis_index("dp")
    mp = lax.axis_index("mp")
    core, high = lax.rem(dp, 2), dp // 2
    near, ring = lax.rem(mp, 2), mp // 2
    per_layer = part1_ref.shape[1]
    width = FILTERS * 2
    quarter = width // 4
    parts = (part1_ref, part0_ref, part2_ref)
    vocab = table_ref.shape[0] - small_ref.shape[0]
    core_peer = {"dp": dp + 1 - 2 * core, "mp": mp}
    high_peer = {"dp": dp + 2 - 4 * high, "mp": mp}
    near_peer = {"dp": dp, "mp": mp + 1 - 2 * near}

    def ring_index(offset):
        return lax.rem(ring + offset, 4)

    def ring_peer(offset):
        return {"dp": dp, "mp": 2 * ring_index(offset) + near}

    def remote(src, dst, send, recv, peer):
        return pltpu.make_async_remote_copy(
            src_ref=src, dst_ref=dst, send_sem=send, recv_sem=recv, device_id=peer, device_id_type=MESH
        )

    def y_copy(part, chunk, row):
        return remote(
            part.at[1 - high, row], got_y_ref.at[chunk], y_send.at[chunk], y_recv.at[chunk], high_peer
        )

    def y_start(chunk):
        for layer, part in enumerate(parts):

            @pl.when(chunk // per_layer == layer)
            def _():
                y_copy(part, chunk, chunk - layer * per_layer).start()

    def load(chunk, act):
        slot = lax.rem(chunk, 2)
        for layer, part in enumerate(parts):

            @pl.when(chunk // per_layer == layer)
            def _():
                copy = pltpu.make_async_copy(
                    part.at[high, chunk - layer * per_layer], own_ref.at[slot], load_sem.at[slot]
                )
                getattr(copy, act)()

    def x_copy(chunk):
        return remote(
            got_y_ref.at[chunk, 1 - near],
            got_x_ref.at[chunk],
            x_send.at[chunk],
            x_recv.at[chunk],
            near_peer,
        )

    def columns(index):
        return pl.ds(pl.multiple_of(index * quarter, quarter), quarter)

    def z_copy(chunk, offset):
        return remote(
            got_x_ref.at[chunk, :, columns(ring_index(offset))],
            got_z_ref.at[chunk, offset - 1],
            z_send.at[chunk, offset - 1],
            z_recv.at[chunk, offset - 1],
            ring_peer(offset),
        )

    def g_copy(chunk, offset, incoming):
        cols = columns(ring_index(4 - offset) if incoming else ring)
        return remote(
            all_z_ref.at[chunk, :, cols],
            all_z_ref.at[chunk, :, cols],
            g_send.at[chunk, offset - 1],
            g_recv.at[chunk, offset - 1],
            ring_peer(offset),
        )

    def h_copy(chunk):
        return remote(
            all_z_ref.at[chunk], all_x_ref.at[chunk], h_send.at[chunk], h_recv.at[chunk], near_peer
        )

    def store(chunk):
        slot = lax.rem(chunk, 2)
        return wide_ref.at[slot], store_sem.at[slot]

    def store_act(chunk, act):
        src, sem = store(chunk)
        layer, row = chunk // per_layer, lax.rem(chunk, per_layer)

        @pl.when(layer < 2)
        def _():
            getattr(pltpu.make_async_copy(src, high_sum_ref.at[1 - layer, row], sem), act)()

        @pl.when(layer == 2)
        def _():
            getattr(pltpu.make_async_copy(src, proj_sum_ref.at[row], sem), act)()

    def when_chunk(chunk, body):
        @pl.when(jnp.logical_and(chunk >= 0, chunk < chunks))
        def _():
            body(chunk)

    def do_y(chunk):
        y_copy(part1_ref, chunk, 0).wait_recv()
        load(chunk, "wait")
        slot = lax.rem(chunk, 2)
        for half in range(2):
            got_y_ref[chunk, half] = (
                got_y_ref[chunk, half].astype(jnp.float32) + own_ref[slot, half].astype(jnp.float32)
            ).astype(jnp.bfloat16)
        x_copy(chunk).start()

        @pl.when(chunk + AHEAD < chunks)
        def _():
            y_start(chunk + AHEAD)

        @pl.when(chunk + 2 < chunks)
        def _():
            load(chunk + 2, "start")

    def do_x(chunk):
        x_copy(chunk).wait_recv()
        got_x_ref[chunk] = (
            got_x_ref[chunk].astype(jnp.float32) + got_y_ref[chunk, near].astype(jnp.float32)
        ).astype(jnp.bfloat16)
        for offset in range(1, 4):
            z_copy(chunk, offset).start()

    def do_z(chunk):
        cols = columns(ring)
        total = got_x_ref[chunk, :, cols].astype(jnp.float32)
        for offset in range(1, 4):
            z_copy(chunk, offset).wait_recv()
            total = total + got_z_ref[chunk, offset - 1].astype(jnp.float32)
        all_z_ref[chunk, :, cols] = total.astype(jnp.bfloat16)
        for offset in range(1, 4):
            g_copy(chunk, offset, False).start()

    def do_g(chunk):
        for offset in range(1, 4):
            g_copy(chunk, offset, True).wait_recv()
        h_copy(chunk).start()

    def do_h(chunk):
        h_copy(chunk).wait_recv()

        @pl.when(chunk >= 2)
        def _():
            store_act(chunk - 2, "wait")

        slot = lax.rem(chunk, 2)
        wide_ref[slot, near] = all_z_ref[chunk]
        wide_ref[slot, 1 - near] = all_x_ref[chunk]
        store_act(chunk, "start")

    def small_copies(stage):
        if stage == 0:
            copies = [
                remote(
                    conv_two_ref.at[1, y],
                    conv_in_ref.at[y],
                    small_send.at[0, y],
                    small_recv.at[0, y],
                    core_peer,
                )
                for y in range(2)
            ]
            peer = core_peer
        else:
            if stage == 1:
                src = conv_two_ref.at[0, 1 - high]
                peer = high_peer
            else:
                src = conv_acc_ref.at[stage - 2]
                bit = 1 << (stage - 2)
                flip = lax.rem(mp // bit, 2)
                peer = {"dp": dp, "mp": mp + bit - 2 * bit * flip}
            copies = [
                remote(
                    src,
                    conv_got_ref.at[stage - 1],
                    small_send.at[stage, 0],
                    small_recv.at[stage, 0],
                    peer,
                )
            ]
        count = table_ref.shape[0] - (BIAS_ROWS if stage > 1 else 0)
        copies.append(
            remote(
                table_acc_ref.at[stage, pl.ds(0, count)],
                table_got_ref.at[stage, pl.ds(0, count)],
                small_send.at[stage, 2],
                small_recv.at[stage, 2],
                peer,
            )
        )
        return copies

    def small_start(stage):
        for copy in small_copies(stage):
            copy.start()

    def small_finish(stage):
        for copy in small_copies(stage):
            copy.wait()
        count = table_ref.shape[0] - (BIAS_ROWS if stage > 1 else 0)
        total = table_acc_ref[stage, :count] + table_got_ref[stage, :count]
        if stage == 1:
            table_ref[count - BIAS_ROWS :] = total[count - BIAS_ROWS :]
        if stage < 4:
            table_acc_ref[stage + 1, :count] = total
        else:
            table_ref[:count] = total
        if stage == 0:
            for y in range(2):
                conv_two_ref[0, y] = conv_two_ref[0, y] + conv_in_ref[y]
        elif stage == 1:
            conv_acc_ref[0] = conv_two_ref[0, high] + conv_got_ref[0]
        else:
            value = conv_acc_ref[stage - 2] + conv_got_ref[stage - 1]
            if stage < 4:
                conv_acc_ref[stage - 1] = value
            else:
                conv_ref[...] = value

    @pl.when(tick == 0)
    def _():
        barrier = pltpu.get_barrier_semaphore()
        for peer in [core_peer, high_peer, near_peer] + [ring_peer(offset) for offset in (1, 2, 3)]:
            pl.semaphore_signal(barrier, inc=1, device_id=peer, device_id_type=MESH)
        pl.semaphore_wait(barrier, 6)

        for chunk in range(AHEAD):
            y_start(jnp.int32(chunk))

        load(jnp.int32(0), "start")
        load(jnp.int32(1), "start")

    @pl.when(tick < SHIFTS)
    def _():
        conv_shift_step(
            tick,
            vec_ref,
            turned_ref,
            turned_extra_ref,
            ratio_ref,
            weight_ref,
            grad_ref,
            low_ref,
            char_ref,
            held_ref,
        )

    @pl.when(tick == SHIFTS - 1)
    def _():
        table_acc_ref[0, :vocab] = table_gradient(hot_ref, hot_extra_ref, char_ref, vocab)
        table_acc_ref[0, vocab:] = small_ref[...]
        span = FILTERS // 4
        for y in range(2):
            mine = pl.ds(pl.multiple_of((2 * y + core) * span, span), span)
            theirs = pl.ds(pl.multiple_of((2 * y + 1 - core) * span, span), span)
            conv_two_ref[0, y] = grad_ref[:, mine]
            conv_two_ref[1, y] = grad_ref[:, theirs]
        small_start(0)

    for stage in range(5):

        @pl.when(tick == SHIFTS + stage)
        def _():
            small_finish(stage)
            if stage < 4:
                small_start(stage + 1)

    for beat in range(BEATS):
        at = tick * BEATS + beat
        when_chunk(at, do_y)
        when_chunk(at - SLACK, do_x)
        when_chunk(at - 2 * SLACK, do_z)
        when_chunk(at - 3 * SLACK, do_g)
        when_chunk(at - 4 * SLACK, do_h)

    @pl.when(tick == pl.num_programs(0) - 1)
    def _():
        for chunk in (chunks - 2, chunks - 1):
            store_act(jnp.int32(chunk), "wait")

        @pl.loop(0, chunks)
        def _(chunk):
            y_copy(part1_ref, chunk, 0).wait_send()
            x_copy(chunk).wait_send()
            for offset in range(1, 4):
                z_copy(chunk, offset).wait_send()
                g_copy(chunk, offset, False).wait_send()
            h_copy(chunk).wait_send()


def conv_backward_and_sum(ids, vectors, ratio, weights, parts, small):
    groups, tokens, _ = vectors.shape
    full, _ = group_counts()
    vocab = -(-VOCAB // 8) * 8
    width = parts[0].shape[1]
    parts = [part.reshape(2, -1, 2, CHUNK_ROWS, width) for part in parts]
    chunks = sum(part.shape[1] for part in parts)
    table_rows = vocab + small.shape[0]
    conv_rows = TAPS * CDIM
    span = FILTERS // 4
    bf16, f32 = jnp.bfloat16, jnp.float32
    dma = pltpu.SemaphoreType.DMA
    last = SHIFTS - 1
    high_sum, proj_sum, grad, table = pl.pallas_call(
        functools.partial(tail_kernel, chunks),
        grid=(-(-(chunks + 4 * SLACK) // BEATS),),
        in_specs=[pl.BlockSpec(memory_space=pltpu.VMEM)] * 6
        + [pl.BlockSpec((1, 2 * GROUP, FILTERS), lambda t: (jnp.minimum(t, last), 0, 0))]
        + [pl.BlockSpec(memory_space=pl.ANY)] * 3
        + [pl.BlockSpec(memory_space=pltpu.VMEM)],
        out_specs=[
            pl.BlockSpec(memory_space=pl.ANY),
            pl.BlockSpec(memory_space=pl.ANY),
            pl.BlockSpec(memory_space=pltpu.VMEM),
            pl.BlockSpec(memory_space=pltpu.VMEM),
        ],
        out_shape=[
            jax.ShapeDtypeStruct((2,) + parts[0].shape[1:], bf16),
            jax.ShapeDtypeStruct(parts[2].shape[1:], bf16),
            jax.ShapeDtypeStruct((conv_rows, span), f32),
            jax.ShapeDtypeStruct((table_rows, GROUP), f32),
        ],
        scratch_shapes=[
            pltpu.VMEM((conv_rows, FILTERS), f32),
            pltpu.VMEM((full * tokens, FILTERS), bf16),
            pltpu.VMEM((groups, tokens, GROUP), f32),
            pltpu.VMEM((2 * GROUP, FBLOCK), f32),
            pltpu.VMEM((2, 2, CHUNK_ROWS, width), bf16),
            pltpu.VMEM((chunks, 2, CHUNK_ROWS, width), bf16),
            pltpu.VMEM((chunks, CHUNK_ROWS, width), bf16),
            pltpu.VMEM((chunks, 3, CHUNK_ROWS, width // 4), bf16),
            pltpu.VMEM((chunks, CHUNK_ROWS, width), bf16),
            pltpu.VMEM((chunks, CHUNK_ROWS, width), bf16),
            pltpu.VMEM((2, 2, CHUNK_ROWS, width), bf16),
            pltpu.VMEM((3, conv_rows, span), f32),
            pltpu.VMEM((4, conv_rows, span), f32),
            pltpu.VMEM((2, 2, conv_rows, span), f32),
            pltpu.VMEM((2, conv_rows, span), f32),
            pltpu.VMEM((5, table_rows, GROUP), f32),
            pltpu.VMEM((5, table_rows, GROUP), f32),
            dma((2,)),
            dma((2,)),
            dma((chunks,)),
            dma((chunks,)),
            dma((chunks,)),
            dma((chunks,)),
            dma((chunks, 3)),
            dma((chunks, 3)),
            dma((chunks, 3)),
            dma((chunks, 3)),
            dma((chunks,)),
            dma((chunks,)),
            dma((5, 3)),
            dma((5, 3)),
        ],
        compiler_params=pltpu.CompilerParams(
            collective_id=3, has_side_effects=True, vmem_limit_bytes=62 * 2**20
        ),
    )(*conv_operands(ids, vectors), ratio, weights, *parts, small)
    rest = table[vocab:]
    table = table[:vocab].reshape(vocab, SHIFTS, CDIM).sum(axis=1)[:VOCAB]
    return high_sum.reshape(2, -1, width), proj_sum, grad, table, rest


GROUPS = tuple(("high", layer, part) for layer in range(2) for part in range(2)) + (("proj", 0, 0),)
LOCAL = tuple((item, other) for other in range(2) for item in range(3))
START_STEPS = len(LOCAL) + 4


def start_kernel(
    ids_ref,
    table_ref,
    conv_ref,
    high_ref,
    proj_ref,
    win_ref,
    wst_ref,
    wpr_ref,
    total_ref,
    vec_ref,
    weight_ref,
    high_one,
    high_two,
    proj_all,
    win_all,
    wst_all,
    wpr_all,
    conv_got,
    conv_send,
    conv_recv,
    own_sem,
    core_send,
    core_recv,
    y_send,
    y_recv,
    x_send,
    x_recv,
    z_send,
    z_recv,
    c_send,
    c_recv,
    ly_send,
    ly_recv,
    lc_send,
    lc_recv,
    lx_send,
    lx_recv,
):
    step = pl.program_id(0)
    dp = lax.axis_index("dp")
    mp = lax.axis_index("mp")
    core, high = lax.rem(dp, 2), dp // 2
    near, ring = lax.rem(mp, 2), lax.rem(mp // 2, 2)
    across = dp + 2 - 4 * high
    core_peer = {"dp": dp + 1 - 2 * core, "mp": mp}
    high_peer = {"dp": across, "mp": mp}
    both_peer = {"dp": across + 1 - 2 * core, "mp": mp}
    near_peer = {"dp": dp, "mp": mp + 1 - 2 * near}
    ring_peer = {"dp": dp, "mp": mp + 2 - 4 * ring}
    lanes = wpr_ref.shape[2]
    mine = 2 * ring + near
    beside = 2 * ring + 1 - near
    beyond = 2 * (1 - ring)

    def from_shard(index, place):
        kind, layer, part = GROUPS[index]
        if kind == "high":
            return high_ref.at[layer, 4 * part + place]
        return proj_ref.at[place]

    def in_full(index, place, quarter):
        kind, layer, part = GROUPS[index]
        if kind == "high":
            return (high_one, high_two)[layer].at[quarter, 4 * part + place]
        return proj_all.at[quarter, place]

    def local_full(item, side, quarter):
        if item == 2:
            cols = pl.ds(pl.multiple_of(quarter * lanes, lanes), lanes)
            return wpr_all.at[side, :, cols]
        return (win_all, wst_all)[item].at[side, quarter]

    def side_of(index):
        return 1 - near if LOCAL[index][1] else near

    def local_source(index):
        item, other = LOCAL[index]
        if other:
            return local_full(item, 1 - near, dp)
        return (win_ref, wst_ref, wpr_ref)[item].at[near]

    def lx_copy(item):
        return remote(
            (win_ref, wst_ref, wpr_ref)[item].at[1 - near],
            local_full(item, near, dp),
            lx_send.at[item],
            lx_recv.at[item],
            near_peer,
        )

    def own_pair(index):
        if index < 2:
            return high_ref.at[index], (high_one, high_two)[index].at[dp]
        if index == 2:
            return proj_ref, proj_all.at[dp]
        return local_source(index - 3), local_full(LOCAL[index - 3][0], side_of(index - 3), dp)

    owned = 3 + len(LOCAL)

    def remote(src, dst, send, recv, peer):
        return pltpu.make_async_remote_copy(
            src_ref=src, dst_ref=dst, send_sem=send, recv_sem=recv, device_id=peer, device_id_type=MESH
        )

    def own_copy(index):
        src, dst = own_pair(index)
        return pltpu.make_async_copy(src, dst, own_sem.at[index])

    def core_copy(index):
        src, dst = own_pair(index)
        return remote(src, dst, core_send.at[index], core_recv.at[index], core_peer)

    def y_copy(index):
        return remote(
            from_shard(index, mine),
            in_full(index, mine, dp),
            y_send.at[index],
            y_recv.at[index],
            high_peer,
        )

    def x_copy(index):
        place = in_full(index, mine, across)
        return remote(place, place, x_send.at[index], x_recv.at[index], near_peer)

    def z_copy(index, which):
        place = in_full(index, 2 * ring + which, across)
        return remote(
            place, place, z_send.at[index, which], z_recv.at[index, which], ring_peer
        )

    def c_copy(index, place):
        ref = in_full(index, place, across)
        return remote(ref, ref, c_send.at[index, place], c_recv.at[index, place], core_peer)

    def ly_copy(index):
        return remote(
            local_source(index),
            local_full(LOCAL[index][0], side_of(index), dp),
            ly_send.at[index],
            ly_recv.at[index],
            high_peer,
        )

    def lc_copy(index):
        ref = local_full(LOCAL[index][0], side_of(index), across)
        return remote(ref, ref, lc_send.at[index], lc_recv.at[index], core_peer)

    conv_peers = (core_peer, high_peer, both_peer)

    def conv_copy(index):
        return remote(
            conv_ref, conv_got.at[dp], conv_send.at[index], conv_recv.at[index], conv_peers[index]
        )

    @pl.when(step == 0)
    def _():
        barrier = pltpu.get_barrier_semaphore()
        for peer in (core_peer, high_peer, both_peer, near_peer, ring_peer):
            pl.semaphore_signal(barrier, inc=1, device_id=peer, device_id_type=MESH)
        pl.semaphore_wait(barrier, 5)
        for index in range(3):
            conv_copy(index).start()
        y_copy(0).start()
        y_copy(1).start()
        ly_copy(0).start()
        for item in range(3):
            lx_copy(item).start()
        for index in range(2):
            core_copy(index).start()
            own_copy(index).start()
        char_vectors(ids_ref, table_ref, vec_ref)
        weight_ref[...] = jnp.zeros(weight_ref.shape, jnp.bfloat16)
        conv_got[dp] = conv_ref[...]
        for index in range(3):
            conv_copy(index).wait()
        span = conv_ref.shape[1]
        tap = lax.broadcasted_iota(jnp.int32, (TAPS * CDIM, span), 0) // CDIM
        for quarter in range(4):
            bound = position_bound(quarter * span, span, TAPS)
            part = conv_got[quarter]
            part = part * jnp.where(tap < CHARS - bound, 1.0, 0.0).astype(jnp.bfloat16)
            for shift in range(SHIFTS):
                weight_ref[
                    shift,
                    CDIM * shift : CDIM * (shift + TAPS),
                    quarter * span : (quarter + 1) * span,
                ] = part

    for index in range(len(GROUPS)):

        @pl.when(step == index + 1)
        def _():
            y_copy(index).wait_recv()
            if index + 2 < len(GROUPS):
                y_copy(index + 2).start()
            x_copy(index).start()
            z_copy(index, near).start()
            c_copy(index, mine).start()

        @pl.when(step == index + 2)
        def _():
            x_copy(index).wait_recv()
            z_copy(index, 1 - near).start()
            c_copy(index, beside).start()

        @pl.when(step == index + 3)
        def _():
            for which in range(2):
                z_copy(index, which).wait_recv()
                c_copy(index, beyond + which).start()

    for index in range(len(LOCAL)):
        if index:

            @pl.when(step == index)
            def _():
                if LOCAL[index][1]:
                    lx_copy(LOCAL[index][0]).wait_recv()
                ly_copy(index).start()

        @pl.when(step == index + 1)
        def _():
            core_copy(index + 3).start()
            if not LOCAL[index][1]:
                own_copy(index + 3).start()

        @pl.when(step == index + 3)
        def _():
            ly_copy(index).wait_recv()
            lc_copy(index).start()

    @pl.when(step == 1)
    def _():
        core_copy(2).start()
        own_copy(2).start()

    @pl.when(jnp.logical_and(step >= 1, step <= FILTERS // (2 * FBLOCK)))
    def _():
        for half in range(2):
            block = 2 * (step - 1) + half
            cols = pl.ds(pl.multiple_of(block * FBLOCK, FBLOCK), FBLOCK)
            conv_block(block, cols, vec_ref, weight_ref, total_ref)

    @pl.when(step == START_STEPS - 1)
    def _():
        for index in range(owned):
            if index < owned - 3:
                own_copy(index).wait()
            core_copy(index).wait()
        for item in range(3):
            lx_copy(item).wait_send()
        for index in range(len(GROUPS)):
            y_copy(index).wait_send()
            x_copy(index).wait_send()
            for which in range(2):
                z_copy(index, which).wait_send()
            for place in range(4):
                c_copy(index, place).wait()
        for index in range(len(LOCAL)):
            ly_copy(index).wait_send()
            lc_copy(index).wait()


def start_gather(ids, table_shift, conv, highway, proj, win, wst, wpr):
    tokens = ids.shape[0]
    groups = -(-CHARS // SHIFTS)
    bf16 = jnp.bfloat16
    depth, wide = highway.shape[1:]
    rows = proj.shape[0]
    highway = highway.reshape(2, 8, depth // 8, wide)
    proj = proj.reshape(4, rows // 4, PROJ)
    vmem = pl.BlockSpec(memory_space=pltpu.VMEM)
    hbm = pl.BlockSpec(memory_space=pl.ANY)
    dma = pltpu.SemaphoreType.DMA
    count, local = len(GROUPS), len(LOCAL)
    total, vec, weight, one, two, proj, win, wst, wpr = pl.pallas_call(
        start_kernel,
        grid=(START_STEPS,),
        in_specs=[vmem] * 8,
        out_specs=[vmem] * 3 + [hbm] * 6,
        out_shape=[
            jax.ShapeDtypeStruct((tokens, FILTERS), jnp.float32),
            jax.ShapeDtypeStruct((groups, tokens, GROUP), bf16),
            jax.ShapeDtypeStruct((SHIFTS, 2 * GROUP, FILTERS), bf16),
            jax.ShapeDtypeStruct((4,) + highway.shape[1:], bf16),
            jax.ShapeDtypeStruct((4,) + highway.shape[1:], bf16),
            jax.ShapeDtypeStruct((4,) + proj.shape, bf16),
            jax.ShapeDtypeStruct((2, 4) + win.shape[1:], bf16),
            jax.ShapeDtypeStruct((2, 4) + wst.shape[1:], bf16),
            jax.ShapeDtypeStruct(wpr.shape[:2] + (4 * wpr.shape[2],), bf16),
        ],
        scratch_shapes=[pltpu.VMEM((4,) + conv.shape, bf16)]
        + [dma((3,))] * 2
        + [dma((3 + local,))] * 3
        + [dma((count,))] * 4
        + [dma((count, 2))] * 2
        + [dma((count, 4))] * 2
        + [dma((local,))] * 4
        + [dma((3,))] * 2,
        compiler_params=pltpu.CompilerParams(
            collective_id=4, has_side_effects=True, vmem_limit_bytes=40 * 2**20
        ),
    )(ids, table_shift, conv, highway, proj, win, wst, wpr)
    return (
        total,
        vec,
        weight,
        [one.reshape(4 * depth, wide), two.reshape(4 * depth, wide)],
        proj.reshape(4 * rows, PROJ),
        win.reshape(2, PROJ, -1),
        wst.reshape(2, PROJ, -1),
        wpr,
    )


def swap(value, axis, bit):
    size = lax.axis_size(axis)
    return lax.ppermute(value, axis, [(index, index ^ bit) for index in range(size)])


def scatter_start(value, axis, dim):
    index = lax.axis_index(axis)
    quarter = value.shape[dim] // 4
    low, high = index % 2, index // 2

    def pick(side, part):
        return lax.dynamic_slice_in_dim(value, (2 * side + part) * quarter, quarter, dim)

    def both(side):
        got = swap(pick(side, 1 - low), axis, 1)
        return (pick(side, low).astype(jnp.float32) + got.astype(jnp.float32)).astype(value.dtype)

    return both(high), both(1 - high)


def weight_part(left, right):
    tokens, depth = left.shape
    core = lax.axis_index("dp") % 2
    quarter = depth // 4

    def columns(which):
        return jnp.concatenate(
            [
                lax.dynamic_slice_in_dim(left, (2 * half + which) * quarter, quarter, 1)
                for half in range(2)
            ],
            axis=1,
        )

    own, other = columns(core), columns(1 - core)
    left_all = jnp.concatenate([own, swap(other, "dp", 1)], axis=0)
    right_all = jnp.concatenate([right, swap(right, "dp", 1)], axis=0)
    return jnp.dot(left_all.T, right_all, preferred_element_type=jnp.float32).astype(jnp.bfloat16)


def weight_grad(left, right):
    part = jnp.dot(left.T, right, preferred_element_type=jnp.float32).astype(jnp.bfloat16)
    return lax.psum_scatter(part, "dp", scatter_dimension=0, tiled=True)


def shards(
    char_ids,
    doc_lengths,
    window_doc,
    window_offset,
    char_table,
    conv_weight,
    conv_bias,
    highway_weight,
    highway_bias,
    proj_weight,
    proj_bias,
    lstm_input_weight,
    lstm_state_weight,
    lstm_bias,
    lstm_proj,
    init_cell,
    init_hidden,
    cotangent,
):
    tok_share = char_ids.shape[0]
    row_count = window_doc.shape[0]
    cell_local = init_cell.shape[2]
    gate_local = lstm_bias.shape[1]
    mp_index = lax.axis_index("mp")
    mp_size = lax.axis_size("mp")
    paired = lax.axis_size("dp") == 4 and mp_size == 8
    dp_index = lax.axis_index("dp")
    dp_width = conv_weight.shape[2]
    widths = filter_widths(FILTERS)
    tap_mask = jnp.arange(TAPS)[:, None] < widths[None, :]
    lows = [
        value.astype(jnp.bfloat16)
        for value in (
            conv_weight,
            highway_weight,
            proj_weight,
            lstm_input_weight,
            lstm_state_weight,
            lstm_proj,
        )
    ]
    counts = (CHARS + 1 - widths).astype(jnp.float32)
    table_low = char_table.astype(jnp.bfloat16)
    table_shifted = jnp.stack(
        [
            jnp.pad(
                table_low,
                ((0, -VOCAB % UNIT_BLOCK), (CDIM * shift, GROUP - CDIM * (shift + 1))),
            )
            for shift in range(SHIFTS)
        ]
    )
    rows_own = row_count // mp_size
    ids_time = char_ids.reshape(rows_own, WIN, CHARS).transpose(1, 0, 2).reshape(tok_share, CHARS)
    tok_pad = -tok_share % 16
    ids_time = jnp.pad(ids_time, ((0, tok_pad), (0, 0)))
    if paired:
        lows[0] = lows[0].reshape(TAPS * CDIM, dp_width)
        (
            exp_total,
            char_vecs,
            conv_shifted,
            high_full,
            proj_full,
            input_full,
            state_full,
            lproj_full,
        ) = start_gather(ids_time, table_shifted, *lows)
    else:
        conv_full, high_full, proj_full, input_full, state_full, lproj_full = (
            lax.all_gather(value, "dp", axis=dim, tiled=True)
            for value, dim in zip(lows, (2, 1, 0, 1, 1, 2))
        )
        conv_matrix = (conv_full * tap_mask[:, None, :].astype(jnp.bfloat16)).reshape(
            TAPS * CDIM, FILTERS
        )
        conv_shifted = jnp.stack(
            [
                jnp.pad(conv_matrix, ((CDIM * shift, 2 * GROUP - CDIM * (shift + TAPS)), (0, 0)))
                for shift in range(SHIFTS)
            ]
        )
        exp_total, char_vecs = conv_forward(ids_time, table_shifted, conv_shifted)
    pooled = jnp.log(exp_total[:tok_share] / counts)
    pre_pool = pooled + conv_bias
    layer_value = jax.nn.silu(pre_pool)
    kept_inputs = []
    kept_mixed = []
    for layer_index in range(2):
        mixed = (
            jnp.dot(
                layer_value.astype(jnp.bfloat16),
                high_full[layer_index],
                preferred_element_type=jnp.float32,
            )
            + highway_bias[layer_index]
        )
        kept_inputs.append(layer_value)
        kept_mixed.append(mixed)
        gate_value = jax.nn.sigmoid(mixed[:, FILTERS:])
        layer_value = gate_value * layer_value + (1.0 - gate_value) * jax.nn.silu(
            mixed[:, :FILTERS]
        )
    top_low = layer_value.astype(jnp.bfloat16)
    embed_local = jnp.dot(top_low, proj_full, preferred_element_type=jnp.float32) + proj_bias
    part_rows = -(-rows_own // 16) * 16
    rows = mp_size * part_rows

    def pad_rows(value, axis):
        shape = value.shape
        split = value.reshape(shape[:axis] + (mp_size, rows_own) + shape[axis + 1 :])
        widths = [(0, 0)] * split.ndim
        widths[axis + 1] = (0, part_rows - rows_own)
        return jnp.pad(split, widths)

    def drop_rows(value, axis):
        shape = value.shape
        split = value.reshape(shape[:axis] + (mp_size, part_rows) + shape[axis + 1 :])
        kept = lax.slice_in_dim(split, 0, rows_own, axis=axis + 1)
        return kept.reshape(shape[:axis] + (row_count,) + shape[axis + 1 :])

    embed_own = jnp.pad(
        embed_local.astype(jnp.bfloat16).reshape(WIN, rows_own, PROJ),
        ((0, 0), (0, part_rows - rows_own), (0, 0)),
    )
    embed_all = lax.all_gather(embed_own, "mp", axis=0)
    doc_index = jnp.arange(doc_lengths.shape[0])
    chosen_len = jnp.sum(
        jnp.where(window_doc[:, None] == doc_index[None, :], doc_lengths[None, :], 0), axis=1
    )
    reset_at = (chosen_len - window_offset).astype(jnp.int32)
    near, ring = mp_index % 2, mp_index // 2

    def by_near(own, got):
        return jnp.where(near == 0, jnp.stack([own, got]), jnp.stack([got, own]))

    def take(value, index, dim=0):
        size = value.shape[dim] // 2
        return lax.dynamic_slice_in_dim(value, index * size, size, dim)

    def to_owner(value):
        return by_near(
            take(value, near).reshape(value.shape[1:]),
            swap(take(value, 1 - near), "mp", 1).reshape(value.shape[1:]),
        )

    def chains(value, axis):
        shape = value.shape
        split = value.reshape(shape[:axis] + (4, 2, rows_own) + shape[axis + 1 :])
        widths = [(0, 0)] * split.ndim
        widths[axis + 2] = (0, part_rows - rows_own)
        split = jnp.moveaxis(jnp.pad(split, widths), axis + 1, 0)
        return split.reshape((2,) + shape[:axis] + (4 * part_rows,) + shape[axis + 1 :])

    if paired:
        reset_wide = jnp.broadcast_to(
            chains(reset_at, 0)[:, :, None], (2, 4 * part_rows, UNIT_BLOCK)
        )
        hidden_rows = chains(take(init_hidden, near)[0], 0).reshape(2, 4, part_rows, PROJ)
        embed_time, gates, cprevs, cnews, lows, hprevs, stats, outs = ring_forward(
            embed_all.reshape(4, 2, WIN, part_rows, PROJ),
            input_full,
            state_full,
            lproj_full,
            to_owner(lstm_bias)[:, None, :],
            chains(to_owner(init_cell), 1),
            hidden_rows,
            reset_wide,
        )
        hidden = jnp.concatenate(
            [
                jnp.transpose(drop_rows(outs[way].reshape(WIN, rows, PROJ), 1), (1, 0, 2))
                for way in range(2)
            ],
            axis=-1,
        )
        own_cot = lax.dynamic_slice(
            cotangent, (ring * 2 * rows_own, 0, near * PROJ), (2 * rows_own, WIN, PROJ)
        )
        own_cot = jnp.transpose(own_cot.reshape(2, rows_own, WIN, PROJ), (0, 2, 1, 3))
        own_cot = jnp.pad(own_cot, ((0, 0), (0, 0), (0, part_rows - rows_own), (0, 0)))
        das, dss, bias_part, embed_back = ring_backward(
            gates, cprevs, cnews, own_cot, stats, input_full, state_full, lproj_full, reset_wide
        )
        bias_part = jnp.sum(bias_part, axis=0).reshape(2, gate_local)
        grad_bias = to_owner(bias_part)
        grad_embed_local = embed_back[:, :rows_own].reshape(tok_share, PROJ)
    else:
        reset_rows = pad_rows(reset_at[:, None], 0).reshape(rows, 1)
        reset_wide = jnp.broadcast_to(reset_rows, (rows, UNIT_BLOCK))
        cell_rows = pad_rows(init_cell, 1).reshape(2, rows, cell_local)
        hidden_rows = pad_rows(init_hidden, 1)
        kept = lstm_forward(
            mp_size,
            embed_all,
            input_full,
            state_full,
            lproj_full,
            lstm_bias[:, None, :],
            cell_rows,
            hidden_rows,
            reset_wide,
        )
        embed_time = kept[0]
        gates, cprevs, cnews, lows, hprevs, stats, outs = (
            kept[1 + 2 * index : 3 + 2 * index] for index in range(7)
        )
        hidden = jnp.concatenate(
            [jnp.transpose(drop_rows(value, 1), (1, 0, 2)) for value in outs], axis=-1
        )
        own_cot = lax.dynamic_slice_in_dim(cotangent, mp_index * rows_own, rows_own, 0)
        own_cot = jnp.pad(
            jnp.transpose(own_cot, (1, 0, 2)), ((0, 0), (0, part_rows - rows_own), (0, 0))
        )
        cots = (own_cot[:, :, :PROJ], own_cot[:, :, PROJ:])
        back = lstm_backward(
            mp_size, gates, cprevs, cnews, cots, stats, input_full, state_full, lproj_full, reset_wide
        )
        das, dss = back[0:2], back[2:4]
        grad_bias = jnp.sum(back[4], axis=1)
        grad_embed_local = back[5][:, :rows_own].reshape(tok_share, PROJ)

    def outer(left, right):
        return jnp.dot(
            left.reshape(WIN * rows, -1).T,
            right.reshape(WIN * rows, -1),
            preferred_element_type=jnp.float32,
        ).astype(jnp.bfloat16)

    if paired:
        lstm_parts = [
            (outer(embed_time, das), 0, 1),
            (outer(hprevs, das), 0, 1),
            (outer(lows, dss), 1, 0),
        ]
        outers, grad_embed_local = lax.optimization_barrier(
            ([scatter_start(part, "dp", over) for part, over, _ in lstm_parts], grad_embed_local)
        )
        lstm_grads = []
        for (own, other), (_, _, dim) in zip(outers, lstm_parts):
            got = swap(other, "dp", 2)
            sums = [
                take(own, which, dim).astype(jnp.float32) + take(got, which, dim).astype(jnp.float32)
                for which in (near, 1 - near)
            ]
            lstm_grads.append((sums[0], swap(sums[1].astype(jnp.bfloat16), "mp", 1)))
    else:
        lstm_parts = [
            (outer(left[way], right[way]), dim)
            for left, right, dim in (((embed_time,) * 2, das, 0), (hprevs, das, 0), (lows, dss, 1))
            for way in range(2)
        ]
    grad_pb = jnp.sum(grad_embed_local.astype(jnp.float32), axis=0)
    summed = []
    grad_hb = [None, None]
    grad_layer = jnp.dot(grad_embed_local, proj_full.T, preferred_element_type=jnp.float32)
    for layer_index in (1, 0):
        layer_in = kept_inputs[layer_index]
        mixed = kept_mixed[layer_index]
        transform = mixed[:, :FILTERS]
        gate_value = jax.nn.sigmoid(mixed[:, FILTERS:])
        grad_gate = (
            grad_layer * (layer_in - jax.nn.silu(transform)) * gate_value * (1.0 - gate_value)
        )
        grad_trans = grad_layer * (1.0 - gate_value) * silu_slope(transform)
        grad_mixed = jnp.concatenate([grad_trans, grad_gate], axis=1).astype(jnp.bfloat16)
        layer_low = layer_in.astype(jnp.bfloat16)
        if paired:
            summed.append(weight_part(layer_low, grad_mixed))
        else:
            summed.append(lax.psum(weight_grad(layer_low, grad_mixed), "mp"))
        grad_hb[layer_index] = jnp.sum(grad_mixed.astype(jnp.float32), axis=0)
        grad_layer = grad_layer * gate_value + jnp.dot(
            grad_mixed, high_full[layer_index].T, preferred_element_type=jnp.float32
        )
    grad_pre_pool = grad_layer * silu_slope(pre_pool)
    grad_cb = jnp.sum(grad_pre_pool, axis=0)

    ratio = jnp.pad(grad_pre_pool / exp_total[:tok_share], ((0, tok_pad), (0, 0)))
    low_mask = tap_mask[:, None, :].astype(jnp.float32)
    shared = [grad_cb, jnp.stack(grad_hb), grad_pb]

    def flatten(values, unit):
        flat = jnp.concatenate([value.reshape(-1) for value in values])
        return jnp.pad(flat, (0, -flat.size % unit)).reshape(-1, UNIT_BLOCK)

    def unflatten(flat, values):
        flat, pieces, start = flat.reshape(-1), [], 0
        for value in values:
            pieces.append(flat[start : start + value.size].reshape(value.shape))
            start += value.size
        return pieces

    if paired:
        pw_part = weight_part(top_low, grad_embed_local).reshape(2, -1, summed[0].shape[1])
        small = flatten(shared, 8 * UNIT_BLOCK)
        count = small.shape[0]
        small = jnp.concatenate([small, grad_bias.reshape(BIAS_ROWS, UNIT_BLOCK)])
        high_sum, pw_sum, grad_conv, grad_table, rest = conv_backward_and_sum(
            ids_time, char_vecs, ratio, conv_shifted, summed + [pw_part], small
        )
        lstm_grads, rest = lax.optimization_barrier((lstm_grads, rest))
        lstm_grads = [by_near(own, got.astype(jnp.float32)) for own, got in lstm_grads]
        own_mask = lax.dynamic_slice_in_dim(low_mask, dp_index * dp_width, dp_width, 2)
        grad_cw = grad_conv.reshape(TAPS, CDIM, dp_width) * own_mask
        grad_cb, grad_hbs, grad_pb = unflatten(rest[:count], shared)
        grad_lbias = rest[count:].reshape(grad_bias.shape)
        grad_hws = high_sum.astype(jnp.float32)
        grad_pws = pw_sum.reshape(-1, PROJ).astype(jnp.float32)
    else:
        lstm_parts = [
            lax.psum_scatter(part, "dp", scatter_dimension=dim, tiled=True).astype(jnp.float32)
            for part, dim in lstm_parts
        ]
        pw_part = weight_grad(top_low, grad_embed_local)
        grad_pws = lax.psum(pw_part, "mp").astype(jnp.float32)
        grad_conv, grad_table = conv_backward(ids_time, char_vecs, ratio, conv_shifted)
        grad_conv = grad_conv.reshape(TAPS, CDIM, FILTERS) * low_mask
        grad_hws = jnp.stack([summed[1].astype(jnp.float32), summed[0].astype(jnp.float32)])
        shared = [grad_table, grad_conv] + shared
        flat = lax.psum(flatten(shared, 8 * UNIT_BLOCK), ("dp", "mp"))
        grad_table, grad_conv, grad_cb, grad_hbs, grad_pb = unflatten(flat, shared)
        grad_cw = lax.dynamic_slice_in_dim(grad_conv, dp_index * dp_width, dp_width, 2)
        grad_lbias = lax.psum(grad_bias, "dp")
    if not paired:
        lstm_grads = [jnp.stack(lstm_parts[2 * index : 2 * index + 2]) for index in range(3)]
    grad_input, grad_state, grad_lproj = lstm_grads
    return (
        hidden,
        grad_table,
        grad_cw,
        grad_cb,
        grad_hws,
        grad_hbs,
        grad_pws,
        grad_pb,
        grad_input,
        grad_state,
        grad_lbias,
        grad_lproj,
    )


def solution(mesh):
    in_specs = (
        P(("dp", "mp"), None),
        P(),
        P("dp"),
        P("dp"),
        P(),
        P(None, None, "dp"),
        P(),
        P(None, "dp", None),
        P(),
        P("dp", None),
        P(),
        P(None, "dp", "mp"),
        P(None, "dp", "mp"),
        P(None, "mp"),
        P(None, "mp", "dp"),
        P(None, "dp", "mp"),
        P(None, "dp", None),
        P("dp", None, None),
    )
    out_specs = (
        P("dp", None, None),
        P(),
        P(None, None, "dp"),
        P(),
        P(None, "dp", None),
        P(),
        P("dp", None),
        P(),
        P(None, "dp", "mp"),
        P(None, "dp", "mp"),
        P(None, "mp"),
        P(None, "mp", "dp"),
    )
    return jax.shard_map(shards, mesh=mesh, in_specs=in_specs, out_specs=out_specs, check_vma=False)
```

```python
import functools
import math

import jax
import jax.numpy as jnp
from jax import lax
from jax.experimental import pallas as pl
from jax.experimental.pallas import tpu as pltpu
from jax.sharding import PartitionSpec as P

VOCAB = 262
CHARS = 50
CDIM = 16
TAPS = 7
FILTERS = 2048
PROJ = 512
UNIT_BLOCK = 128
WIN = 20
GATES = 16384


CLIP = 3.0


def filter_widths(count):
    unit_size = count // 64
    index_row = jnp.arange(count)
    widths = jnp.ones((count,), jnp.int32)
    for exponent in range(6):
        widths = widths + (index_row >= unit_size * (1 << exponent)).astype(jnp.int32)
    return widths


def silu_slope(value):
    sigma = jax.nn.sigmoid(value)
    return sigma * (1.0 + value * (1.0 - sigma))


def sigmoid_of(value):
    return 0.5 * jnp.tanh(0.5 * value) + 0.5


def mp_barrier(size):
    me = lax.axis_index("mp")
    barrier = pltpu.get_barrier_semaphore()
    for offset in range(1, size):
        peer = lax.rem(me + offset, size)
        pl.semaphore_signal(
            barrier, inc=1, device_id={"mp": peer}, device_id_type=pl.DeviceIdType.MESH
        )
    pl.semaphore_wait(barrier, size - 1)


class Exchange:
    def __init__(self, size, part_ref, sum_ref, all_ref, sems):
        self.size = size
        self.me = lax.axis_index("mp")
        self.part_ref, self.sum_ref, self.all_ref = part_ref, sum_ref, all_ref
        self.part_send, self.part_recv, self.all_send, self.all_recv = sems

    def part_copy(self, way, offset, incoming):
        peer = lax.rem(self.me + (self.size - offset if incoming else offset), self.size)
        return pltpu.make_async_remote_copy(
            src_ref=self.part_ref.at[way, peer],
            dst_ref=self.sum_ref.at[way, peer if incoming else self.me],
            send_sem=self.part_send.at[way, offset],
            recv_sem=self.part_recv.at[way, offset],
            device_id={"mp": peer},
            device_id_type=pl.DeviceIdType.MESH,
        )

    def all_copy(self, way, offset, incoming):
        peer = lax.rem(self.me + (self.size - offset if incoming else offset), self.size)
        slot = peer if incoming else self.me
        return pltpu.make_async_remote_copy(
            src_ref=self.all_ref.at[way, slot],
            dst_ref=self.all_ref.at[way, slot],
            send_sem=self.all_send.at[way, offset],
            recv_sem=self.all_recv.at[way, offset],
            device_id={"mp": peer},
            device_id_type=pl.DeviceIdType.MESH,
        )

    def send_parts(self, way):
        for offset in range(1, self.size):
            self.part_copy(way, offset, False).start()

    def take_sum(self, way):
        total = self.part_ref[way, self.me].astype(jnp.float32)
        for offset in range(1, self.size):
            self.part_copy(way, offset, True).wait_recv()
            peer = lax.rem(self.me + self.size - offset, self.size)
            total = total + self.sum_ref[way, peer].astype(jnp.float32)
        for offset in range(1, self.size):
            self.part_copy(way, offset, False).wait_send()
        return total

    def send_all(self, way, value):
        self.all_ref[way, self.me] = value
        for offset in range(1, self.size):
            self.all_copy(way, offset, False).start()

    def wait_all(self, way):
        for offset in range(1, self.size):
            self.all_copy(way, offset, True).wait_recv()
        for offset in range(1, self.size):
            self.all_copy(way, offset, False).wait_send()


def forward_kernel(
    size,
    emb_ref,
    win_ref,
    wst_ref,
    wpr_ref,
    bias_ref,
    cell_ref,
    hid_ref,
    reset_ref,
    embt_ref,
    gate0_ref,
    gate1_ref,
    cprev0_ref,
    cprev1_ref,
    cnew0_ref,
    cnew1_ref,
    low0_ref,
    low1_ref,
    hprev0_ref,
    hprev1_ref,
    stat0_ref,
    stat1_ref,
    out0_ref,
    out1_ref,
    pre_ref,
    state_ref,
    part_ref,
    sum_ref,
    all_ref,
    part_send,
    part_recv,
    all_send,
    all_recv,
):
    step = pl.program_id(0)
    rows = reset_ref.shape[0]
    units = cell_ref.shape[2]
    blocks = units // UNIT_BLOCK
    wide = 4 * UNIT_BLOCK
    comm = Exchange(size, part_ref, sum_ref, all_ref, (part_send, part_recv, all_send, all_recv))
    gate_refs = (gate0_ref, gate1_ref)
    cprev_refs = (cprev0_ref, cprev1_ref)
    cnew_refs = (cnew0_ref, cnew1_ref)
    low_refs = (low0_ref, low1_ref)
    hprev_refs = (hprev0_ref, hprev1_ref)
    stat_refs = (stat0_ref, stat1_ref)
    out_refs = (out0_ref, out1_ref)

    def time_of(way, at):
        return at if way == 0 else WIN - 1 - at

    def input_part(way, at):
        emb = emb_ref[:, time_of(way, at)].reshape(rows, PROJ)
        for block in range(blocks):
            cols = slice(block * wide, (block + 1) * wide)
            pre_ref[way, :, cols] = (
                jnp.dot(emb, win_ref[way, :, cols], preferred_element_type=jnp.float32)
                + bias_ref[way, :, cols]
            )

    def emit_hidden(way):
        out_refs[way][0] = all_ref[way].reshape(rows, PROJ)

    def cell_step(way):
        now = time_of(way, step)
        keep = jnp.where(reset_ref[...] - way == now, 0.0, 1.0)
        keep_low = jnp.concatenate([keep.astype(jnp.bfloat16)] * (PROJ // UNIT_BLOCK), axis=1)
        hidden_prev = all_ref[way].reshape(rows, PROJ) * keep_low
        hprev_refs[way][0] = hidden_prev
        if way == 0:
            embt_ref[0] = emb_ref[:, step].reshape(rows, PROJ)
        for block in range(blocks):
            cols = slice(block * wide, (block + 1) * wide)
            unit = slice(block * UNIT_BLOCK, (block + 1) * UNIT_BLOCK)
            pre = pre_ref[way, :, cols] + jnp.dot(
                hidden_prev, wst_ref[way, :, cols], preferred_element_type=jnp.float32
            )
            gate_in = sigmoid_of(pre[:, :UNIT_BLOCK])
            gate_forget = sigmoid_of(pre[:, UNIT_BLOCK : 2 * UNIT_BLOCK])
            gate_cand = jnp.tanh(pre[:, 2 * UNIT_BLOCK : 3 * UNIT_BLOCK])
            gate_out = sigmoid_of(pre[:, 3 * UNIT_BLOCK :])
            cell_prev = state_ref[way, :, unit] * keep
            cell_new = CLIP * jnp.tanh(
                (gate_forget * cell_prev + gate_in * gate_cand) * (1.0 / CLIP)
            )
            gate_refs[way][0, :, cols] = jnp.concatenate(
                [gate_in, gate_forget, gate_cand, gate_out], axis=1
            )
            cprev_refs[way][0, :, unit] = cell_prev
            cnew_refs[way][0, :, unit] = cell_new
            state_ref[way, :, unit] = cell_new
            low_refs[way][0, :, unit] = (gate_out * jnp.tanh(cell_new)).astype(jnp.bfloat16)
        partial = jnp.dot(low_refs[way][0], wpr_ref[way], preferred_element_type=jnp.float32)
        part_ref[way] = partial.astype(jnp.bfloat16).reshape(size, rows // size, PROJ)
        comm.send_parts(way)

    def close_step(way):
        total = comm.take_sum(way)
        stat_refs[way][0] = total
        comm.send_all(way, (CLIP * jnp.tanh(total * (1.0 / CLIP))).astype(jnp.bfloat16))

    @pl.when(step == 0)
    def _():
        for way in range(2):
            all_ref[way] = hid_ref[way]
            state_ref[way] = cell_ref[way]
            input_part(way, 0)
        mp_barrier(size)

    @pl.when(step > 0)
    def _():
        comm.wait_all(0)
        emit_hidden(0)

    @pl.when(step < WIN)
    def _():
        cell_step(0)

    @pl.when(step > 0)
    def _():
        close_step(1)

    @pl.when(step < WIN)
    def _():
        @pl.when(step < WIN - 1)
        def _():
            input_part(0, step + 1)

        close_step(0)

    @pl.when(step > 0)
    def _():
        comm.wait_all(1)
        emit_hidden(1)

    @pl.when(step < WIN)
    def _():
        cell_step(1)

        @pl.when(step < WIN - 1)
        def _():
            input_part(1, step + 1)


def lstm_forward(size, emb, win, wst, wpr, bias, cell, hid, reset):
    rows = reset.shape[0]
    part = rows // size
    gates = win.shape[2]
    units = cell.shape[2]
    last = WIN - 1
    vmem = pl.BlockSpec(memory_space=pltpu.VMEM)

    def block(shape, index):
        return pl.BlockSpec((1,) + shape, lambda w: (index(w), 0, 0))

    now0 = lambda w: jnp.minimum(w, last)
    now1 = lambda w: last - jnp.minimum(w, last)
    past0 = lambda w: jnp.maximum(w - 1, 0)
    past1 = lambda w: last - jnp.maximum(w - 1, 0)
    outs = [((rows, PROJ), jnp.bfloat16, now0)]
    for width, kind in ((gates, jnp.float32), (units, jnp.float32), (units, jnp.float32), (units, jnp.bfloat16), (PROJ, jnp.bfloat16)):
        outs += [((rows, width), kind, now0), ((rows, width), kind, now1)]
    outs += [((part, PROJ), jnp.float32, now0), ((part, PROJ), jnp.float32, past1)]
    outs += [((rows, PROJ), jnp.bfloat16, past0), ((rows, PROJ), jnp.bfloat16, past1)]
    return pl.pallas_call(
        functools.partial(forward_kernel, size),
        grid=(WIN + 1,),
        in_specs=[vmem] * 8,
        out_specs=[block(shape, index) for shape, kind, index in outs],
        out_shape=[jax.ShapeDtypeStruct((WIN,) + shape, kind) for shape, kind, index in outs],
        scratch_shapes=[
            pltpu.VMEM((2, rows, gates), jnp.float32),
            pltpu.VMEM((2, rows, units), jnp.float32),
            pltpu.VMEM((2, size, part, PROJ), jnp.bfloat16),
            pltpu.VMEM((2, size, part, PROJ), jnp.bfloat16),
            pltpu.VMEM((2, size, part, PROJ), jnp.bfloat16),
        ]
        + [pltpu.SemaphoreType.DMA((2, size))] * 4,
        compiler_params=pltpu.CompilerParams(
            collective_id=1, has_side_effects=True, vmem_limit_bytes=56 * 2**20
        ),
    )(emb, win, wst, wpr, bias, cell, hid, reset)


def backward_kernel(
    size,
    gate0_ref,
    gate1_ref,
    cprev0_ref,
    cprev1_ref,
    cnew0_ref,
    cnew1_ref,
    cot0_ref,
    cot1_ref,
    stat0_ref,
    stat1_ref,
    win_ref,
    wst_ref,
    wpr_ref,
    reset_ref,
    first_cot_ref,
    first_stat_ref,
    da0_ref,
    da1_ref,
    ds0_ref,
    ds1_ref,
    bias_ref,
    de_ref,
    cell_ref,
    part_ref,
    sum_ref,
    all_ref,
    part_send,
    part_recv,
    all_send,
    all_recv,
    held_ref,
    embed_part_ref,
    embed_got_ref,
    embed_send,
    embed_recv,
):
    step = pl.program_id(0)
    rows = reset_ref.shape[0]
    part = rows // size
    units = cell_ref.shape[2]
    blocks = units // UNIT_BLOCK
    wide = 4 * UNIT_BLOCK
    comm = Exchange(size, part_ref, sum_ref, all_ref, (part_send, part_recv, all_send, all_recv))
    gate_refs = (gate0_ref, gate1_ref)
    cprev_refs = (cprev0_ref, cprev1_ref)
    cnew_refs = (cnew0_ref, cnew1_ref)
    da_refs = (da0_ref, da1_ref)
    ds_refs = (ds0_ref, ds1_ref)

    def time_of(way, at):
        return WIN - 1 - at if way == 0 else at

    def stat_step(way, at, cot, stat, total):
        grad = cot.astype(jnp.float32)
        if total is not None:
            own = reset_ref[pl.ds(comm.me * part, part), :] - way
            keep = jnp.where(own == time_of(way, at - 1), 0.0, 1.0)
            grad = grad + total * jnp.concatenate([keep] * (PROJ // UNIT_BLOCK), axis=1)
        slope = jnp.tanh(stat * (1.0 / CLIP))
        comm.send_all(way, (grad * (1.0 - slope * slope)).astype(jnp.bfloat16))

    def cell_step(way):
        comm.wait_all(way)
        now = time_of(way, step)
        keep = jnp.where(reset_ref[...] - way == now, 0.0, 1.0)
        grad_stat = all_ref[way].reshape(rows, PROJ)
        ds_refs[way][0] = grad_stat
        for block in range(blocks):
            cols = slice(block * wide, (block + 1) * wide)
            unit = slice(block * UNIT_BLOCK, (block + 1) * UNIT_BLOCK)
            grad_out = lax.dot_general(
                grad_stat,
                wpr_ref[way, unit, :],
                (((1,), (1,)), ((), ())),
                preferred_element_type=jnp.float32,
            )
            gates = gate_refs[way][0, :, cols]
            gate_in = gates[:, :UNIT_BLOCK]
            gate_forget = gates[:, UNIT_BLOCK : 2 * UNIT_BLOCK]
            gate_cand = gates[:, 2 * UNIT_BLOCK : 3 * UNIT_BLOCK]
            gate_out = gates[:, 3 * UNIT_BLOCK :]
            cell_prev = cprev_refs[way][0, :, unit]
            cell_new = cnew_refs[way][0, :, unit]
            tanh_cell = jnp.tanh(cell_new)
            grad_total = (
                grad_out * gate_out * (1.0 - tanh_cell * tanh_cell) + cell_ref[way, :, unit]
            )
            scaled = cell_new * (1.0 / CLIP)
            grad_inner = grad_total * (1.0 - scaled * scaled)
            cell_ref[way, :, unit] = grad_inner * gate_forget * keep
            grad_pre = jnp.concatenate(
                [
                    grad_inner * gate_cand * gate_in * (1.0 - gate_in),
                    grad_inner * cell_prev * gate_forget * (1.0 - gate_forget),
                    grad_inner * gate_in * (1.0 - gate_cand * gate_cand),
                    grad_out * tanh_cell * gate_out * (1.0 - gate_out),
                ],
                axis=1,
            ).astype(jnp.bfloat16)
            da_refs[way][0, :, cols] = grad_pre
            bias_ref[way, :, cols] += jnp.sum(
                grad_pre.astype(jnp.float32).reshape(rows // 8, 8, wide), axis=0
            )

        @pl.when(step < WIN - 1)
        def _():
            partial = lax.dot_general(
                da_refs[way][0],
                wst_ref[way],
                (((1,), (1,)), ((), ())),
                preferred_element_type=jnp.float32,
            )
            part_ref[way] = partial.astype(jnp.bfloat16).reshape(size, part, PROJ)
            comm.send_parts(way)

    def embed_copy(src, dst, offset):
        return pltpu.make_async_remote_copy(
            src_ref=src,
            dst_ref=dst,
            send_sem=embed_send.at[offset],
            recv_sem=embed_recv.at[offset],
            device_id={"mp": lax.rem(comm.me + offset, size)},
            device_id_type=pl.DeviceIdType.MESH,
        )

    def embed_step(way):
        now = time_of(way, step)
        value = lax.dot_general(
            da_refs[way][0],
            win_ref[way],
            (((1,), (1,)), ((), ())),
            preferred_element_type=jnp.float32,
        )

        @pl.when(step < WIN // 2)
        def _():
            held_ref[now] = value

        @pl.when(step >= WIN // 2)
        def _():
            both = (value + held_ref[now]).astype(jnp.bfloat16)
            embed_part_ref[now] = both.reshape(size, part, PROJ)
            for offset in range(1, size):
                peer = lax.rem(comm.me + offset, size)
                embed_copy(
                    embed_part_ref.at[now, peer], embed_got_ref.at[comm.me, now], offset
                ).start()

    def embed_finish():
        total = embed_part_ref[:, comm.me].astype(jnp.float32)
        for offset in range(1, size):
            peer = lax.rem(comm.me + size - offset, size)
            embed_copy(embed_got_ref.at[peer], embed_got_ref.at[peer], offset).wait_recv()
            total = total + embed_got_ref[peer].astype(jnp.float32)
        de_ref[...] = total.astype(jnp.bfloat16)
        for offset in range(1, size):
            embed_copy(embed_got_ref.at[comm.me], embed_got_ref.at[comm.me], offset).wait_send()

    @pl.when(step == 0)
    def _():
        cell_ref[...] = jnp.zeros(cell_ref.shape, jnp.float32)
        bias_ref[...] = jnp.zeros(bias_ref.shape, jnp.float32)
        mp_barrier(size)
        for way in range(2):
            stat_step(way, 0, first_cot_ref[way], first_stat_ref[way], None)

    cell_step(0)

    @pl.when(step > 0)
    def _():
        stat_step(1, step, cot1_ref[0], stat1_ref[0], comm.take_sum(1))

    embed_step(0)

    @pl.when(step < WIN - 1)
    def _():
        stat_step(0, step + 1, cot0_ref[0], stat0_ref[0], comm.take_sum(0))

    cell_step(1)
    embed_step(1)

    @pl.when(step == WIN - 1)
    def _():
        embed_finish()


def lstm_backward(size, gates, cprevs, cnews, cots, stats, win, wst, wpr, reset):
    rows = reset.shape[0]
    part = rows // size
    width = win.shape[2]
    units = cprevs[0].shape[2]
    last = WIN - 1
    vmem = pl.BlockSpec(memory_space=pltpu.VMEM)

    def block(shape, index):
        return pl.BlockSpec((1,) + shape, lambda w: (index(w), 0, 0))

    now0 = lambda w: last - w
    now1 = lambda w: w
    next0 = lambda w: jnp.maximum(last - 1 - w, 0)
    ins = []
    for size_of in (width, units, units):
        ins += [block((rows, size_of), now0), block((rows, size_of), now1)]
    ins += [block((part, PROJ), next0), block((part, PROJ), now1)] * 2
    ins += [vmem] * 6
    outs = []
    for size_of, kind in ((width, jnp.bfloat16), (PROJ, jnp.bfloat16)):
        outs += [((rows, size_of), kind, now0), ((rows, size_of), kind, now1)]
    first_cot = jnp.stack([cots[0][last], cots[1][0]])
    first_stat = jnp.stack([stats[0][last], stats[1][0]])
    return pl.pallas_call(
        functools.partial(backward_kernel, size),
        grid=(WIN,),
        in_specs=ins,
        out_specs=[block(shape, index) for shape, kind, index in outs]
        + [pl.BlockSpec((2, 8, width), lambda w: (0, 0, 0)), vmem],
        out_shape=[jax.ShapeDtypeStruct((WIN,) + shape, kind) for shape, kind, index in outs]
        + [
            jax.ShapeDtypeStruct((2, 8, width), jnp.float32),
            jax.ShapeDtypeStruct((WIN, part, PROJ), jnp.bfloat16),
        ],
        scratch_shapes=[
            pltpu.VMEM((2, rows, units), jnp.float32),
            pltpu.VMEM((2, size, part, PROJ), jnp.bfloat16),
            pltpu.VMEM((2, size, part, PROJ), jnp.bfloat16),
            pltpu.VMEM((2, size, part, PROJ), jnp.bfloat16),
        ]
        + [pltpu.SemaphoreType.DMA((2, size))] * 4
        + [
            pltpu.VMEM((WIN, rows, PROJ), jnp.float32),
            pltpu.VMEM((WIN, size, part, PROJ), jnp.bfloat16),
            pltpu.VMEM((size, WIN, part, PROJ), jnp.bfloat16),
        ]
        + [pltpu.SemaphoreType.DMA((size,))] * 2,
        compiler_params=pltpu.CompilerParams(
            collective_id=2, has_side_effects=True, vmem_limit_bytes=56 * 2**20
        ),
    )(*gates, *cprevs, *cnews, *cots, *stats, win, wst, wpr, reset, first_cot, first_stat)


class RingExchange(Exchange):
    def __init__(self, part_ref, sum_ref, all_ref, sems):
        super().__init__(4, part_ref, sum_ref, all_ref, sems)
        self.near = lax.rem(self.me, 2)
        self.me = self.me // 2

    def part_copy(self, way, offset, incoming):
        peer = lax.rem(self.me + (4 - offset if incoming else offset), 4)
        return pltpu.make_async_remote_copy(
            src_ref=self.part_ref.at[way, peer],
            dst_ref=self.sum_ref.at[way, peer if incoming else self.me],
            send_sem=self.part_send.at[way, offset],
            recv_sem=self.part_recv.at[way, offset],
            device_id={"mp": 2 * peer + self.near},
            device_id_type=pl.DeviceIdType.MESH,
        )

    def all_copy(self, way, offset, incoming):
        peer = lax.rem(self.me + (4 - offset if incoming else offset), 4)
        slot = peer if incoming else self.me
        return pltpu.make_async_remote_copy(
            src_ref=self.all_ref.at[way, slot],
            dst_ref=self.all_ref.at[way, slot],
            send_sem=self.all_send.at[way, offset],
            recv_sem=self.all_recv.at[way, offset],
            device_id={"mp": 2 * peer + self.near},
            device_id_type=pl.DeviceIdType.MESH,
        )


def ring_forward_kernel(
    emb_ref,
    win_ref,
    wst_ref,
    wpr_ref,
    bias_ref,
    cell_ref,
    hid_ref,
    reset_ref,
    embt_ref,
    gate_ref,
    cprev_ref,
    cnew_ref,
    low_ref,
    hprev_ref,
    stat_ref,
    out_ref,
    pre_ref,
    state_ref,
    part_ref,
    sum_ref,
    all_ref,
    stage_ref,
    part_send,
    part_recv,
    all_send,
    all_recv,
    out_sem,
    out_send,
    out_recv,
):
    step = pl.program_id(0)
    half_rows = reset_ref.shape[1]
    part = half_rows // 4
    units = wpr_ref.shape[1]
    blocks = units // UNIT_BLOCK
    wide = 4 * UNIT_BLOCK
    comm = RingExchange(part_ref, sum_ref, all_ref, (part_send, part_recv, all_send, all_recv))
    near = comm.near

    def time_of(at):
        return at + near * (WIN - 1 - 2 * at)

    def input_part(at):
        emb = emb_ref[:, :, time_of(at)]
        halves = [emb[:, way].reshape(half_rows, PROJ) for way in range(2)]
        both = jnp.concatenate(halves, axis=0)
        slot = lax.rem(at, 2)
        for owner in range(2):
            for block in range(blocks):
                cols = slice(block * wide, (block + 1) * wide)
                pre_ref[slot, owner, :, cols] = (
                    jnp.dot(both, win_ref[owner, :, cols], preferred_element_type=jnp.float32)
                    + bias_ref[owner, :, cols]
                )

    def out_copies(way, at, incoming):
        slot = lax.rem(at, 2)
        now = time_of(at)
        src = stage_ref.at[way, slot]
        other = WIN - 1 - now if incoming else now
        return (
            pltpu.make_async_copy(src, out_ref.at[near, now, :, way], out_sem.at[way, slot]),
            pltpu.make_async_remote_copy(
                src_ref=src,
                dst_ref=out_ref.at[1 - near if incoming else near, other, :, way],
                send_sem=out_send.at[way, slot],
                recv_sem=out_recv.at[way, at],
                device_id={"mp": 2 * comm.me + 1 - near},
                device_id_type=pl.DeviceIdType.MESH,
            ),
        )

    def emit_hidden(way):
        at = step - 1

        @pl.when(at >= 2)
        def _():
            local, remote = out_copies(way, at - 2, False)
            local.wait()
            remote.wait_send()

        stage_ref[way, lax.rem(at, 2)] = all_ref[way]
        for copy in out_copies(way, at, False):
            copy.start()

    def cell_step(way):
        now = time_of(step)
        keep = jnp.where(reset_ref[way] - near == now, 0.0, 1.0)
        keep_low = jnp.concatenate([keep.astype(jnp.bfloat16)] * (PROJ // UNIT_BLOCK), axis=1)
        hidden_prev = all_ref[way].reshape(half_rows, PROJ) * keep_low
        hprev_ref[0, way] = hidden_prev
        embt_ref[0, way] = emb_ref[:, way, now].reshape(half_rows, PROJ)
        slot = lax.rem(step, 2)
        rows = slice(way * half_rows, (way + 1) * half_rows)
        partial = None
        for owner in range(2):
            for block in range(blocks):
                cols = slice(block * wide, (block + 1) * wide)
                unit = slice(block * UNIT_BLOCK, (block + 1) * UNIT_BLOCK)
                spot = slice(
                    owner * units + block * UNIT_BLOCK, owner * units + (block + 1) * UNIT_BLOCK
                )
                place = slice((owner * blocks + block) * wide, (owner * blocks + block + 1) * wide)
                pre = pre_ref[slot, owner, rows, cols] + jnp.dot(
                    hidden_prev, wst_ref[owner, :, cols], preferred_element_type=jnp.float32
                )
                gate_in = sigmoid_of(pre[:, :UNIT_BLOCK])
                gate_forget = sigmoid_of(pre[:, UNIT_BLOCK : 2 * UNIT_BLOCK])
                gate_cand = jnp.tanh(pre[:, 2 * UNIT_BLOCK : 3 * UNIT_BLOCK])
                gate_out = sigmoid_of(pre[:, 3 * UNIT_BLOCK :])
                cell_prev = state_ref[way, owner, :, unit] * keep
                cell_new = CLIP * jnp.tanh(
                    (gate_forget * cell_prev + gate_in * gate_cand) * (1.0 / CLIP)
                )
                gate_ref[0, way, :, place] = jnp.concatenate(
                    [gate_in, gate_forget, gate_cand, gate_out], axis=1
                )
                cprev_ref[0, way, :, spot] = cell_prev
                cnew_ref[0, way, :, spot] = cell_new
                state_ref[way, owner, :, unit] = cell_new
                low_ref[0, way, :, spot] = (gate_out * jnp.tanh(cell_new)).astype(jnp.bfloat16)
            term = jnp.dot(
                low_ref[0, way, :, owner * units : (owner + 1) * units],
                wpr_ref[owner],
                preferred_element_type=jnp.float32,
            )
            partial = term if partial is None else partial + term
        part_ref[way] = partial.astype(jnp.bfloat16).reshape(4, part, PROJ)
        comm.send_parts(way)

    def close_step(way, at):
        total = comm.take_sum(way)
        stat_ref[way, at] = total
        comm.send_all(way, (CLIP * jnp.tanh(total * (1.0 / CLIP))).astype(jnp.bfloat16))

    @pl.when(step == 0)
    def _():
        for way in range(2):
            all_ref[way] = hid_ref[way]
            state_ref[way] = cell_ref[way]
        input_part(jnp.int32(0))
        mp_barrier(8)

    @pl.when(step > 0)
    def _():
        comm.wait_all(0)
        emit_hidden(0)

    @pl.when(step < WIN)
    def _():
        cell_step(0)

    @pl.when(step > 0)
    def _():
        close_step(1, step - 1)

    @pl.when(step < WIN)
    def _():
        @pl.when(step < WIN - 1)
        def _():
            input_part(step + 1)

        close_step(0, step)

    @pl.when(step > 0)
    def _():
        comm.wait_all(1)
        emit_hidden(1)

    @pl.when(step < WIN)
    def _():
        cell_step(1)

    @pl.when(step == WIN)
    def _():
        for way in range(2):
            for at in (WIN - 2, WIN - 1):
                local, remote = out_copies(way, jnp.int32(at), False)
                local.wait()
                remote.wait_send()

            @pl.loop(0, WIN)
            def _(at):
                out_copies(way, at, True)[1].wait_recv()


def ring_forward(emb, win, wst, wpr, bias, cell, hid, reset):
    half_rows = reset.shape[1]
    part = half_rows // 4
    gates = 2 * win.shape[2]
    units = 2 * wpr.shape[1]
    last = WIN - 1
    vmem = pl.BlockSpec(memory_space=pltpu.VMEM)
    bf16, f32 = jnp.bfloat16, jnp.float32
    dma = pltpu.SemaphoreType.DMA
    widths = (
        (PROJ, bf16),
        (gates, f32),
        (units, f32),
        (units, f32),
        (units, bf16),
        (PROJ, bf16),
    )
    return pl.pallas_call(
        ring_forward_kernel,
        grid=(WIN + 1,),
        in_specs=[vmem] * 8,
        out_specs=[
            pl.BlockSpec((1, 2, half_rows, width), lambda w: (jnp.minimum(w, last), 0, 0, 0))
            for width, kind in widths
        ]
        + [vmem, pl.BlockSpec(memory_space=pl.ANY)],
        out_shape=[
            jax.ShapeDtypeStruct((WIN, 2, half_rows, width), kind) for width, kind in widths
        ]
        + [
            jax.ShapeDtypeStruct((2, WIN, part, PROJ), f32),
            jax.ShapeDtypeStruct((2, WIN, 4, 2, part, PROJ), bf16),
        ],
        scratch_shapes=[
            pltpu.VMEM((2, 2, 2 * half_rows, gates // 2), f32),
            pltpu.VMEM((2, 2, half_rows, units // 2), f32),
            pltpu.VMEM((2, 4, part, PROJ), bf16),
            pltpu.VMEM((2, 4, part, PROJ), bf16),
            pltpu.VMEM((2, 4, part, PROJ), bf16),
            pltpu.VMEM((2, 2, 4, part, PROJ), bf16),
        ]
        + [dma((2, 4))] * 4
        + [dma((2, 2))] * 2
        + [dma((2, WIN))],
        compiler_params=pltpu.CompilerParams(
            collective_id=5, has_side_effects=True, vmem_limit_bytes=56 * 2**20
        ),
    )(emb, win, wst, wpr, bias, cell, hid, reset)


def ring_backward_kernel(
    gate_ref,
    cprev_ref,
    cnew_ref,
    cot_ref,
    stat_ref,
    win_ref,
    wst_ref,
    wpr_ref,
    reset_ref,
    da_ref,
    ds_ref,
    bias_ref,
    de_ref,
    cell_ref,
    part_ref,
    sum_ref,
    all_ref,
    part_send,
    part_recv,
    all_send,
    all_recv,
    embed_part_ref,
    embed_got_ref,
    embed_send,
    embed_recv,
):
    step = pl.program_id(0)
    half_rows = reset_ref.shape[1]
    part = half_rows // 4
    units = wpr_ref.shape[1]
    blocks = units // UNIT_BLOCK
    wide = 4 * UNIT_BLOCK
    comm = RingExchange(part_ref, sum_ref, all_ref, (part_send, part_recv, all_send, all_recv))
    near = comm.near
    device = lax.axis_index("mp")

    def scan_of(at):
        return WIN - 1 - at

    def time_of(at):
        back = scan_of(at)
        return back + near * (WIN - 1 - 2 * back)

    def stat_step(way, at, total):
        grad = cot_ref[way, time_of(at)].astype(jnp.float32)
        if total is not None:
            own = reset_ref[way, pl.ds(comm.me * part, part), :] - near
            keep = jnp.where(own == time_of(at - 1), 0.0, 1.0)
            grad = grad + total * jnp.concatenate([keep] * (PROJ // UNIT_BLOCK), axis=1)
        slope = jnp.tanh(stat_ref[way, scan_of(at)] * (1.0 / CLIP))
        comm.send_all(way, (grad * (1.0 - slope * slope)).astype(jnp.bfloat16))

    def cell_step(way):
        comm.wait_all(way)
        keep = jnp.where(reset_ref[way] - near == time_of(step), 0.0, 1.0)
        grad_stat = all_ref[way].reshape(half_rows, PROJ)
        ds_ref[0, way] = grad_stat
        for owner in range(2):
            for block in range(blocks):
                unit = slice(block * UNIT_BLOCK, (block + 1) * UNIT_BLOCK)
                spot = slice(
                    owner * units + block * UNIT_BLOCK, owner * units + (block + 1) * UNIT_BLOCK
                )
                place = slice((owner * blocks + block) * wide, (owner * blocks + block + 1) * wide)
                grad_out = lax.dot_general(
                    grad_stat,
                    wpr_ref[owner, unit, :],
                    (((1,), (1,)), ((), ())),
                    preferred_element_type=jnp.float32,
                )
                gates = gate_ref[0, way, :, place]
                gate_in = gates[:, :UNIT_BLOCK]
                gate_forget = gates[:, UNIT_BLOCK : 2 * UNIT_BLOCK]
                gate_cand = gates[:, 2 * UNIT_BLOCK : 3 * UNIT_BLOCK]
                gate_out = gates[:, 3 * UNIT_BLOCK :]
                cell_prev = cprev_ref[0, way, :, spot]
                cell_new = cnew_ref[0, way, :, spot]
                tanh_cell = jnp.tanh(cell_new)
                grad_total = (
                    grad_out * gate_out * (1.0 - tanh_cell * tanh_cell) + cell_ref[way, :, spot]
                )
                scaled = cell_new * (1.0 / CLIP)
                grad_inner = grad_total * (1.0 - scaled * scaled)
                cell_ref[way, :, spot] = grad_inner * gate_forget * keep
                grad_pre = jnp.concatenate(
                    [
                        grad_inner * gate_cand * gate_in * (1.0 - gate_in),
                        grad_inner * cell_prev * gate_forget * (1.0 - gate_forget),
                        grad_inner * gate_in * (1.0 - gate_cand * gate_cand),
                        grad_out * tanh_cell * gate_out * (1.0 - gate_out),
                    ],
                    axis=1,
                ).astype(jnp.bfloat16)
                da_ref[0, way, :, place] = grad_pre
                bias_ref[:, place] += jnp.sum(
                    grad_pre.astype(jnp.float32).reshape(half_rows // 8, 8, wide), axis=0
                )

        @pl.when(step < WIN - 1)
        def _():
            partial = None
            for owner in range(2):
                span = slice(owner * blocks * wide, (owner + 1) * blocks * wide)
                term = lax.dot_general(
                    da_ref[0, way, :, span],
                    wst_ref[owner],
                    (((1,), (1,)), ((), ())),
                    preferred_element_type=jnp.float32,
                )
                partial = term if partial is None else partial + term
            part_ref[way] = partial.astype(jnp.bfloat16).reshape(4, part, PROJ)
            comm.send_parts(way)

    def embed_copy(src, dst, offset):
        return pltpu.make_async_remote_copy(
            src_ref=src,
            dst_ref=dst,
            send_sem=embed_send.at[offset],
            recv_sem=embed_recv.at[offset],
            device_id={"mp": lax.rem(device + offset, 8)},
            device_id_type=pl.DeviceIdType.MESH,
        )

    def embed_step():
        now = time_of(step)
        total = None
        for owner in range(2):
            span = slice(owner * blocks * wide, (owner + 1) * blocks * wide)
            both = jnp.concatenate([da_ref[0, 0, :, span], da_ref[0, 1, :, span]], axis=0)
            term = lax.dot_general(
                both,
                win_ref[owner],
                (((1,), (1,)), ((), ())),
                preferred_element_type=jnp.float32,
            )
            total = term if total is None else total + term
        total = total.astype(jnp.bfloat16)
        for way in range(2):
            embed_part_ref[now, way] = total[way * half_rows : (way + 1) * half_rows].reshape(
                4, part, PROJ
            )
        for offset in range(1, 8):
            peer = lax.rem(device + offset, 8)
            embed_copy(
                embed_part_ref.at[now, lax.rem(peer, 2), peer // 2],
                embed_got_ref.at[device, now],
                offset,
            ).start()

    def embed_finish():
        total = embed_part_ref[:, near, comm.me].astype(jnp.float32)
        for offset in range(1, 8):
            peer = lax.rem(device + 8 - offset, 8)
            embed_copy(embed_got_ref.at[peer], embed_got_ref.at[peer], offset).wait_recv()
            total = total + embed_got_ref[peer].astype(jnp.float32)
        de_ref[...] = total.astype(jnp.bfloat16)
        for offset in range(1, 8):
            embed_copy(embed_got_ref.at[device], embed_got_ref.at[device], offset).wait_send()

    @pl.when(step == 0)
    def _():
        cell_ref[...] = jnp.zeros(cell_ref.shape, jnp.float32)
        bias_ref[...] = jnp.zeros(bias_ref.shape, jnp.float32)
        mp_barrier(8)
        for way in range(2):
            stat_step(way, 0, None)

    cell_step(0)

    @pl.when(step > 0)
    def _():
        stat_step(1, step, comm.take_sum(1))

    @pl.when(step < WIN - 1)
    def _():
        stat_step(0, step + 1, comm.take_sum(0))

    cell_step(1)
    embed_step()

    @pl.when(step == WIN - 1)
    def _():
        embed_finish()


def ring_backward(gates, cprevs, cnews, cots, stats, win, wst, wpr, reset):
    half_rows = reset.shape[1]
    part = half_rows // 4
    width = 2 * win.shape[2]
    units = 2 * wpr.shape[1]
    last = WIN - 1
    vmem = pl.BlockSpec(memory_space=pltpu.VMEM)
    bf16, f32 = jnp.bfloat16, jnp.float32
    dma = pltpu.SemaphoreType.DMA

    def block(size):
        return pl.BlockSpec((1, 2, half_rows, size), lambda w: (last - w, 0, 0, 0))

    return pl.pallas_call(
        ring_backward_kernel,
        grid=(WIN,),
        in_specs=[block(width), block(units), block(units)] + [vmem] * 6,
        out_specs=[block(width), block(PROJ), vmem, vmem],
        out_shape=[
            jax.ShapeDtypeStruct((WIN, 2, half_rows, width), bf16),
            jax.ShapeDtypeStruct((WIN, 2, half_rows, PROJ), bf16),
            jax.ShapeDtypeStruct((8, width), f32),
            jax.ShapeDtypeStruct((WIN, part, PROJ), bf16),
        ],
        scratch_shapes=[
            pltpu.VMEM((2, half_rows, units), f32),
            pltpu.VMEM((2, 4, part, PROJ), bf16),
            pltpu.VMEM((2, 4, part, PROJ), bf16),
            pltpu.VMEM((2, 4, part, PROJ), bf16),
        ]
        + [dma((2, 4))] * 4
        + [
            pltpu.VMEM((WIN, 2, 4, part, PROJ), bf16),
            pltpu.VMEM((8, WIN, part, PROJ), bf16),
        ]
        + [dma((8,))] * 2,
        compiler_params=pltpu.CompilerParams(
            collective_id=6, has_side_effects=True, vmem_limit_bytes=56 * 2**20
        ),
    )(gates, cprevs, cnews, cots, stats, win, wst, wpr, reset)


SHIFTS = 8
GROUP = SHIFTS * CDIM
FBLOCK = 256


def position_bound(first, width, taps):
    index = first + lax.broadcasted_iota(jnp.int32, (1, width), 1)
    bound = jnp.full((1, width), CHARS - 1, jnp.int32)
    for exponent in range(taps - 1):
        bound = bound - (index >= (FILTERS // 64) * (1 << exponent)).astype(jnp.int32)
    return bound


def group_counts():
    full = (CHARS - SHIFTS) // SHIFTS + 1
    return full, CHARS - full * SHIFTS


def windows(vec_ref, count):
    tokens = vec_ref.shape[1]
    low = vec_ref[0:count].reshape(count * tokens, GROUP)
    high = vec_ref[1 : count + 1].reshape(count * tokens, GROUP)
    return jnp.concatenate([low, high], axis=1)


def char_vectors(ids_ref, table_ref, vec_ref):
    groups, tokens, _ = vec_ref.shape
    vocab = table_ref.shape[1]
    for group in range(groups):
        acc = jnp.zeros((tokens, GROUP), jnp.float32)
        for shift in range(SHIFTS):
            place = group * SHIFTS + shift
            if place < CHARS:
                column = ids_ref[:, place : place + 1]
                hot = column == lax.broadcasted_iota(jnp.int32, (tokens, vocab), 1)
                acc = acc + jnp.dot(
                    jnp.where(hot, 1.0, 0.0).astype(jnp.bfloat16),
                    table_ref[shift],
                    preferred_element_type=jnp.float32,
                )
        vec_ref[group] = acc.astype(jnp.bfloat16)


def conv_block(block, cols, vec_ref, weight_ref, total_ref):
    _, tokens, _ = vec_ref.shape
    full, extra = group_counts()
    bound = position_bound(block * FBLOCK, FBLOCK, TAPS)
    left = windows(vec_ref, full)
    total = jnp.zeros((tokens, FBLOCK), jnp.float32)
    for shift in range(SHIFTS):
        out = jnp.dot(left, weight_ref[shift, :, cols], preferred_element_type=jnp.float32)
        values = jnp.exp(out).reshape(full, tokens, FBLOCK)
        for group in range(full):
            place = group * SHIFTS + shift
            term = values[group]
            if place > CHARS - TAPS:
                term = jnp.where(bound >= place, term, 0.0)
            total = total + term
    total_ref[:, cols] = total

    @pl.when(block == 0)
    def _():
        for shift in range(extra):
            out = jnp.dot(
                vec_ref[full], weight_ref[shift, :GROUP, cols], preferred_element_type=jnp.float32
            )
            total_ref[:, cols] += jnp.where(
                bound >= full * SHIFTS + shift, jnp.exp(out), 0.0
            )


def conv_forward_kernel(ids_ref, table_ref, weight_ref, total_ref, vec_ref):
    block = pl.program_id(0)

    @pl.when(block == 0)
    def _():
        char_vectors(ids_ref, table_ref, vec_ref)

    conv_block(block, slice(None), vec_ref, weight_ref, total_ref)


def conv_forward(ids, table_shift, weights):
    tokens = ids.shape[0]
    groups = -(-CHARS // SHIFTS)
    vocab = table_shift.shape[1]
    return pl.pallas_call(
        conv_forward_kernel,
        grid=(FILTERS // FBLOCK,),
        in_specs=[
            pl.BlockSpec((tokens, CHARS), lambda f: (0, 0)),
            pl.BlockSpec((SHIFTS, vocab, GROUP), lambda f: (0, 0, 0)),
            pl.BlockSpec((SHIFTS, 2 * GROUP, FBLOCK), lambda f: (0, 0, f)),
        ],
        out_specs=[
            pl.BlockSpec((tokens, FBLOCK), lambda f: (0, f)),
            pl.BlockSpec((groups, tokens, GROUP), lambda f: (0, 0, 0)),
        ],
        out_shape=[
            jax.ShapeDtypeStruct((tokens, FILTERS), jnp.float32),
            jax.ShapeDtypeStruct((groups, tokens, GROUP), jnp.bfloat16),
        ],
        compiler_params=pltpu.CompilerParams(vmem_limit_bytes=56 * 2**20),
        cost_estimate=pl.CostEstimate(
            flops=2 * tokens * CHARS * 256 * FILTERS,
            bytes_accessed=12 * 2**20,
            transcendentals=tokens * CHARS * FILTERS,
        ),
    )(ids, table_shift, weights)


def conv_shift_step(
    shift, vec_ref, turned_ref, turned_extra_ref, ratio_ref, weight_ref, grad_ref, low_ref, char_ref, held_ref
):
    groups, tokens, _ = vec_ref.shape
    full, extra = group_counts()
    left = windows(vec_ref, full)
    own_rows = pl.ds(pl.multiple_of(shift * CDIM, CDIM), TAPS * CDIM)

    @pl.when(shift == 0)
    def _():
        grad_ref[...] = jnp.zeros(grad_ref.shape, jnp.float32)
        char_ref[...] = jnp.zeros(char_ref.shape, jnp.float32)

    @pl.loop(0, FILTERS // FBLOCK)
    def _(block):
        cols = pl.ds(pl.multiple_of(block * FBLOCK, FBLOCK), FBLOCK)
        bound = position_bound(block * FBLOCK, FBLOCK, TAPS)
        ratio = ratio_ref[:, cols]
        out = jnp.dot(left, weight_ref[0, :, cols], preferred_element_type=jnp.float32)
        values = jnp.exp(out).reshape(full, tokens, FBLOCK)
        for group in range(full):
            term = values[group] * ratio
            if (group + 1) * SHIFTS - 1 > CHARS - TAPS:
                term = jnp.where(bound >= group * SHIFTS + shift, term, 0.0)
            low_ref[pl.ds(group * tokens, tokens), cols] = term.astype(jnp.bfloat16)
        held_ref[...] = jnp.dot(
            turned_ref[...], low_ref[:, cols], preferred_element_type=jnp.float32
        )
        grad_ref[:, cols] += held_ref[own_rows, :]

    back = lax.dot_general(
        low_ref[...],
        weight_ref[0],
        (((1,), (1,)), ((), ())),
        preferred_element_type=jnp.float32,
    ).reshape(full, tokens, 2 * GROUP)
    for group in range(full):
        char_ref[group] += back[group, :, :GROUP]
        char_ref[group + 1] += back[group, :, GROUP:]

    @pl.when(shift < extra)
    def _():
        cols = slice(0, FBLOCK)
        bound = position_bound(0, FBLOCK, TAPS)
        out = jnp.dot(
            vec_ref[full], weight_ref[0, :GROUP, cols], preferred_element_type=jnp.float32
        )
        term = jnp.exp(out) * ratio_ref[:, cols]
        term = jnp.where(bound >= full * SHIFTS + shift, term, 0.0).astype(jnp.bfloat16)
        held_ref[...] = jnp.concatenate(
            [
                jnp.dot(turned_extra_ref[...], term, preferred_element_type=jnp.float32),
                jnp.zeros((GROUP, FBLOCK), jnp.float32),
            ],
            axis=0,
        )
        grad_ref[:, cols] += held_ref[own_rows, :]
        char_ref[full] += lax.dot_general(
            term,
            weight_ref[0, :GROUP, cols],
            (((1,), (1,)), ((), ())),
            preferred_element_type=jnp.float32,
        )


def table_gradient(hot_ref, hot_extra_ref, char_ref, vocab):
    tokens = char_ref.shape[1]
    full, extra = group_counts()
    lane = lax.broadcasted_iota(jnp.int32, (vocab, GROUP), 1) // CDIM

    def split(value):
        high = value.astype(jnp.bfloat16)
        rest = (value - high.astype(jnp.float32)).astype(jnp.bfloat16)
        return jnp.concatenate([high, rest], axis=1)

    main = split(char_ref[0:full].reshape(full * tokens, GROUP))
    last = split(char_ref[full])
    acc = jnp.zeros((vocab, GROUP), jnp.float32)
    for at in range(SHIFTS):
        row = hot_ref[at : at + 1, :]
        hot = row == lax.broadcasted_iota(jnp.int32, (vocab, full * tokens), 0)
        out = jnp.dot(
            jnp.where(hot, 1.0, 0.0).astype(jnp.bfloat16),
            main,
            preferred_element_type=jnp.float32,
        )
        if at < extra:
            row = hot_extra_ref[at : at + 1, :]
            hot = row == lax.broadcasted_iota(jnp.int32, (vocab, tokens), 0)
            out = out + jnp.dot(
                jnp.where(hot, 1.0, 0.0).astype(jnp.bfloat16),
                last,
                preferred_element_type=jnp.float32,
            )
        acc = jnp.where(lane == at, out[:, :GROUP] + out[:, GROUP:], acc)
    return acc


def conv_backward_kernel(
    hot_ref,
    hot_extra_ref,
    vec_ref,
    turned_ref,
    turned_extra_ref,
    ratio_ref,
    weight_ref,
    grad_ref,
    table_ref,
    low_ref,
    char_ref,
    held_ref,
):
    shift = pl.program_id(0)
    conv_shift_step(
        shift, vec_ref, turned_ref, turned_extra_ref, ratio_ref, weight_ref, grad_ref, low_ref, char_ref, held_ref
    )

    @pl.when(shift == SHIFTS - 1)
    def _():
        table_ref[...] = table_gradient(hot_ref, hot_extra_ref, char_ref, table_ref.shape[0])


def conv_operands(ids, vectors):
    groups, tokens, _ = vectors.shape
    full, extra = group_counts()
    turned = jnp.transpose(vectors, (0, 2, 1))
    pieces = [
        jnp.transpose(turned[half : half + full], (1, 0, 2)).reshape(GROUP, full * tokens)
        for half in range(2)
    ]
    ids_turned = ids.T
    hot_main = jnp.transpose(ids_turned[: full * SHIFTS].reshape(full, SHIFTS, tokens), (1, 0, 2))
    hot_main = hot_main.reshape(SHIFTS, full * tokens)
    hot_extra = ids_turned[full * SHIFTS :]
    return hot_main, hot_extra, vectors, jnp.concatenate(pieces, axis=0), turned[full]


def conv_backward(ids, vectors, ratio, weights):
    groups, tokens, _ = vectors.shape
    full, _ = group_counts()
    vocab = -(-VOCAB // 8) * 8
    grad, table = pl.pallas_call(
        conv_backward_kernel,
        grid=(SHIFTS,),
        in_specs=[pl.BlockSpec(memory_space=pltpu.VMEM)] * 6
        + [pl.BlockSpec((1, 2 * GROUP, FILTERS), lambda s: (s, 0, 0))],
        out_specs=[
            pl.BlockSpec((TAPS * CDIM, FILTERS), lambda s: (0, 0)),
            pl.BlockSpec((vocab, GROUP), lambda s: (0, 0)),
        ],
        out_shape=[
            jax.ShapeDtypeStruct((TAPS * CDIM, FILTERS), jnp.float32),
            jax.ShapeDtypeStruct((vocab, GROUP), jnp.float32),
        ],
        scratch_shapes=[
            pltpu.VMEM((full * tokens, FILTERS), jnp.bfloat16),
            pltpu.VMEM((groups, tokens, GROUP), jnp.float32),
            pltpu.VMEM((2 * GROUP, FBLOCK), jnp.float32),
        ],
        compiler_params=pltpu.CompilerParams(vmem_limit_bytes=58 * 2**20),
        cost_estimate=pl.CostEstimate(
            flops=6 * tokens * CHARS * 256 * FILTERS,
            bytes_accessed=16 * 2**20,
            transcendentals=tokens * CHARS * FILTERS,
        ),
    )(*conv_operands(ids, vectors), ratio, weights)
    table = table.reshape(vocab, SHIFTS, CDIM).sum(axis=1)[:VOCAB]
    return grad, table


MESH = pl.DeviceIdType.MESH
CHUNK_ROWS = 16
SLACK = 2
BEATS = 2
AHEAD = 2
BIAS_ROWS = 32


def tail_kernel(
    chunks,
    hot_ref,
    hot_extra_ref,
    vec_ref,
    turned_ref,
    turned_extra_ref,
    ratio_ref,
    weight_ref,
    part1_ref,
    part0_ref,
    part2_ref,
    small_ref,
    high_sum_ref,
    proj_sum_ref,
    conv_ref,
    table_ref,
    grad_ref,
    low_ref,
    char_ref,
    held_ref,
    own_ref,
    got_y_ref,
    got_x_ref,
    got_z_ref,
    all_z_ref,
    all_x_ref,
    wide_ref,
    conv_acc_ref,
    conv_got_ref,
    conv_two_ref,
    conv_in_ref,
    table_acc_ref,
    table_got_ref,
    load_sem,
    store_sem,
    y_send,
    y_recv,
    x_send,
    x_recv,
    z_send,
    z_recv,
    g_send,
    g_recv,
    h_send,
    h_recv,
    small_send,
    small_recv,
):
    tick = pl.program_id(0)
    dp = lax.axis_index("dp")
    mp = lax.axis_index("mp")
    core, high = lax.rem(dp, 2), dp // 2
    near, ring = lax.rem(mp, 2), mp // 2
    per_layer = part1_ref.shape[1]
    width = FILTERS * 2
    quarter = width // 4
    parts = (part1_ref, part0_ref, part2_ref)
    vocab = table_ref.shape[0] - small_ref.shape[0]
    core_peer = {"dp": dp + 1 - 2 * core, "mp": mp}
    high_peer = {"dp": dp + 2 - 4 * high, "mp": mp}
    near_peer = {"dp": dp, "mp": mp + 1 - 2 * near}

    def ring_index(offset):
        return lax.rem(ring + offset, 4)

    def ring_peer(offset):
        return {"dp": dp, "mp": 2 * ring_index(offset) + near}

    def remote(src, dst, send, recv, peer):
        return pltpu.make_async_remote_copy(
            src_ref=src, dst_ref=dst, send_sem=send, recv_sem=recv, device_id=peer, device_id_type=MESH
        )

    def y_copy(part, chunk, row):
        return remote(
            part.at[1 - high, row], got_y_ref.at[chunk], y_send.at[chunk], y_recv.at[chunk], high_peer
        )

    def y_start(chunk):
        for layer, part in enumerate(parts):

            @pl.when(chunk // per_layer == layer)
            def _():
                y_copy(part, chunk, chunk - layer * per_layer).start()

    def load(chunk, act):
        slot = lax.rem(chunk, 2)
        for layer, part in enumerate(parts):

            @pl.when(chunk // per_layer == layer)
            def _():
                copy = pltpu.make_async_copy(
                    part.at[high, chunk - layer * per_layer], own_ref.at[slot], load_sem.at[slot]
                )
                getattr(copy, act)()

    def x_copy(chunk):
        return remote(
            got_y_ref.at[chunk, 1 - near],
            got_x_ref.at[chunk],
            x_send.at[chunk],
            x_recv.at[chunk],
            near_peer,
        )

    def columns(index):
        return pl.ds(pl.multiple_of(index * quarter, quarter), quarter)

    def z_copy(chunk, offset):
        return remote(
            got_x_ref.at[chunk, :, columns(ring_index(offset))],
            got_z_ref.at[chunk, offset - 1],
            z_send.at[chunk, offset - 1],
            z_recv.at[chunk, offset - 1],
            ring_peer(offset),
        )

    def g_copy(chunk, offset, incoming):
        cols = columns(ring_index(4 - offset) if incoming else ring)
        return remote(
            all_z_ref.at[chunk, :, cols],
            all_z_ref.at[chunk, :, cols],
            g_send.at[chunk, offset - 1],
            g_recv.at[chunk, offset - 1],
            ring_peer(offset),
        )

    def h_copy(chunk):
        return remote(
            all_z_ref.at[chunk], all_x_ref.at[chunk], h_send.at[chunk], h_recv.at[chunk], near_peer
        )

    def store(chunk):
        slot = lax.rem(chunk, 2)
        return wide_ref.at[slot], store_sem.at[slot]

    def store_act(chunk, act):
        src, sem = store(chunk)
        layer, row = chunk // per_layer, lax.rem(chunk, per_layer)

        @pl.when(layer < 2)
        def _():
            getattr(pltpu.make_async_copy(src, high_sum_ref.at[1 - layer, row], sem), act)()

        @pl.when(layer == 2)
        def _():
            getattr(pltpu.make_async_copy(src, proj_sum_ref.at[row], sem), act)()

    def when_chunk(chunk, body):
        @pl.when(jnp.logical_and(chunk >= 0, chunk < chunks))
        def _():
            body(chunk)

    def do_y(chunk):
        y_copy(part1_ref, chunk, 0).wait_recv()
        load(chunk, "wait")
        slot = lax.rem(chunk, 2)
        for half in range(2):
            got_y_ref[chunk, half] = (
                got_y_ref[chunk, half].astype(jnp.float32) + own_ref[slot, half].astype(jnp.float32)
            ).astype(jnp.bfloat16)
        x_copy(chunk).start()

        @pl.when(chunk + AHEAD < chunks)
        def _():
            y_start(chunk + AHEAD)

        @pl.when(chunk + 2 < chunks)
        def _():
            load(chunk + 2, "start")

    def do_x(chunk):
        x_copy(chunk).wait_recv()
        got_x_ref[chunk] = (
            got_x_ref[chunk].astype(jnp.float32) + got_y_ref[chunk, near].astype(jnp.float32)
        ).astype(jnp.bfloat16)
        for offset in range(1, 4):
            z_copy(chunk, offset).start()

    def do_z(chunk):
        cols = columns(ring)
        total = got_x_ref[chunk, :, cols].astype(jnp.float32)
        for offset in range(1, 4):
            z_copy(chunk, offset).wait_recv()
            total = total + got_z_ref[chunk, offset - 1].astype(jnp.float32)
        all_z_ref[chunk, :, cols] = total.astype(jnp.bfloat16)
        for offset in range(1, 4):
            g_copy(chunk, offset, False).start()

    def do_g(chunk):
        for offset in range(1, 4):
            g_copy(chunk, offset, True).wait_recv()
        h_copy(chunk).start()

    def do_h(chunk):
        h_copy(chunk).wait_recv()

        @pl.when(chunk >= 2)
        def _():
            store_act(chunk - 2, "wait")

        slot = lax.rem(chunk, 2)
        wide_ref[slot, near] = all_z_ref[chunk]
        wide_ref[slot, 1 - near] = all_x_ref[chunk]
        store_act(chunk, "start")

    def small_copies(stage):
        if stage == 0:
            copies = [
                remote(
                    conv_two_ref.at[1, y],
                    conv_in_ref.at[y],
                    small_send.at[0, y],
                    small_recv.at[0, y],
                    core_peer,
                )
                for y in range(2)
            ]
            peer = core_peer
        else:
            if stage == 1:
                src = conv_two_ref.at[0, 1 - high]
                peer = high_peer
            else:
                src = conv_acc_ref.at[stage - 2]
                bit = 1 << (stage - 2)
                flip = lax.rem(mp // bit, 2)
                peer = {"dp": dp, "mp": mp + bit - 2 * bit * flip}
            copies = [
                remote(
                    src,
                    conv_got_ref.at[stage - 1],
                    small_send.at[stage, 0],
                    small_recv.at[stage, 0],
                    peer,
                )
            ]
        count = table_ref.shape[0] - (BIAS_ROWS if stage > 1 else 0)
        copies.append(
            remote(
                table_acc_ref.at[stage, pl.ds(0, count)],
                table_got_ref.at[stage, pl.ds(0, count)],
                small_send.at[stage, 2],
                small_recv.at[stage, 2],
                peer,
            )
        )
        return copies

    def small_start(stage):
        for copy in small_copies(stage):
            copy.start()

    def small_finish(stage):
        for copy in small_copies(stage):
            copy.wait()
        count = table_ref.shape[0] - (BIAS_ROWS if stage > 1 else 0)
        total = table_acc_ref[stage, :count] + table_got_ref[stage, :count]
        if stage == 1:
            table_ref[count - BIAS_ROWS :] = total[count - BIAS_ROWS :]
        if stage < 4:
            table_acc_ref[stage + 1, :count] = total
        else:
            table_ref[:count] = total
        if stage == 0:
            for y in range(2):
                conv_two_ref[0, y] = conv_two_ref[0, y] + conv_in_ref[y]
        elif stage == 1:
            conv_acc_ref[0] = conv_two_ref[0, high] + conv_got_ref[0]
        else:
            value = conv_acc_ref[stage - 2] + conv_got_ref[stage - 1]
            if stage < 4:
                conv_acc_ref[stage - 1] = value
            else:
                conv_ref[...] = value

    @pl.when(tick == 0)
    def _():
        barrier = pltpu.get_barrier_semaphore()
        for peer in [core_peer, high_peer, near_peer] + [ring_peer(offset) for offset in (1, 2, 3)]:
            pl.semaphore_signal(barrier, inc=1, device_id=peer, device_id_type=MESH)
        pl.semaphore_wait(barrier, 6)

        for chunk in range(AHEAD):
            y_start(jnp.int32(chunk))

        load(jnp.int32(0), "start")
        load(jnp.int32(1), "start")

    @pl.when(tick < SHIFTS)
    def _():
        conv_shift_step(
            tick,
            vec_ref,
            turned_ref,
            turned_extra_ref,
            ratio_ref,
            weight_ref,
            grad_ref,
            low_ref,
            char_ref,
            held_ref,
        )

    @pl.when(tick == SHIFTS - 1)
    def _():
        table_acc_ref[0, :vocab] = table_gradient(hot_ref, hot_extra_ref, char_ref, vocab)
        table_acc_ref[0, vocab:] = small_ref[...]
        span = FILTERS // 4
        for y in range(2):
            mine = pl.ds(pl.multiple_of((2 * y + core) * span, span), span)
            theirs = pl.ds(pl.multiple_of((2 * y + 1 - core) * span, span), span)
            conv_two_ref[0, y] = grad_ref[:, mine]
            conv_two_ref[1, y] = grad_ref[:, theirs]
        small_start(0)

    for stage in range(5):

        @pl.when(tick == SHIFTS + stage)
        def _():
            small_finish(stage)
            if stage < 4:
                small_start(stage + 1)

    for beat in range(BEATS):
        at = tick * BEATS + beat
        when_chunk(at, do_y)
        when_chunk(at - SLACK, do_x)
        when_chunk(at - 2 * SLACK, do_z)
        when_chunk(at - 3 * SLACK, do_g)
        when_chunk(at - 4 * SLACK, do_h)

    @pl.when(tick == pl.num_programs(0) - 1)
    def _():
        for chunk in (chunks - 2, chunks - 1):
            store_act(jnp.int32(chunk), "wait")

        @pl.loop(0, chunks)
        def _(chunk):
            y_copy(part1_ref, chunk, 0).wait_send()
            x_copy(chunk).wait_send()
            for offset in range(1, 4):
                z_copy(chunk, offset).wait_send()
                g_copy(chunk, offset, False).wait_send()
            h_copy(chunk).wait_send()


def conv_backward_and_sum(ids, vectors, ratio, weights, parts, small):
    groups, tokens, _ = vectors.shape
    full, _ = group_counts()
    vocab = -(-VOCAB // 8) * 8
    width = parts[0].shape[1]
    parts = [part.reshape(2, -1, 2, CHUNK_ROWS, width) for part in parts]
    chunks = sum(part.shape[1] for part in parts)
    table_rows = vocab + small.shape[0]
    conv_rows = TAPS * CDIM
    span = FILTERS // 4
    bf16, f32 = jnp.bfloat16, jnp.float32
    dma = pltpu.SemaphoreType.DMA
    last = SHIFTS - 1
    high_sum, proj_sum, grad, table = pl.pallas_call(
        functools.partial(tail_kernel, chunks),
        grid=(-(-(chunks + 4 * SLACK) // BEATS),),
        in_specs=[pl.BlockSpec(memory_space=pltpu.VMEM)] * 6
        + [pl.BlockSpec((1, 2 * GROUP, FILTERS), lambda t: (jnp.minimum(t, last), 0, 0))]
        + [pl.BlockSpec(memory_space=pl.ANY)] * 3
        + [pl.BlockSpec(memory_space=pltpu.VMEM)],
        out_specs=[
            pl.BlockSpec(memory_space=pl.ANY),
            pl.BlockSpec(memory_space=pl.ANY),
            pl.BlockSpec(memory_space=pltpu.VMEM),
            pl.BlockSpec(memory_space=pltpu.VMEM),
        ],
        out_shape=[
            jax.ShapeDtypeStruct((2,) + parts[0].shape[1:], bf16),
            jax.ShapeDtypeStruct(parts[2].shape[1:], bf16),
            jax.ShapeDtypeStruct((conv_rows, span), f32),
            jax.ShapeDtypeStruct((table_rows, GROUP), f32),
        ],
        scratch_shapes=[
            pltpu.VMEM((conv_rows, FILTERS), f32),
            pltpu.VMEM((full * tokens, FILTERS), bf16),
            pltpu.VMEM((groups, tokens, GROUP), f32),
            pltpu.VMEM((2 * GROUP, FBLOCK), f32),
            pltpu.VMEM((2, 2, CHUNK_ROWS, width), bf16),
            pltpu.VMEM((chunks, 2, CHUNK_ROWS, width), bf16),
            pltpu.VMEM((chunks, CHUNK_ROWS, width), bf16),
            pltpu.VMEM((chunks, 3, CHUNK_ROWS, width // 4), bf16),
            pltpu.VMEM((chunks, CHUNK_ROWS, width), bf16),
            pltpu.VMEM((chunks, CHUNK_ROWS, width), bf16),
            pltpu.VMEM((2, 2, CHUNK_ROWS, width), bf16),
            pltpu.VMEM((3, conv_rows, span), f32),
            pltpu.VMEM((4, conv_rows, span), f32),
            pltpu.VMEM((2, 2, conv_rows, span), f32),
            pltpu.VMEM((2, conv_rows, span), f32),
            pltpu.VMEM((5, table_rows, GROUP), f32),
            pltpu.VMEM((5, table_rows, GROUP), f32),
            dma((2,)),
            dma((2,)),
            dma((chunks,)),
            dma((chunks,)),
            dma((chunks,)),
            dma((chunks,)),
            dma((chunks, 3)),
            dma((chunks, 3)),
            dma((chunks, 3)),
            dma((chunks, 3)),
            dma((chunks,)),
            dma((chunks,)),
            dma((5, 3)),
            dma((5, 3)),
        ],
        compiler_params=pltpu.CompilerParams(
            collective_id=3, has_side_effects=True, vmem_limit_bytes=62 * 2**20
        ),
    )(*conv_operands(ids, vectors), ratio, weights, *parts, small)
    rest = table[vocab:]
    table = table[:vocab].reshape(vocab, SHIFTS, CDIM).sum(axis=1)[:VOCAB]
    return high_sum.reshape(2, -1, width), proj_sum, grad, table, rest


GROUPS = tuple(("high", layer, part) for layer in range(2) for part in range(2)) + (("proj", 0, 0),)
LOCAL = tuple((item, other) for other in range(2) for item in range(3))
START_STEPS = len(LOCAL) + 4


def start_kernel(
    ids_ref,
    table_ref,
    conv_ref,
    high_ref,
    proj_ref,
    win_ref,
    wst_ref,
    wpr_ref,
    total_ref,
    vec_ref,
    weight_ref,
    high_one,
    high_two,
    proj_all,
    win_all,
    wst_all,
    wpr_all,
    conv_got,
    conv_send,
    conv_recv,
    own_sem,
    core_send,
    core_recv,
    y_send,
    y_recv,
    x_send,
    x_recv,
    z_send,
    z_recv,
    c_send,
    c_recv,
    ly_send,
    ly_recv,
    lc_send,
    lc_recv,
    lx_send,
    lx_recv,
):
    step = pl.program_id(0)
    dp = lax.axis_index("dp")
    mp = lax.axis_index("mp")
    core, high = lax.rem(dp, 2), dp // 2
    near, ring = lax.rem(mp, 2), lax.rem(mp // 2, 2)
    across = dp + 2 - 4 * high
    core_peer = {"dp": dp + 1 - 2 * core, "mp": mp}
    high_peer = {"dp": across, "mp": mp}
    both_peer = {"dp": across + 1 - 2 * core, "mp": mp}
    near_peer = {"dp": dp, "mp": mp + 1 - 2 * near}
    ring_peer = {"dp": dp, "mp": mp + 2 - 4 * ring}
    lanes = wpr_ref.shape[2]
    mine = 2 * ring + near
    beside = 2 * ring + 1 - near
    beyond = 2 * (1 - ring)

    def from_shard(index, place):
        kind, layer, part = GROUPS[index]
        if kind == "high":
            return high_ref.at[layer, 4 * part + place]
        return proj_ref.at[place]

    def in_full(index, place, quarter):
        kind, layer, part = GROUPS[index]
        if kind == "high":
            return (high_one, high_two)[layer].at[quarter, 4 * part + place]
        return proj_all.at[quarter, place]

    def local_full(item, side, quarter):
        if item == 2:
            cols = pl.ds(pl.multiple_of(quarter * lanes, lanes), lanes)
            return wpr_all.at[side, :, cols]
        return (win_all, wst_all)[item].at[side, quarter]

    def side_of(index):
        return 1 - near if LOCAL[index][1] else near

    def local_source(index):
        item, other = LOCAL[index]
        if other:
            return local_full(item, 1 - near, dp)
        return (win_ref, wst_ref, wpr_ref)[item].at[near]

    def lx_copy(item):
        return remote(
            (win_ref, wst_ref, wpr_ref)[item].at[1 - near],
            local_full(item, near, dp),
            lx_send.at[item],
            lx_recv.at[item],
            near_peer,
        )

    def own_pair(index):
        if index < 2:
            return high_ref.at[index], (high_one, high_two)[index].at[dp]
        if index == 2:
            return proj_ref, proj_all.at[dp]
        return local_source(index - 3), local_full(LOCAL[index - 3][0], side_of(index - 3), dp)

    owned = 3 + len(LOCAL)

    def remote(src, dst, send, recv, peer):
        return pltpu.make_async_remote_copy(
            src_ref=src, dst_ref=dst, send_sem=send, recv_sem=recv, device_id=peer, device_id_type=MESH
        )

    def own_copy(index):
        src, dst = own_pair(index)
        return pltpu.make_async_copy(src, dst, own_sem.at[index])

    def core_copy(index):
        src, dst = own_pair(index)
        return remote(src, dst, core_send.at[index], core_recv.at[index], core_peer)

    def y_copy(index):
        return remote(
            from_shard(index, mine),
            in_full(index, mine, dp),
            y_send.at[index],
            y_recv.at[index],
            high_peer,
        )

    def x_copy(index):
        place = in_full(index, mine, across)
        return remote(place, place, x_send.at[index], x_recv.at[index], near_peer)

    def z_copy(index, which):
        place = in_full(index, 2 * ring + which, across)
        return remote(
            place, place, z_send.at[index, which], z_recv.at[index, which], ring_peer
        )

    def c_copy(index, place):
        ref = in_full(index, place, across)
        return remote(ref, ref, c_send.at[index, place], c_recv.at[index, place], core_peer)

    def ly_copy(index):
        return remote(
            local_source(index),
            local_full(LOCAL[index][0], side_of(index), dp),
            ly_send.at[index],
            ly_recv.at[index],
            high_peer,
        )

    def lc_copy(index):
        ref = local_full(LOCAL[index][0], side_of(index), across)
        return remote(ref, ref, lc_send.at[index], lc_recv.at[index], core_peer)

    conv_peers = (core_peer, high_peer, both_peer)

    def conv_copy(index):
        return remote(
            conv_ref, conv_got.at[dp], conv_send.at[index], conv_recv.at[index], conv_peers[index]
        )

    @pl.when(step == 0)
    def _():
        barrier = pltpu.get_barrier_semaphore()
        for peer in (core_peer, high_peer, both_peer, near_peer, ring_peer):
            pl.semaphore_signal(barrier, inc=1, device_id=peer, device_id_type=MESH)
        pl.semaphore_wait(barrier, 5)
        for index in range(3):
            conv_copy(index).start()
        y_copy(0).start()
        for item in range(3):
            lx_copy(item).start()
        for index in range(2):
            core_copy(index).start()
            own_copy(index).start()
        char_vectors(ids_ref, table_ref, vec_ref)
        weight_ref[...] = jnp.zeros(weight_ref.shape, jnp.bfloat16)
        conv_got[dp] = conv_ref[...]
        for index in range(3):
            conv_copy(index).wait()
        span = conv_ref.shape[1]
        tap = lax.broadcasted_iota(jnp.int32, (TAPS * CDIM, span), 0) // CDIM
        for quarter in range(4):
            bound = position_bound(quarter * span, span, TAPS)
            part = conv_got[quarter]
            part = part * jnp.where(tap < CHARS - bound, 1.0, 0.0).astype(jnp.bfloat16)
            for shift in range(SHIFTS):
                weight_ref[
                    shift,
                    CDIM * shift : CDIM * (shift + TAPS),
                    quarter * span : (quarter + 1) * span,
                ] = part

    for index in reversed(range(len(GROUPS))):

        @pl.when(step == index + 1)
        def _():
            y_copy(index).wait_recv()
            if index + 1 < len(GROUPS):
                y_copy(index + 1).start()
            x_copy(index).start()
            z_copy(index, near).start()
            c_copy(index, mine).start()

        @pl.when(step == index + 2)
        def _():
            x_copy(index).wait_recv()
            z_copy(index, 1 - near).start()
            c_copy(index, beside).start()

        @pl.when(step == index + 3)
        def _():
            for which in range(2):
                z_copy(index, which).wait_recv()
                c_copy(index, beyond + which).start()

    for index in range(len(LOCAL)):
        @pl.when(step == index + 1)
        def _():
            if LOCAL[index][1]:
                lx_copy(LOCAL[index][0]).wait_recv()
            ly_copy(index).start()
            core_copy(index + 3).start()
            if not LOCAL[index][1]:
                own_copy(index + 3).start()

        @pl.when(step == index + 3)
        def _():
            ly_copy(index).wait_recv()
            lc_copy(index).start()

    @pl.when(step == 1)
    def _():
        core_copy(2).start()
        own_copy(2).start()

    @pl.when(jnp.logical_and(step >= 1, step <= FILTERS // (2 * FBLOCK)))
    def _():
        for half in range(2):
            block = 2 * (step - 1) + half
            cols = pl.ds(pl.multiple_of(block * FBLOCK, FBLOCK), FBLOCK)
            conv_block(block, cols, vec_ref, weight_ref, total_ref)

    @pl.when(step == START_STEPS - 1)
    def _():
        for index in range(owned):
            if index < owned - 3:
                own_copy(index).wait()
            core_copy(index).wait()
        for item in range(3):
            lx_copy(item).wait_send()
        for index in range(len(GROUPS)):
            y_copy(index).wait_send()
            x_copy(index).wait_send()
            for which in range(2):
                z_copy(index, which).wait_send()
            for place in range(4):
                c_copy(index, place).wait()
        for index in range(len(LOCAL)):
            ly_copy(index).wait_send()
            lc_copy(index).wait()


def start_gather(ids, table_shift, conv, highway, proj, win, wst, wpr):
    tokens = ids.shape[0]
    groups = -(-CHARS // SHIFTS)
    bf16 = jnp.bfloat16
    depth, wide = highway.shape[1:]
    rows = proj.shape[0]
    highway = highway.reshape(2, 8, depth // 8, wide)
    proj = proj.reshape(4, rows // 4, PROJ)
    vmem = pl.BlockSpec(memory_space=pltpu.VMEM)
    hbm = pl.BlockSpec(memory_space=pl.ANY)
    dma = pltpu.SemaphoreType.DMA
    count, local = len(GROUPS), len(LOCAL)
    total, vec, weight, one, two, proj, win, wst, wpr = pl.pallas_call(
        start_kernel,
        grid=(START_STEPS,),
        in_specs=[vmem] * 8,
        out_specs=[vmem] * 3 + [hbm] * 6,
        out_shape=[
            jax.ShapeDtypeStruct((tokens, FILTERS), jnp.float32),
            jax.ShapeDtypeStruct((groups, tokens, GROUP), bf16),
            jax.ShapeDtypeStruct((SHIFTS, 2 * GROUP, FILTERS), bf16),
            jax.ShapeDtypeStruct((4,) + highway.shape[1:], bf16),
            jax.ShapeDtypeStruct((4,) + highway.shape[1:], bf16),
            jax.ShapeDtypeStruct((4,) + proj.shape, bf16),
            jax.ShapeDtypeStruct((2, 4) + win.shape[1:], bf16),
            jax.ShapeDtypeStruct((2, 4) + wst.shape[1:], bf16),
            jax.ShapeDtypeStruct(wpr.shape[:2] + (4 * wpr.shape[2],), bf16),
        ],
        scratch_shapes=[pltpu.VMEM((4,) + conv.shape, bf16)]
        + [dma((3,))] * 2
        + [dma((3 + local,))] * 3
        + [dma((count,))] * 4
        + [dma((count, 2))] * 2
        + [dma((count, 4))] * 2
        + [dma((local,))] * 4
        + [dma((3,))] * 2,
        compiler_params=pltpu.CompilerParams(
            collective_id=4, has_side_effects=True, vmem_limit_bytes=40 * 2**20
        ),
    )(ids, table_shift, conv, highway, proj, win, wst, wpr)
    return (
        total,
        vec,
        weight,
        [one.reshape(4 * depth, wide), two.reshape(4 * depth, wide)],
        proj.reshape(4 * rows, PROJ),
        win.reshape(2, PROJ, -1),
        wst.reshape(2, PROJ, -1),
        wpr,
    )


def swap(value, axis, bit):
    size = lax.axis_size(axis)
    return lax.ppermute(value, axis, [(index, index ^ bit) for index in range(size)])


def scatter_start(value, axis, dim):
    index = lax.axis_index(axis)
    quarter = value.shape[dim] // 4
    low, high = index % 2, index // 2

    def pick(side, part):
        return lax.dynamic_slice_in_dim(value, (2 * side + part) * quarter, quarter, dim)

    def both(side):
        got = swap(pick(side, 1 - low), axis, 1)
        return (pick(side, low).astype(jnp.float32) + got.astype(jnp.float32)).astype(value.dtype)

    return both(high), both(1 - high)


def weight_part(left, right):
    tokens, depth = left.shape
    core = lax.axis_index("dp") % 2
    quarter = depth // 4

    def columns(which):
        return jnp.concatenate(
            [
                lax.dynamic_slice_in_dim(left, (2 * half + which) * quarter, quarter, 1)
                for half in range(2)
            ],
            axis=1,
        )

    own, other = columns(core), columns(1 - core)
    left_all = jnp.concatenate([own, swap(other, "dp", 1)], axis=0)
    right_all = jnp.concatenate([right, swap(right, "dp", 1)], axis=0)
    return jnp.dot(left_all.T, right_all, preferred_element_type=jnp.float32).astype(jnp.bfloat16)


def weight_grad(left, right):
    part = jnp.dot(left.T, right, preferred_element_type=jnp.float32).astype(jnp.bfloat16)
    return lax.psum_scatter(part, "dp", scatter_dimension=0, tiled=True)


def shards(
    char_ids,
    doc_lengths,
    window_doc,
    window_offset,
    char_table,
    conv_weight,
    conv_bias,
    highway_weight,
    highway_bias,
    proj_weight,
    proj_bias,
    lstm_input_weight,
    lstm_state_weight,
    lstm_bias,
    lstm_proj,
    init_cell,
    init_hidden,
    cotangent,
):
    tok_share = char_ids.shape[0]
    row_count = window_doc.shape[0]
    cell_local = init_cell.shape[2]
    gate_local = lstm_bias.shape[1]
    mp_index = lax.axis_index("mp")
    mp_size = lax.axis_size("mp")
    paired = lax.axis_size("dp") == 4 and mp_size == 8
    dp_index = lax.axis_index("dp")
    dp_width = conv_weight.shape[2]
    widths = filter_widths(FILTERS)
    tap_mask = jnp.arange(TAPS)[:, None] < widths[None, :]
    lows = [
        value.astype(jnp.bfloat16)
        for value in (
            conv_weight,
            highway_weight,
            proj_weight,
            lstm_input_weight,
            lstm_state_weight,
            lstm_proj,
        )
    ]
    counts = (CHARS + 1 - widths).astype(jnp.float32)
    table_low = char_table.astype(jnp.bfloat16)
    table_shifted = jnp.stack(
        [
            jnp.pad(
                table_low,
                ((0, -VOCAB % UNIT_BLOCK), (CDIM * shift, GROUP - CDIM * (shift + 1))),
            )
            for shift in range(SHIFTS)
        ]
    )
    rows_own = row_count // mp_size
    ids_time = char_ids.reshape(rows_own, WIN, CHARS).transpose(1, 0, 2).reshape(tok_share, CHARS)
    tok_pad = -tok_share % 16
    ids_time = jnp.pad(ids_time, ((0, tok_pad), (0, 0)))
    if paired:
        lows[0] = lows[0].reshape(TAPS * CDIM, dp_width)
        (
            exp_total,
            char_vecs,
            conv_shifted,
            high_full,
            proj_full,
            input_full,
            state_full,
            lproj_full,
        ) = start_gather(ids_time, table_shifted, *lows)
    else:
        conv_full, high_full, proj_full, input_full, state_full, lproj_full = (
            lax.all_gather(value, "dp", axis=dim, tiled=True)
            for value, dim in zip(lows, (2, 1, 0, 1, 1, 2))
        )
        conv_matrix = (conv_full * tap_mask[:, None, :].astype(jnp.bfloat16)).reshape(
            TAPS * CDIM, FILTERS
        )
        conv_shifted = jnp.stack(
            [
                jnp.pad(conv_matrix, ((CDIM * shift, 2 * GROUP - CDIM * (shift + TAPS)), (0, 0)))
                for shift in range(SHIFTS)
            ]
        )
        exp_total, char_vecs = conv_forward(ids_time, table_shifted, conv_shifted)
    pooled = jnp.log(exp_total[:tok_share] / counts)
    pre_pool = pooled + conv_bias
    layer_value = jax.nn.silu(pre_pool)
    kept_inputs = []
    kept_mixed = []
    for layer_index in range(2):
        mixed = (
            jnp.dot(
                layer_value.astype(jnp.bfloat16),
                high_full[layer_index],
                preferred_element_type=jnp.float32,
            )
            + highway_bias[layer_index]
        )
        kept_inputs.append(layer_value)
        kept_mixed.append(mixed)
        gate_value = jax.nn.sigmoid(mixed[:, FILTERS:])
        layer_value = gate_value * layer_value + (1.0 - gate_value) * jax.nn.silu(
            mixed[:, :FILTERS]
        )
    top_low = layer_value.astype(jnp.bfloat16)
    embed_local = jnp.dot(top_low, proj_full, preferred_element_type=jnp.float32) + proj_bias
    part_rows = -(-rows_own // 16) * 16
    rows = mp_size * part_rows

    def pad_rows(value, axis):
        shape = value.shape
        split = value.reshape(shape[:axis] + (mp_size, rows_own) + shape[axis + 1 :])
        widths = [(0, 0)] * split.ndim
        widths[axis + 1] = (0, part_rows - rows_own)
        return jnp.pad(split, widths)

    def drop_rows(value, axis):
        shape = value.shape
        split = value.reshape(shape[:axis] + (mp_size, part_rows) + shape[axis + 1 :])
        kept = lax.slice_in_dim(split, 0, rows_own, axis=axis + 1)
        return kept.reshape(shape[:axis] + (row_count,) + shape[axis + 1 :])

    embed_own = jnp.pad(
        embed_local.astype(jnp.bfloat16).reshape(WIN, rows_own, PROJ),
        ((0, 0), (0, part_rows - rows_own), (0, 0)),
    )
    embed_all = lax.all_gather(embed_own, "mp", axis=0)
    doc_index = jnp.arange(doc_lengths.shape[0])
    chosen_len = jnp.sum(
        jnp.where(window_doc[:, None] == doc_index[None, :], doc_lengths[None, :], 0), axis=1
    )
    reset_at = (chosen_len - window_offset).astype(jnp.int32)
    near, ring = mp_index % 2, mp_index // 2

    def by_near(own, got):
        return jnp.where(near == 0, jnp.stack([own, got]), jnp.stack([got, own]))

    def take(value, index, dim=0):
        size = value.shape[dim] // 2
        return lax.dynamic_slice_in_dim(value, index * size, size, dim)

    def to_owner(value):
        return by_near(
            take(value, near).reshape(value.shape[1:]),
            swap(take(value, 1 - near), "mp", 1).reshape(value.shape[1:]),
        )

    def chains(value, axis):
        shape = value.shape
        split = value.reshape(shape[:axis] + (4, 2, rows_own) + shape[axis + 1 :])
        widths = [(0, 0)] * split.ndim
        widths[axis + 2] = (0, part_rows - rows_own)
        split = jnp.moveaxis(jnp.pad(split, widths), axis + 1, 0)
        return split.reshape((2,) + shape[:axis] + (4 * part_rows,) + shape[axis + 1 :])

    if paired:
        reset_wide = jnp.broadcast_to(
            chains(reset_at, 0)[:, :, None], (2, 4 * part_rows, UNIT_BLOCK)
        )
        hidden_rows = chains(take(init_hidden, near)[0], 0).reshape(2, 4, part_rows, PROJ)
        embed_time, gates, cprevs, cnews, lows, hprevs, stats, outs = ring_forward(
            embed_all.reshape(4, 2, WIN, part_rows, PROJ),
            input_full,
            state_full,
            lproj_full,
            to_owner(lstm_bias)[:, None, :],
            chains(to_owner(init_cell), 1),
            hidden_rows,
            reset_wide,
        )
        hidden = jnp.concatenate(
            [
                jnp.transpose(drop_rows(outs[way].reshape(WIN, rows, PROJ), 1), (1, 0, 2))
                for way in range(2)
            ],
            axis=-1,
        )
        own_cot = lax.dynamic_slice(
            cotangent, (ring * 2 * rows_own, 0, near * PROJ), (2 * rows_own, WIN, PROJ)
        )
        own_cot = jnp.transpose(own_cot.reshape(2, rows_own, WIN, PROJ), (0, 2, 1, 3))
        own_cot = jnp.pad(own_cot, ((0, 0), (0, 0), (0, part_rows - rows_own), (0, 0)))
        das, dss, bias_part, embed_back = ring_backward(
            gates, cprevs, cnews, own_cot, stats, input_full, state_full, lproj_full, reset_wide
        )
        bias_part = jnp.sum(bias_part, axis=0).reshape(2, gate_local)
        grad_bias = to_owner(bias_part)
        grad_embed_local = embed_back[:, :rows_own].reshape(tok_share, PROJ)
    else:
        reset_rows = pad_rows(reset_at[:, None], 0).reshape(rows, 1)
        reset_wide = jnp.broadcast_to(reset_rows, (rows, UNIT_BLOCK))
        cell_rows = pad_rows(init_cell, 1).reshape(2, rows, cell_local)
        hidden_rows = pad_rows(init_hidden, 1)
        kept = lstm_forward(
            mp_size,
            embed_all,
            input_full,
            state_full,
            lproj_full,
            lstm_bias[:, None, :],
            cell_rows,
            hidden_rows,
            reset_wide,
        )
        embed_time = kept[0]
        gates, cprevs, cnews, lows, hprevs, stats, outs = (
            kept[1 + 2 * index : 3 + 2 * index] for index in range(7)
        )
        hidden = jnp.concatenate(
            [jnp.transpose(drop_rows(value, 1), (1, 0, 2)) for value in outs], axis=-1
        )
        own_cot = lax.dynamic_slice_in_dim(cotangent, mp_index * rows_own, rows_own, 0)
        own_cot = jnp.pad(
            jnp.transpose(own_cot, (1, 0, 2)), ((0, 0), (0, part_rows - rows_own), (0, 0))
        )
        cots = (own_cot[:, :, :PROJ], own_cot[:, :, PROJ:])
        back = lstm_backward(
            mp_size, gates, cprevs, cnews, cots, stats, input_full, state_full, lproj_full, reset_wide
        )
        das, dss = back[0:2], back[2:4]
        grad_bias = jnp.sum(back[4], axis=1)
        grad_embed_local = back[5][:, :rows_own].reshape(tok_share, PROJ)

    def outer(left, right):
        return jnp.dot(
            left.reshape(WIN * rows, -1).T,
            right.reshape(WIN * rows, -1),
            preferred_element_type=jnp.float32,
        ).astype(jnp.bfloat16)

    if paired:
        lstm_parts = [
            (outer(embed_time, das), 0, 1),
            (outer(hprevs, das), 0, 1),
            (outer(lows, dss), 1, 0),
        ]
        outers, grad_embed_local = lax.optimization_barrier(
            ([scatter_start(part, "dp", over) for part, over, _ in lstm_parts], grad_embed_local)
        )
        lstm_grads = []
        for (own, other), (_, _, dim) in zip(outers, lstm_parts):
            got = swap(other, "dp", 2)
            sums = [
                take(own, which, dim).astype(jnp.float32) + take(got, which, dim).astype(jnp.float32)
                for which in (near, 1 - near)
            ]
            lstm_grads.append((sums[0], swap(sums[1].astype(jnp.bfloat16), "mp", 1)))
    else:
        lstm_parts = [
            (outer(left[way], right[way]), dim)
            for left, right, dim in (((embed_time,) * 2, das, 0), (hprevs, das, 0), (lows, dss, 1))
            for way in range(2)
        ]
    grad_pb = jnp.sum(grad_embed_local.astype(jnp.float32), axis=0)
    summed = []
    grad_hb = [None, None]
    grad_layer = jnp.dot(grad_embed_local, proj_full.T, preferred_element_type=jnp.float32)
    for layer_index in (1, 0):
        layer_in = kept_inputs[layer_index]
        mixed = kept_mixed[layer_index]
        transform = mixed[:, :FILTERS]
        gate_value = jax.nn.sigmoid(mixed[:, FILTERS:])
        grad_gate = (
            grad_layer * (layer_in - jax.nn.silu(transform)) * gate_value * (1.0 - gate_value)
        )
        grad_trans = grad_layer * (1.0 - gate_value) * silu_slope(transform)
        grad_mixed = jnp.concatenate([grad_trans, grad_gate], axis=1).astype(jnp.bfloat16)
        layer_low = layer_in.astype(jnp.bfloat16)
        if paired:
            summed.append(weight_part(layer_low, grad_mixed))
        else:
            summed.append(lax.psum(weight_grad(layer_low, grad_mixed), "mp"))
        grad_hb[layer_index] = jnp.sum(grad_mixed.astype(jnp.float32), axis=0)
        grad_layer = grad_layer * gate_value + jnp.dot(
            grad_mixed, high_full[layer_index].T, preferred_element_type=jnp.float32
        )
    grad_pre_pool = grad_layer * silu_slope(pre_pool)
    grad_cb = jnp.sum(grad_pre_pool, axis=0)

    ratio = jnp.pad(grad_pre_pool / exp_total[:tok_share], ((0, tok_pad), (0, 0)))
    low_mask = tap_mask[:, None, :].astype(jnp.float32)
    shared = [grad_cb, jnp.stack(grad_hb), grad_pb]

    def flatten(values, unit):
        flat = jnp.concatenate([value.reshape(-1) for value in values])
        return jnp.pad(flat, (0, -flat.size % unit)).reshape(-1, UNIT_BLOCK)

    def unflatten(flat, values):
        flat, pieces, start = flat.reshape(-1), [], 0
        for value in values:
            pieces.append(flat[start : start + value.size].reshape(value.shape))
            start += value.size
        return pieces

    if paired:
        pw_part = weight_part(top_low, grad_embed_local).reshape(2, -1, summed[0].shape[1])
        small = flatten(shared, 8 * UNIT_BLOCK)
        count = small.shape[0]
        small = jnp.concatenate([small, grad_bias.reshape(BIAS_ROWS, UNIT_BLOCK)])
        high_sum, pw_sum, grad_conv, grad_table, rest = conv_backward_and_sum(
            ids_time, char_vecs, ratio, conv_shifted, summed + [pw_part], small
        )
        lstm_grads, rest = lax.optimization_barrier((lstm_grads, rest))
        lstm_grads = [by_near(own, got.astype(jnp.float32)) for own, got in lstm_grads]
        own_mask = lax.dynamic_slice_in_dim(low_mask, dp_index * dp_width, dp_width, 2)
        grad_cw = grad_conv.reshape(TAPS, CDIM, dp_width) * own_mask
        grad_cb, grad_hbs, grad_pb = unflatten(rest[:count], shared)
        grad_lbias = rest[count:].reshape(grad_bias.shape)
        grad_hws = high_sum.astype(jnp.float32)
        grad_pws = pw_sum.reshape(-1, PROJ).astype(jnp.float32)
    else:
        lstm_parts = [
            lax.psum_scatter(part, "dp", scatter_dimension=dim, tiled=True).astype(jnp.float32)
            for part, dim in lstm_parts
        ]
        pw_part = weight_grad(top_low, grad_embed_local)
        grad_pws = lax.psum(pw_part, "mp").astype(jnp.float32)
        grad_conv, grad_table = conv_backward(ids_time, char_vecs, ratio, conv_shifted)
        grad_conv = grad_conv.reshape(TAPS, CDIM, FILTERS) * low_mask
        grad_hws = jnp.stack([summed[1].astype(jnp.float32), summed[0].astype(jnp.float32)])
        shared = [grad_table, grad_conv] + shared
        flat = lax.psum(flatten(shared, 8 * UNIT_BLOCK), ("dp", "mp"))
        grad_table, grad_conv, grad_cb, grad_hbs, grad_pb = unflatten(flat, shared)
        grad_cw = lax.dynamic_slice_in_dim(grad_conv, dp_index * dp_width, dp_width, 2)
        grad_lbias = lax.psum(grad_bias, "dp")
    if not paired:
        lstm_grads = [jnp.stack(lstm_parts[2 * index : 2 * index + 2]) for index in range(3)]
    grad_input, grad_state, grad_lproj = lstm_grads
    return (
        hidden,
        grad_table,
        grad_cw,
        grad_cb,
        grad_hws,
        grad_hbs,
        grad_pws,
        grad_pb,
        grad_input,
        grad_state,
        grad_lbias,
        grad_lproj,
    )


def solution(mesh):
    in_specs = (
        P(("dp", "mp"), None),
        P(),
        P("dp"),
        P("dp"),
        P(),
        P(None, None, "dp"),
        P(),
        P(None, "dp", None),
        P(),
        P("dp", None),
        P(),
        P(None, "dp", "mp"),
        P(None, "dp", "mp"),
        P(None, "mp"),
        P(None, "mp", "dp"),
        P(None, "dp", "mp"),
        P(None, "dp", None),
        P("dp", None, None),
    )
    out_specs = (
        P("dp", None, None),
        P(),
        P(None, None, "dp"),
        P(),
        P(None, "dp", None),
        P(),
        P("dp", None),
        P(),
        P(None, "dp", "mp"),
        P(None, "dp", "mp"),
        P(None, "mp"),
        P(None, "mp", "dp"),
    )
    return jax.shard_map(shards, mesh=mesh, in_specs=in_specs, out_specs=out_specs, check_vma=False)
```
